32 devices in a mesh: wide: 16 (over z, x, core), narrow: 2 (over y).
Axes of the slice: x: 2, y: 2, z: 4, core: 2. Of those that a mesh axis runs over, the one named last changes fastest.
Arguments:
- tokens: bfloat16 [6144, 1536], P('wide'), may hold values from -6 to 6
- lengths: int32 [2], replicated, may hold values from 1024 to 3456, as said below
- norm1_gain: bfloat16 [1536], P('wide'), may hold values from 0.5 to 1.5
- w_query: bfloat16 [1536, 1536], P('wide', 'narrow'), may hold values from -0.15625 to 0.15625
- b_query: bfloat16 [12, 128], P('narrow', 'wide'), may hold values from -3 to 3
- key_projection: bfloat16 [1536, 256], P('wide', 'narrow'), may hold values from -0.15625 to 0.15625
- key_bias_vector: bfloat16 [2, 128], P('narrow', 'wide'), may hold values from -3 to 3
- value_projection: bfloat16 [1536, 256], P('wide', 'narrow'), may hold values from -0.15625 to 0.15625
- value_bias_vector: bfloat16 [2, 128], P('narrow', 'wide'), may hold values from -3 to 3
- w_out: bfloat16 [1536, 1536], P('narrow', 'wide'), may hold values from -6 to 6
- norm2_gain: bfloat16 [1536], P('wide'), may hold values from 0.5 to 1.5
- w_gate: bfloat16 [1536, 8960], P('wide', 'narrow'), may hold values from -0.15625 to 0.15625
- w_up: bfloat16 [1536, 8960], P('wide', 'narrow'), may hold values from -0.15625 to 0.15625
- w_down: bfloat16 [8960, 1536], P('narrow', 'wide'), may hold values from -0.0625 to 0.0625
- cotangent: bfloat16 [6144, 1536], P('wide'), may hold values from -6 to 6
Outputs:
- result: bfloat16 [6144, 1536], P('wide')
- grad_tokens: bfloat16 [6144, 1536], P('wide')
- grad_norm1_gain: float32 [1536], P('wide')
- grad_w_query: float32 [1536, 1536], P('wide', 'narrow')
- grad_b_query: float32 [12, 128], P('narrow', 'wide')
- grad_w_key: float32 [1536, 256], P('wide', 'narrow')
- grad_b_key: float32 [2, 128], P('narrow', 'wide')
- grad_w_value: float32 [1536, 256], P('wide', 'narrow')
- grad_b_value: float32 [2, 128], P('narrow', 'wide')
- grad_w_out: float32 [1536, 1536], P('narrow', 'wide')
- grad_norm2_gain: float32 [1536], P('wide')
- grad_w_gate: float32 [1536, 8960], P('wide', 'narrow')
- grad_w_up: float32 [1536, 8960], P('wide', 'narrow')
- grad_w_down: float32 [8960, 1536], P('narrow', 'wide')
The draws below stay inside these ranges and needn't reach their ends.
Inputs may be any that keep to these rules, and one draw needn't show every extreme that they name: Every sequence has 1024 tokens or more, the lengths add up to 6144, and the longest has exactly 3456 tokens.
All inputs are finite; a program needn't handle non-finite values.
Results may differ from the reference program's by a relative error of at most 0.038.
Values may be sent and summed in bfloat16 or wider, within the bound.
No kernel may reach another device: no remote copies, remote signals or barrier semaphores. Data moves between devices by JAX's collectives and lax.ppermute only.
A program may use at most 256 MiB of HBM per device.

```python
import math
import jax
import jax.numpy as jnp
from jax import lax

MODEL_WIDTH = 1536
QUERY_HEADS = 12
KEY_VALUE_HEADS = 2
HEAD_SIZE = 128
FF = 8960
MINLEN = 1024
TOTAL_TOKENS = 6144
LONGEST_TOKENS = 3456
NSEQ = 2


def draw_lengths(key, part):
    extra_total = TOTAL_TOKENS - LONGEST_TOKENS - (NSEQ - 1) * MINLEN
    key_cut, key_place = jax.random.split(key)
    cuts = jnp.sort(jax.random.randint(key_cut, (NSEQ - 2,), 0, extra_total + 1, dtype=jnp.int32))
    bounds = jnp.concatenate([jnp.zeros((1,), jnp.int32), cuts, jnp.full((1,), extra_total, jnp.int32)])
    extras = bounds[1:] - bounds[:-1]
    shorter = MINLEN + extras
    every = jnp.concatenate([jnp.full((1,), LONGEST_TOKENS, jnp.int32), shorter.astype(jnp.int32)])
    shift = jax.random.randint(key_place, (), 0, NSEQ, dtype=jnp.int32)
    return jnp.roll(every, shift)


def strengthened(values, rng, source, target, parts, factor):
    owner, partner = [(jnp.arange(values.shape[position]) // (values.shape[position] // parts)).reshape([-1 if axis == position else 1 for axis in range(values.ndim)]) for position in (source, target)]
    chosen = jax.random.permutation(rng, parts)[partner]
    strong = (owner == chosen) | (owner == (partner + parts // 2) % parts)
    return jnp.where(strong, factor * values, values)


def block_levels(rng, dims, shards, low, high):
    loudness = 1.0
    for position, parts in shards:
        steps = jax.random.uniform(jax.random.fold_in(jax.random.fold_in(rng, 6), position), (parts,), jnp.float32, low / len(shards), high / len(shards))
        loudness = loudness * jnp.repeat(jnp.exp(steps), dims[position] // parts).reshape((-1,) + (1,) * (len(dims) - 1 - position))
    return loudness


def bell_draw(rng, extent, scale, most, cuts=(), kind=jnp.bfloat16):
    array = jax.random.normal(rng, extent, jnp.float32) * scale
    if len(cuts) > 0:
        array = block_levels(rng, extent, cuts, -0.22, 0.18) * array
    return jnp.clip(array, min=-most, max=most).astype(kind)


def heavy_noise(stream_key, extent, width, bound, cuts, heavy, kind=jnp.bfloat16):
    array = width * jax.random.normal(stream_key, extent, jnp.float32)
    if cuts:
        array = array * block_levels(stream_key, extent, cuts, -0.22, 0.18)
    return jnp.clip(strengthened(array, jax.random.fold_in(stream_key, 3), *heavy), -bound, bound).astype(kind)


def setup_inputs(seed: int = 0) -> dict:
    arg_keys = jax.random.split(jax.random.key(seed), 16)
    tokens = bell_draw(arg_keys[0], (TOTAL_TOKENS, MODEL_WIDTH), 1.0, 6.0, ((0, 16),))
    lengths = draw_lengths(jax.random.fold_in(arg_keys[15], 71), 0)
    norm1_gain = jnp.clip(1.0 + 0.1 * jax.random.normal(arg_keys[2], (MODEL_WIDTH,), jnp.float32), 0.5, 1.5).astype(jnp.bfloat16)
    w_query = bell_draw(arg_keys[3], (MODEL_WIDTH, QUERY_HEADS * HEAD_SIZE), MODEL_WIDTH ** -0.5, 0.15625, ((0, 16), (1, 2)))
    b_query = bell_draw(arg_keys[4], (QUERY_HEADS, HEAD_SIZE), 0.5, 3.0, ((0, 2), (1, 16)))
    key_projection = bell_draw(arg_keys[5], (MODEL_WIDTH, KEY_VALUE_HEADS * HEAD_SIZE), MODEL_WIDTH ** -0.5, 0.15625, ((0, 16), (1, 2)))
    key_bias_vector = bell_draw(arg_keys[6], (KEY_VALUE_HEADS, HEAD_SIZE), 0.5, 3.0, ((0, 2), (1, 16)))
    value_projection = bell_draw(arg_keys[7], (MODEL_WIDTH, KEY_VALUE_HEADS * HEAD_SIZE), MODEL_WIDTH ** -0.5, 0.15625, ((0, 16), (1, 2)))
    value_bias_vector = bell_draw(arg_keys[8], (KEY_VALUE_HEADS, HEAD_SIZE), 0.5, 3.0, ((0, 2), (1, 16)))
    w_out = bell_draw(arg_keys[9], (QUERY_HEADS * HEAD_SIZE, MODEL_WIDTH), (max(1, QUERY_HEADS * HEAD_SIZE * 4 // LONGEST_TOKENS)) ** -0.5, 6.0, ((0, 2), (1, 16)))
    norm2_gain = jnp.clip(1.0 + 0.1 * jax.random.normal(arg_keys[10], (MODEL_WIDTH,), jnp.float32), 0.5, 1.5).astype(jnp.bfloat16)
    w_gate = bell_draw(arg_keys[11], (MODEL_WIDTH, FF), MODEL_WIDTH ** -0.5, 0.15625, ((0, 16), (1, 2)))
    w_up = bell_draw(arg_keys[12], (MODEL_WIDTH, FF), MODEL_WIDTH ** -0.5, 0.15625, ((0, 16), (1, 2)))
    w_down = bell_draw(arg_keys[13], (FF, MODEL_WIDTH), FF ** -0.5, 0.0625, ((0, 2), (1, 16)))
    cotangent = heavy_noise(arg_keys[14], (TOTAL_TOKENS, MODEL_WIDTH), 1.0, 6.0, ((0, 16),), (0, 1, 16, 2.0))
    return {"tokens": tokens, "lengths": lengths, "norm1_gain": norm1_gain, "w_query": w_query, "b_query": b_query, "key_projection": key_projection, "key_bias_vector": key_bias_vector, "value_projection": value_projection, "value_bias_vector": value_bias_vector, "w_out": w_out, "norm2_gain": norm2_gain, "w_gate": w_gate, "w_up": w_up, "w_down": w_down, "cotangent": cotangent}


HIGHEST = lax.Precision.HIGHEST
ROPE_BASE = 10000.0
EPSILON = 1e-06

@jax.custom_vjp
def lower_bound(v):
    return lax.optimization_barrier(v.astype(jnp.bfloat16)).astype(jnp.float32)

@jax.custom_vjp
def low_back(v):
    return v

def low_keep(v):
    return (lower_bound(v), None)

def low_pass(kept, grad):
    return (grad,)

def back_keep(v):
    return (v, None)

def back_low(kept, grad):
    return (lower_bound(grad),)
lower_bound.defvjp(low_keep, low_pass)
low_back.defvjp(back_keep, back_low)

def matmul(left, right):
    return jnp.dot(left, right, precision=HIGHEST, preferred_element_type=jnp.float32)

def rms_norm(value_rows, gain):
    return value_rows * lax.rsqrt(lax.optimization_barrier(jnp.mean(value_rows * value_rows, axis=-1, keepdims=True)) + EPSILON) * gain

def rotate_halves(value_rows, cosine_table, sine_table):
    middle_at = value_rows.shape[-1] // 2
    first = value_rows[..., :middle_at]
    second = value_rows[..., middle_at:]
    return jnp.concatenate([first * cosine_table - second * sine_table, second * cosine_table + first * sine_table], axis=-1)

def reference(tokens, lengths, norm1_gain, w_query, b_query, key_projection, key_bias_vector, value_projection, value_bias_vector, w_out, norm2_gain, w_gate, w_up, w_down, cotangent):
    index = jnp.arange(TOTAL_TOKENS, dtype=jnp.int32)
    ends = jnp.cumsum(lengths, dtype=jnp.int32)
    starts = (ends - lengths).astype(jnp.int32)
    seq_start = lax.optimization_barrier(jnp.max(jnp.where(starts[None, :] <= index[:, None], starts[None, :], 0), axis=1)).astype(jnp.int32)
    middle_at = HEAD_SIZE // 2
    freq = 1.0 / ROPE_BASE ** (jnp.arange(middle_at, dtype=jnp.float32) * 2.0 / HEAD_SIZE)
    angle = (index - seq_start).astype(jnp.float32)[:, None] * freq[None, :]
    cosine_table = jnp.cos(angle)[:, None, :]
    sine_table = jnp.sin(angle)[:, None, :]
    current_block = min(512, TOTAL_TOKENS)
    factor = 1.0 / math.sqrt(HEAD_SIZE)
    query_group = QUERY_HEADS // KEY_VALUE_HEADS

    def layer(inputs, gain_one, query_weight, query_bias, key_weight, key_bias, value_weight, value_bias, out_weight, gain_two, gate_weight, up_weight, down_weight):
        normed_one = lower_bound(rms_norm(inputs, gain_one))
        query_pre = low_back(matmul(normed_one, query_weight) + query_bias.reshape(-1))
        key_before_rotation = low_back(matmul(normed_one, key_weight) + key_bias.reshape(-1))
        value_projected = low_back(matmul(normed_one, value_weight) + value_bias.reshape(-1))
        query_rows = lower_bound(rotate_halves(query_pre.reshape(TOTAL_TOKENS, QUERY_HEADS, HEAD_SIZE), cosine_table, sine_table))
        key_rows = lower_bound(rotate_halves(key_before_rotation.reshape(TOTAL_TOKENS, KEY_VALUE_HEADS, HEAD_SIZE), cosine_table, sine_table))
        value_rows = lower_bound(value_projected).reshape(TOTAL_TOKENS, KEY_VALUE_HEADS, HEAD_SIZE)
        padding_rows = jnp.zeros((LONGEST_TOKENS, KEY_VALUE_HEADS, HEAD_SIZE), jnp.float32)
        key_padded = jnp.concatenate([padding_rows, key_rows], axis=0)
        value_padded = jnp.concatenate([padding_rows, value_rows], axis=0)

        def one_block(number):
            begin_offset = number * current_block
            block_of_queries = lax.dynamic_slice_in_dim(query_rows, begin_offset, current_block, 0).reshape(current_block, KEY_VALUE_HEADS, query_group, HEAD_SIZE)
            key_window = lax.dynamic_slice_in_dim(key_padded, begin_offset, LONGEST_TOKENS + current_block, 0)
            value_window = lax.dynamic_slice_in_dim(value_padded, begin_offset, LONGEST_TOKENS + current_block, 0)
            key_index = begin_offset - LONGEST_TOKENS + jnp.arange(LONGEST_TOKENS + current_block, dtype=jnp.int32)
            query_index = lax.dynamic_slice_in_dim(index, begin_offset, current_block, 0)
            query_start = lax.dynamic_slice_in_dim(seq_start, begin_offset, current_block, 0)
            allowed = (key_index[None, :] >= query_start[:, None]) & (key_index[None, :] <= query_index[:, None])
            scores = low_back(jnp.einsum('qhgd,khd->hgqk', block_of_queries, key_window, precision=HIGHEST) * factor)
            exp_weights = jnp.where(allowed[None, None], jnp.exp(scores), 0.0)
            totals = lax.optimization_barrier(jnp.sum(exp_weights, axis=-1))
            accum = low_back(jnp.einsum('hgqk,khd->qhgd', lower_bound(exp_weights), value_window, precision=HIGHEST))
            attended = accum / jnp.transpose(totals, (2, 0, 1))[..., None]
            return attended.reshape(current_block, QUERY_HEADS * HEAD_SIZE)
        blocks = lax.map(jax.checkpoint(one_block), jnp.arange(TOTAL_TOKENS // current_block, dtype=jnp.int32))
        attended_low = lower_bound(blocks.reshape(TOTAL_TOKENS, QUERY_HEADS * HEAD_SIZE))
        attention = low_back(matmul(attended_low, out_weight))
        middle = inputs + attention
        normed_two = lower_bound(rms_norm(middle, gain_two))
        gate = low_back(matmul(normed_two, gate_weight))
        up_part = low_back(matmul(normed_two, up_weight))
        hidden = lower_bound(jax.nn.silu(gate) * up_part)
        return middle + matmul(hidden, down_weight)
    primal = [item.astype(jnp.float32) for item in (tokens, norm1_gain, w_query, b_query, key_projection, key_bias_vector, value_projection, value_bias_vector, w_out, norm2_gain, w_gate, w_up, w_down)]
    output, pullback = jax.vjp(layer, *primal)
    grads = pullback(cotangent.astype(jnp.float32))
    return (output.astype(jnp.bfloat16), grads[0].astype(jnp.bfloat16), grads[1], grads[2], grads[3], grads[4], grads[5], grads[6], grads[7], grads[8], grads[9], grads[10], grads[11], grads[12])
```

```python
import math

import jax
import jax.numpy as jnp
from jax import lax
from jax.sharding import Mesh
from jax.sharding import PartitionSpec as P

ROPE_BASE = 10000.0
EPSILON = 1e-06


def product(left, right):
    return jnp.dot(left, right, preferred_element_type=jnp.float32)


def product_left(left, right):
    return lax.dot_general(
        left, right, (((0,), (0,)), ((), ())), preferred_element_type=jnp.float32
    )


def product_right(left, right):
    return lax.dot_general(
        left, right, (((1,), (1,)), ((), ())), preferred_element_type=jnp.float32
    )


def rotate_halves(value_rows, cosine_table, sine_table):
    middle_at = value_rows.shape[-1] // 2
    first = value_rows[..., :middle_at]
    second = value_rows[..., middle_at:]
    return jnp.concatenate(
        [first * cosine_table - second * sine_table, second * cosine_table + first * sine_table],
        axis=-1,
    )


def norm_scale(value_rows):
    return lax.rsqrt(jnp.mean(value_rows * value_rows, axis=-1, keepdims=True) + EPSILON)


def norm_back(value_rows, scale, gain, grad):
    normed = value_rows * scale
    inner = grad * gain
    back = scale * (inner - normed * jnp.mean(inner * normed, axis=-1, keepdims=True))
    return (back, jnp.sum(grad * normed, axis=0))


WIDE = ("z", "x", "c")
GROUP = ("x", "c")


def other(value, axis):
    return lax.ppermute(value, axis, [(0, 1), (1, 0)])


def low(value):
    return value.astype(jnp.bfloat16)


def gather_group(own):
    core = other(own, "c")
    across = other(own, "x")
    far = other(across, "c")
    return jnp.concatenate([own, core, across, far], axis=0)


def scatter_group(partial, rows):
    sent = low(jnp.concatenate([partial[rows : 2 * rows], partial[3 * rows :]], axis=0))
    core = other(sent, "c").astype(jnp.float32)
    across = low(partial[2 * rows : 3 * rows] + core[rows:])
    own = partial[:rows] + core[:rows] + other(across, "x").astype(jnp.float32)
    return sum_narrow(own)


def sum_narrow(partial):
    mine = low(partial)
    return mine.astype(jnp.float32) + other(mine, "y").astype(jnp.float32)


def spread(weight):
    features, hidden = weight.shape
    parts = weight.reshape(features, 4, hidden // 4).transpose(1, 0, 2)
    parts = lax.all_to_all(parts, GROUP, split_axis=0, concat_axis=0, tiled=True)
    return parts.reshape(4 * features, hidden // 4)


def collect(grad):
    summed = lax.psum_scatter(low(grad), "z", scatter_dimension=0, tiled=True)
    features = summed.shape[0] // 4
    parts = summed.reshape(4, features, summed.shape[1])
    parts = lax.all_to_all(parts, GROUP, split_axis=0, concat_axis=0, tiled=True)
    return parts.transpose(1, 0, 2).reshape(features, 4 * summed.shape[1]).astype(jnp.float32)


def local(
    tokens,
    lengths,
    norm1_gain,
    w_query,
    b_query,
    key_projection,
    key_bias_vector,
    value_projection,
    value_bias_vector,
    w_out,
    norm2_gain,
    w_gate,
    w_up,
    w_down,
    cotangent,
):
    rows, width = tokens.shape
    devices = lax.axis_size(WIDE)
    own_index = lax.axis_index(WIDE)
    first = own_index * rows
    index = first + jnp.arange(rows, dtype=jnp.int32)
    ends = jnp.cumsum(lengths, dtype=jnp.int32)
    starts = ends - lengths
    seq_start = jnp.max(jnp.where(starts[None, :] <= index[:, None], starts[None, :], 0), axis=1)
    lowest = jnp.min(seq_start)
    highest = first + rows - 1
    head = key_projection.shape[1]
    freq = 1.0 / ROPE_BASE ** (jnp.arange(head // 2, dtype=jnp.float32) * 2.0 / head)
    angle = (index - seq_start).astype(jnp.float32)[:, None] * freq[None, :]
    cosine_table = jnp.cos(angle)[:, None, :]
    sine_table = jnp.sin(angle)[:, None, :]
    factor = 1.0 / math.sqrt(head)
    span = rows * max(1, devices // 16)
    features = w_query.shape[0]
    heads_width = w_query.shape[1]
    query_group = heads_width // head
    projected = heads_width + 2 * head

    piece = b_query.shape[1]
    small_parts = [norm1_gain, norm2_gain, b_query.reshape(-1), key_bias_vector.reshape(-1),
                   value_bias_vector.reshape(-1)]
    small_sizes = [part.shape[0] for part in small_parts]
    small_rows = -(-sum(small_sizes) // head)
    small = jnp.concatenate(small_parts)
    small = jnp.pad(small, (0, features * head - small.shape[0])).reshape(features, head)
    packed = jnp.concatenate([w_query, key_projection, value_projection, small], axis=1)
    w_project = lax.all_gather(packed, WIDE, axis=0, tiled=True)
    small_all = w_project[:, projected:].reshape(devices, features, head)[:, :small_rows]
    small_all = small_all.reshape(devices, small_rows * head).astype(jnp.float32)
    cuts = [0]
    for size in small_sizes:
        cuts.append(cuts[-1] + size)
    gain_one = small_all[:, cuts[0] : cuts[1]].reshape(-1)
    gain_two = small_all[:, cuts[1] : cuts[2]].reshape(-1)
    bias_query = small_all[:, cuts[2] : cuts[3]].reshape(devices, query_group, piece)
    bias_query = bias_query.transpose(1, 0, 2).reshape(-1)
    bias_key = small_all[:, cuts[3] : cuts[4]].reshape(-1)
    bias_value = small_all[:, cuts[4] : cuts[5]].reshape(-1)

    gate_part = spread(w_gate)
    up_part_weight = spread(w_up)
    down_part_weight = spread(w_down.T)

    inputs = tokens.astype(jnp.float32)
    scale_one = norm_scale(inputs)
    normed_one = low(inputs * scale_one * gain_one)
    projections = product(normed_one, w_project)
    query_pre = projections[:, :heads_width] + bias_query
    query_rows = low(
        rotate_halves(query_pre.reshape(rows, query_group, head), cosine_table, sine_table)
    ).reshape(rows * query_group, head)
    key_pre = projections[:, heads_width : heads_width + head] + bias_key
    key_rows = low(
        rotate_halves(key_pre.reshape(rows, 1, head), cosine_table, sine_table).reshape(rows, head)
    )
    value_rows = low(projections[:, heads_width + head : projected] + bias_value)

    key_value = lax.all_gather(
        jnp.concatenate([key_rows, value_rows], axis=1), WIDE, axis=0, tiled=True
    )
    w_out_all = lax.all_gather(w_out.T, WIDE, axis=0, tiled=True)
    gate_all = lax.all_gather(gate_part, "z", axis=0, tiled=True)
    up_all = lax.all_gather(up_part_weight, "z", axis=0, tiled=True)
    down_all = lax.all_gather(down_part_weight, "z", axis=0, tiled=True)
    count = key_value.shape[0]

    def exp_scores(key_block, key_begin):
        size = key_block.shape[0]
        key_index = key_begin + jnp.arange(size, dtype=jnp.int32)
        allowed = (key_index[None, :] >= seq_start[:, None]) & (
            key_index[None, :] <= index[:, None]
        )
        scores = product_right(query_rows, key_block) * factor
        exp_weights = jnp.where(
            allowed[:, None, :], jnp.exp(scores.reshape(rows, query_group, size)), 0.0
        )
        return exp_weights.reshape(rows * query_group, size)

    def is_live(key_begin, size):
        return (key_begin + size > lowest) & (key_begin <= highest)

    initial = (
        jnp.zeros((rows * query_group, head), jnp.float32),
        jnp.zeros((rows * query_group,), jnp.float32),
    )

    def turn(step, state):
        offset = step * span

        def turn_compute(inner):
            weighted, totals = inner
            block = lax.dynamic_slice_in_dim(key_value, offset, span, 0)
            exp_weights = exp_scores(block[:, :head], offset)
            return (
                weighted + product(low(exp_weights), block[:, head:]),
                totals + jnp.sum(exp_weights, axis=1),
            )

        return lax.cond(is_live(offset, span), turn_compute, lambda inner: inner, state)

    weighted, totals = lax.fori_loop(0, count // span, turn, initial)
    attended = weighted / totals[:, None]
    attended_low = low(attended.reshape(rows, heads_width))
    middle = inputs + sum_narrow(product_right(attended_low, w_out_all))
    scale_two = norm_scale(middle)
    normed_two = low(middle * scale_two * gain_two)

    cotangent_group = gather_group(cotangent)
    normed_group = gather_group(normed_two)
    gate = product(normed_group, gate_all)
    up_part = product(normed_group, up_all)
    sigmoid_gate = jax.nn.sigmoid(gate)
    silu_gate = gate * sigmoid_gate
    hidden = low(silu_gate * up_part)
    result = low(middle + scatter_group(product_right(hidden, down_all), rows))
    grad_down = product_left(cotangent_group, hidden)
    grad_hidden = product(cotangent_group, down_all)
    grad_gate = low(grad_hidden * up_part * sigmoid_gate * (1.0 + gate * (1.0 - sigmoid_gate)))
    grad_up = low(grad_hidden * silu_gate)
    grad_normed_two = scatter_group(
        product_right(grad_gate, gate_all) + product_right(grad_up, up_all), rows
    )
    grad_w_down = collect(grad_down).T
    grad_w_gate = collect(product_left(normed_group, grad_gate))
    grad_w_up = collect(product_left(normed_group, grad_up))

    back_two, grad_gain_two = norm_back(middle, scale_two, gain_two, grad_normed_two)
    grad_middle = cotangent.astype(jnp.float32) + back_two
    grad_att = low(grad_middle)
    grad_w_out = (
        lax.psum_scatter(
            low(product_left(grad_att, attended_low)), WIDE, scatter_dimension=0, tiled=True
        )
        .astype(jnp.float32)
        .T
    )
    grad_attended = product(grad_att, w_out_all).reshape(rows * query_group, head)
    grad_accum = low(grad_attended / totals[:, None])
    delta = jnp.sum(grad_attended * attended, axis=1) / totals

    def back_turn(step, state):
        offset = step * span

        def back_compute(inner):
            grad_queries, buffer = inner
            block = lax.dynamic_slice_in_dim(key_value, offset, span, 0)
            exp_weights = exp_scores(block[:, :head], offset)
            grad_probs = product_right(grad_accum, block[:, head:])
            grad_scores = low(exp_weights * (grad_probs - delta[:, None]))
            grad_keys = product_left(grad_scores, query_rows) * factor
            grad_values = product_left(low(exp_weights), grad_accum)
            update = low(jnp.concatenate([grad_keys, grad_values], axis=1))
            return (
                grad_queries + product(grad_scores, block[:, :head]),
                lax.dynamic_update_slice_in_dim(buffer, update, offset, 0),
            )

        return lax.cond(is_live(offset, span), back_compute, lambda inner: inner, state)

    start_state = (
        jnp.zeros((rows * query_group, head), jnp.float32),
        jnp.zeros((count, 2 * head), jnp.bfloat16),
    )
    grad_queries, buffer = lax.fori_loop(0, count // span, back_turn, start_state)
    key_value_grads = lax.psum_scatter(buffer, WIDE, scatter_dimension=0, tiled=True).astype(
        jnp.float32
    )
    grad_query_pre = low(
        rotate_halves(
            (grad_queries * factor).reshape(rows, query_group, head), cosine_table, -sine_table
        )
    ).reshape(rows, heads_width)
    grad_key_pre = low(
        rotate_halves(key_value_grads[:, :head].reshape(rows, 1, head), cosine_table, -sine_table)
    ).reshape(rows, head)
    grad_value_pre = low(key_value_grads[:, head:])
    grad_project = jnp.concatenate([grad_query_pre, grad_key_pre, grad_value_pre], axis=1)
    grad_bias = jnp.sum(grad_project.astype(jnp.float32), axis=0)
    grad_normed_one = sum_narrow(product_right(grad_project, w_project[:, :projected]))
    back_one, grad_gain_one = norm_back(inputs, scale_one, gain_one, grad_normed_one)
    grad_tokens = low(grad_middle + back_one)

    small_grads = jnp.concatenate(
        [
            grad_gain_one.reshape(devices, -1),
            grad_gain_two.reshape(devices, -1),
            grad_bias[:heads_width]
            .reshape(query_group, devices, piece)
            .transpose(1, 0, 2)
            .reshape(devices, -1),
            grad_bias[heads_width : heads_width + head].reshape(devices, -1),
            grad_bias[heads_width + head :].reshape(devices, -1),
        ],
        axis=1,
    )
    small_grads = jnp.pad(small_grads, ((0, 0), (0, features * head - small_grads.shape[1])))
    packed_grads = low(
        jnp.concatenate(
            [product_left(normed_one, grad_project), small_grads.reshape(devices * features, head)],
            axis=1,
        )
    )
    packed_grads = lax.psum_scatter(packed_grads, WIDE, scatter_dimension=0, tiled=True).astype(
        jnp.float32
    )
    small_own = packed_grads[:, projected:].reshape(-1)
    return (
        result,
        grad_tokens,
        small_own[cuts[0] : cuts[1]],
        packed_grads[:, :heads_width],
        small_own[cuts[2] : cuts[3]].reshape(query_group, piece),
        packed_grads[:, heads_width : heads_width + head],
        small_own[cuts[3] : cuts[4]].reshape(1, piece),
        packed_grads[:, heads_width + head : projected],
        small_own[cuts[4] : cuts[5]].reshape(1, piece),
        grad_w_out,
        small_own[cuts[1] : cuts[2]],
        grad_w_gate,
        grad_w_up,
        grad_w_down,
    )


def solution(mesh):
    wide, narrow = mesh.devices.shape
    grouped = Mesh(mesh.devices.reshape(wide // 4, 2, 2, narrow), WIDE + ("y",))
    rows = P(WIDE, None)
    vector = P(WIDE)
    columns = P(WIDE, "y")
    lines = P("y", WIDE)
    return jax.shard_map(
        local,
        mesh=grouped,
        in_specs=(rows, P(), vector, columns, lines, columns, lines, columns, lines, lines,
                  vector, columns, columns, lines, rows),
        out_specs=(rows, rows, vector, columns, lines, columns, lines, columns, lines, lines,
                   vector, columns, columns, lines),
        check_vma=False,
    )
```

```python
import math

import jax
import jax.numpy as jnp
from jax import lax
from jax.experimental import pallas as pl
from jax.experimental.pallas import tpu as pltpu
from jax.sharding import Mesh
from jax.sharding import PartitionSpec as P

ROPE_BASE = 10000.0
EPSILON = 1e-06


def product(left, right):
    return jnp.dot(left, right, preferred_element_type=jnp.float32)


def product_left(left, right):
    return lax.dot_general(
        left, right, (((0,), (0,)), ((), ())), preferred_element_type=jnp.float32
    )


def product_right(left, right):
    return lax.dot_general(
        left, right, (((1,), (1,)), ((), ())), preferred_element_type=jnp.float32
    )


def rotate_halves(value_rows, cosine_table, sine_table):
    middle_at = value_rows.shape[-1] // 2
    first = value_rows[..., :middle_at]
    second = value_rows[..., middle_at:]
    return jnp.concatenate(
        [first * cosine_table - second * sine_table, second * cosine_table + first * sine_table],
        axis=-1,
    )


def norm_scale(value_rows):
    return lax.rsqrt(jnp.mean(value_rows * value_rows, axis=-1, keepdims=True) + EPSILON)


def norm_back(value_rows, scale, gain, grad):
    normed = value_rows * scale
    inner = grad * gain
    back = scale * (inner - normed * jnp.mean(inner * normed, axis=-1, keepdims=True))
    return (back, jnp.sum(grad * normed, axis=0))


WIDE = ("zh", "zl", "x", "c")
GROUP = ("zl", "c")


def other(value, axis):
    return lax.ppermute(value, axis, [(0, 1), (1, 0)])


def low(value):
    return value.astype(jnp.bfloat16)


def gather_group(own):
    core = other(own, "c")
    across = other(own, "zl")
    far = other(across, "c")
    return jnp.concatenate([own, core, across, far], axis=0)


def scatter_group(partial, rows):
    sent = low(jnp.concatenate([partial[rows : 2 * rows], partial[3 * rows :]], axis=0))
    core = other(sent, "c").astype(jnp.float32)
    across = low(partial[2 * rows : 3 * rows] + core[rows:])
    own = partial[:rows] + core[:rows] + other(across, "zl").astype(jnp.float32)
    return sum_narrow(own)


def sum_narrow(partial):
    mine = low(partial)
    return mine.astype(jnp.float32) + other(mine, "y").astype(jnp.float32)


def spread(weight):
    features, hidden = weight.shape
    parts = weight.reshape(features, 4, hidden // 4).transpose(1, 0, 2)
    parts = lax.all_to_all(parts, GROUP, split_axis=0, concat_axis=0, tiled=True)
    own = parts.reshape(1, 2, 1, 2 * features, hidden // 4)
    high = lax.axis_size("zh")
    at_x = lax.axis_index("x")
    if high == 2:
        at_high = lax.axis_index("zh")
        far = other(own, "zh")
        whole = jnp.zeros((high, 2, 2, 2 * features, hidden // 4), jnp.bfloat16)
        for piece, place in ((own, at_high), (far, 1 - at_high)):
            whole = lax.dynamic_update_slice(whole, piece, (place, 0, at_x, 0, 0))
        mine = jnp.concatenate([own, far], axis=0)
        across = other(mine, "x")
        for number, place in ((0, at_high), (1, 1 - at_high)):
            whole = lax.dynamic_update_slice(
                whole, across[number : number + 1], (place, 0, 1 - at_x, 0, 0)
            )
    else:
        mine = lax.all_gather(own, "zh", axis=0, tiled=True)
        across = other(mine, "x")
        whole = jnp.zeros((high, 2, 2, 2 * features, hidden // 4), jnp.bfloat16)
        whole = lax.dynamic_update_slice(whole, mine, (0, 0, at_x, 0, 0))
        whole = lax.dynamic_update_slice(whole, across, (0, 0, 1 - at_x, 0, 0))
    return whole.reshape(high * 8 * features, hidden // 4)


def halve(grad, axis, position):
    at = lax.axis_index(axis)
    sent = lax.dynamic_slice_in_dim(grad, 1 - at, 1, position)
    kept = lax.dynamic_slice_in_dim(grad, at, 1, position)
    return low(kept.astype(jnp.float32) + other(sent, axis).astype(jnp.float32))


def collect(grad):
    high = lax.axis_size("zh")
    features = grad.shape[0] // (8 * high)
    hidden = grad.shape[1]
    summed = halve(grad.reshape(high, 2, 2, 2 * features, hidden), "x", 2)
    if high == 2:
        summed = halve(summed, "zh", 0)
    else:
        summed = lax.psum_scatter(summed, "zh", scatter_dimension=0, tiled=True)
    parts = summed.reshape(4, features, hidden)
    parts = lax.all_to_all(parts, GROUP, split_axis=0, concat_axis=0, tiled=True)
    return parts.transpose(1, 0, 2).reshape(features, 4 * hidden).astype(jnp.float32)


def rotate_rows(value_rows, cosine, sine):
    return value_rows * cosine + pltpu.roll(value_rows, value_rows.shape[1] // 2, 1) * sine


def mask_bias(place_ref, begin, span):
    rows = place_ref.shape[1]
    key_index = begin + lax.broadcasted_iota(jnp.int32, (span, rows), 0)
    allowed = (key_index >= place_ref[0:1, :]) & (key_index <= place_ref[1:2, :])
    return jnp.where(allowed, 0.0, -1e30)


def turned(value):
    return value.astype(jnp.float32).T.astype(value.dtype)


def attend_kernel(
    bounds_ref, query_ref, cosine_ref, sine_ref, place_ref, pair_ref,
    rotated_ref, attended_ref, totals_ref, sums_ref,
):
    rows, wide = query_ref.shape
    head = cosine_ref.shape[1]
    factor = math.log2(math.e) / math.sqrt(head)
    cosine = cosine_ref[...]
    sine = sine_ref[...]
    for at in range(0, wide, head):
        rotated_ref[:, at : at + head] = low(
            rotate_rows(query_ref[:, at : at + head], cosine, sine)
        )
    sums_ref[...] = jnp.zeros_like(sums_ref)
    totals_ref[...] = jnp.zeros_like(totals_ref)

    def step(number, carry):
        begin = pl.multiple_of(number * rows, rows)
        keys = pair_ref[pl.ds(begin, rows), :head]
        values_turned = turned(pair_ref[pl.ds(begin, rows), head:])
        bias = mask_bias(place_ref, begin, rows)
        for order in range(wide // head):
            at = order * head
            scores = product_right(keys, rotated_ref[:, at : at + head])
            weights = jnp.exp2(scores * factor + bias)
            totals_ref[order : order + 1, :] += jnp.sum(weights, axis=0, keepdims=True)
            sums_ref[at : at + head, :] += product(values_turned, low(weights))
        return carry

    lax.fori_loop(bounds_ref[0], bounds_ref[1] + 1, step, 0)
    for order in range(wide // head):
        at = order * head
        attended_ref[:, at : at + head] = (
            sums_ref[at : at + head, :] / totals_ref[order : order + 1, :]
        ).T


def attend_back_kernel(
    bounds_ref, rotated_ref, accum_ref, delta_ref, cosine_ref, sine_ref, place_ref, pair_ref,
    grad_query_ref, grad_pair_ref, sums_ref,
):
    rows, wide = rotated_ref.shape
    head = cosine_ref.shape[1]
    scale = 1.0 / math.sqrt(head)
    factor = math.log2(math.e) * scale

    def clear(number, carry):
        begin = pl.multiple_of(number * rows, rows)
        grad_pair_ref[pl.ds(begin, rows), :] = jnp.zeros((rows, 2 * head), jnp.bfloat16)
        return carry

    lax.fori_loop(0, grad_pair_ref.shape[0] // rows, clear, 0)
    sums_ref[...] = jnp.zeros_like(sums_ref)

    def step(number, carry):
        begin = pl.multiple_of(number * rows, rows)
        keys = pair_ref[pl.ds(begin, rows), :head]
        values = pair_ref[pl.ds(begin, rows), head:]
        keys_turned = turned(keys)
        bias = mask_bias(place_ref, begin, rows)
        grad_keys = jnp.zeros((rows, head), jnp.float32)
        grad_values = jnp.zeros((rows, head), jnp.float32)
        for order in range(wide // head):
            at = order * head
            query = rotated_ref[:, at : at + head]
            accum = accum_ref[:, at : at + head]
            weights = jnp.exp2(product_right(keys, query) * factor + bias)
            grad_scores = low(
                weights * (product_right(values, accum) - delta_ref[order : order + 1, :])
            )
            grad_values += product(low(weights), accum)
            grad_keys += product(grad_scores, query)
            sums_ref[at : at + head, :] += product(keys_turned, grad_scores)
        grad_pair_ref[pl.ds(begin, rows), :head] = low(grad_keys * scale)
        grad_pair_ref[pl.ds(begin, rows), head:] = low(grad_values)
        return carry

    lax.fori_loop(bounds_ref[0], bounds_ref[1] + 1, step, 0)
    cosine = cosine_ref[...]
    sine = -sine_ref[...]
    for order in range(wide // head):
        at = order * head
        grad_query_ref[:, at : at + head] = low(
            rotate_rows(sums_ref[at : at + head, :].T * scale, cosine, sine)
        )


def in_vmem(count):
    return [pl.BlockSpec(memory_space=pltpu.SMEM)] + [
        pl.BlockSpec(memory_space=pltpu.VMEM) for _ in range(count)
    ]


def attend(bounds, query_pre, cosine, sine, place, pair):
    rows, wide = query_pre.shape
    return pl.pallas_call(
        attend_kernel,
        out_shape=(
            jax.ShapeDtypeStruct((rows, wide), jnp.bfloat16),
            jax.ShapeDtypeStruct((rows, wide), jnp.float32),
            jax.ShapeDtypeStruct((8 * -(-wide // cosine.shape[1] // 8), rows), jnp.float32),
        ),
        in_specs=in_vmem(5),
        out_specs=tuple(in_vmem(3)[1:]),
        scratch_shapes=[pltpu.VMEM((wide, rows), jnp.float32)],
        name="attend",
    )(bounds, query_pre, cosine, sine, place, pair)


def attend_back(bounds, rotated, accum, delta, cosine, sine, place, pair):
    rows, wide = rotated.shape
    return pl.pallas_call(
        attend_back_kernel,
        out_shape=(
            jax.ShapeDtypeStruct((rows, wide), jnp.bfloat16),
            jax.ShapeDtypeStruct(pair.shape, jnp.bfloat16),
        ),
        in_specs=in_vmem(7),
        out_specs=tuple(in_vmem(2)[1:]),
        scratch_shapes=[pltpu.VMEM((wide, rows), jnp.float32)],
        name="attend_back",
    )(bounds, rotated, accum, delta, cosine, sine, place, pair)


def local(
    tokens,
    lengths,
    norm1_gain,
    w_query,
    b_query,
    key_projection,
    key_bias_vector,
    value_projection,
    value_bias_vector,
    w_out,
    norm2_gain,
    w_gate,
    w_up,
    w_down,
    cotangent,
):
    rows, width = tokens.shape
    devices = lax.axis_size(WIDE)
    own_index = lax.axis_index(WIDE)
    first = own_index * rows
    index = first + jnp.arange(rows, dtype=jnp.int32)
    ends = jnp.cumsum(lengths, dtype=jnp.int32)
    starts = ends - lengths
    seq_start = jnp.max(jnp.where(starts[None, :] <= index[:, None], starts[None, :], 0), axis=1)
    lowest = jnp.min(seq_start)
    highest = first + rows - 1
    head = key_projection.shape[1]
    freq = 1.0 / ROPE_BASE ** (jnp.arange(head // 2, dtype=jnp.float32) * 2.0 / head)
    angle = (index - seq_start).astype(jnp.float32)[:, None] * freq[None, :]
    cosine_table = jnp.cos(angle)[:, None, :]
    sine_table = jnp.sin(angle)[:, None, :]
    cosine_head = jnp.concatenate([cosine_table[:, 0], cosine_table[:, 0]], axis=1)
    sine_head = jnp.concatenate([-sine_table[:, 0], sine_table[:, 0]], axis=1)
    place = jnp.concatenate([seq_start[None], index[None], jnp.zeros((6, rows), jnp.int32)], axis=0)
    bounds = jnp.stack([lowest // rows, highest // rows])
    features = w_query.shape[0]
    heads_width = w_query.shape[1]
    query_group = heads_width // head
    projected = heads_width + 2 * head

    piece = b_query.shape[1]
    small_parts = [norm1_gain, norm2_gain, b_query.reshape(-1), key_bias_vector.reshape(-1),
                   value_bias_vector.reshape(-1)]
    small_sizes = [part.shape[0] for part in small_parts]
    small_rows = -(-sum(small_sizes) // head)
    small = jnp.concatenate(small_parts)
    small = jnp.pad(small, (0, features * head - small.shape[0])).reshape(features, head)
    packed = jnp.concatenate([w_query, key_projection, value_projection, small], axis=1)
    w_project = lax.all_gather(packed, WIDE, axis=0, tiled=True)
    small_all = w_project[:, projected:].reshape(devices, features, head)[:, :small_rows]
    small_all = small_all.reshape(devices, small_rows * head).astype(jnp.float32)
    cuts = [0]
    for size in small_sizes:
        cuts.append(cuts[-1] + size)
    gain_one = small_all[:, cuts[0] : cuts[1]].reshape(-1)
    gain_two = small_all[:, cuts[1] : cuts[2]].reshape(-1)
    bias_query = small_all[:, cuts[2] : cuts[3]].reshape(devices, query_group, piece)
    bias_query = bias_query.transpose(1, 0, 2).reshape(-1)
    bias_key = small_all[:, cuts[3] : cuts[4]].reshape(-1)
    bias_value = small_all[:, cuts[4] : cuts[5]].reshape(-1)

    gate_all = spread(w_gate)
    up_all = spread(w_up)
    down_all = spread(w_down.T)

    inputs = tokens.astype(jnp.float32)
    scale_one = norm_scale(inputs)
    normed_one = low(inputs * scale_one * gain_one)
    projections = product(normed_one, w_project)
    query_pre = projections[:, :heads_width] + bias_query
    key_pre = projections[:, heads_width : heads_width + head] + bias_key
    key_rows = low(
        rotate_halves(key_pre.reshape(rows, 1, head), cosine_table, sine_table).reshape(rows, head)
    )
    value_rows = low(projections[:, heads_width + head : projected] + bias_value)

    key_value = lax.all_gather(
        jnp.concatenate([key_rows, value_rows], axis=1), WIDE, axis=0, tiled=True
    )
    w_out_all = lax.all_gather(w_out.T, WIDE, axis=0, tiled=True)
    query_rows, attended, totals = attend(
        bounds, query_pre, cosine_head, sine_head, place, key_value
    )
    totals = totals[:query_group]
    attended_low = low(attended)
    middle = inputs + sum_narrow(product_right(attended_low, w_out_all))
    scale_two = norm_scale(middle)
    normed_two = low(middle * scale_two * gain_two)

    cotangent_group = gather_group(cotangent)
    normed_group = gather_group(normed_two)
    gate = product(normed_group, gate_all)
    up_part = product(normed_group, up_all)
    sigmoid_gate = jax.nn.sigmoid(gate)
    silu_gate = gate * sigmoid_gate
    hidden = low(silu_gate * up_part)
    result = low(middle + scatter_group(product_right(hidden, down_all), rows))
    grad_down = low(product_left(cotangent_group, hidden))
    grad_hidden = product(cotangent_group, down_all)
    grad_gate = low(grad_hidden * up_part * sigmoid_gate * (1.0 + gate * (1.0 - sigmoid_gate)))
    grad_up = low(grad_hidden * silu_gate)
    grad_normed_two = scatter_group(
        product_right(grad_gate, gate_all) + product_right(grad_up, up_all), rows
    )
    grad_gate_all = low(product_left(normed_group, grad_gate))
    grad_up_all = low(product_left(normed_group, grad_up))
    grad_normed_two, grad_gate_all, grad_up_all, grad_down = lax.optimization_barrier(
        (grad_normed_two, grad_gate_all, grad_up_all, grad_down)
    )
    grad_w_down = collect(grad_down).T
    grad_w_gate = collect(grad_gate_all)
    grad_w_up = collect(grad_up_all)

    back_two, grad_gain_two = norm_back(middle, scale_two, gain_two, grad_normed_two)
    grad_middle = cotangent.astype(jnp.float32) + back_two
    grad_att = low(grad_middle)
    grad_w_out = (
        lax.psum_scatter(
            low(product_left(grad_att, attended_low)), WIDE, scatter_dimension=0, tiled=True
        )
        .astype(jnp.float32)
        .T
    )
    grad_attended = product(grad_att, w_out_all).reshape(rows, query_group, head)
    divided = grad_attended / totals.T[:, :, None]
    grad_accum = low(divided).reshape(rows, heads_width)
    delta = jnp.sum(divided * attended.reshape(rows, query_group, head), axis=2).T
    delta = jnp.pad(delta, ((0, -query_group % 8), (0, 0)))
    grad_query_pre, buffer = attend_back(
        bounds, query_rows, grad_accum, delta, cosine_head, sine_head, place, key_value
    )
    key_value_grads = lax.psum_scatter(buffer, WIDE, scatter_dimension=0, tiled=True).astype(
        jnp.float32
    )
    grad_key_pre = low(
        rotate_halves(key_value_grads[:, :head].reshape(rows, 1, head), cosine_table, -sine_table)
    ).reshape(rows, head)
    grad_value_pre = low(key_value_grads[:, head:])
    grad_project = jnp.concatenate([grad_query_pre, grad_key_pre, grad_value_pre], axis=1)
    grad_bias = jnp.sum(grad_project.astype(jnp.float32), axis=0)
    grad_normed_one = sum_narrow(product_right(grad_project, w_project[:, :projected]))
    back_one, grad_gain_one = norm_back(inputs, scale_one, gain_one, grad_normed_one)
    grad_tokens = low(grad_middle + back_one)

    small_grads = jnp.concatenate(
        [
            grad_gain_one.reshape(devices, -1),
            grad_gain_two.reshape(devices, -1),
            grad_bias[:heads_width]
            .reshape(query_group, devices, piece)
            .transpose(1, 0, 2)
            .reshape(devices, -1),
            grad_bias[heads_width : heads_width + head].reshape(devices, -1),
            grad_bias[heads_width + head :].reshape(devices, -1),
        ],
        axis=1,
    )
    small_grads = jnp.pad(small_grads, ((0, 0), (0, features * head - small_grads.shape[1])))
    packed_grads = low(
        jnp.concatenate(
            [product_left(normed_one, grad_project), small_grads.reshape(devices * features, head)],
            axis=1,
        )
    )
    packed_grads = lax.psum_scatter(packed_grads, WIDE, scatter_dimension=0, tiled=True).astype(
        jnp.float32
    )
    small_own = packed_grads[:, projected:].reshape(-1)
    return (
        result,
        grad_tokens,
        small_own[cuts[0] : cuts[1]],
        packed_grads[:, :heads_width],
        small_own[cuts[2] : cuts[3]].reshape(query_group, piece),
        packed_grads[:, heads_width : heads_width + head],
        small_own[cuts[3] : cuts[4]].reshape(1, piece),
        packed_grads[:, heads_width + head : projected],
        small_own[cuts[4] : cuts[5]].reshape(1, piece),
        grad_w_out,
        small_own[cuts[1] : cuts[2]],
        grad_w_gate,
        grad_w_up,
        grad_w_down,
    )


def solution(mesh):
    wide, narrow = mesh.devices.shape
    grouped = Mesh(mesh.devices.reshape(wide // 8, 2, 2, 2, narrow), WIDE + ("y",))
    rows = P(WIDE, None)
    vector = P(WIDE)
    columns = P(WIDE, "y")
    lines = P("y", WIDE)
    return jax.shard_map(
        local,
        mesh=grouped,
        in_specs=(rows, P(), vector, columns, lines, columns, lines, columns, lines, lines,
                  vector, columns, columns, lines, rows),
        out_specs=(rows, rows, vector, columns, lines, columns, lines, columns, lines, lines,
                   vector, columns, columns, lines),
        check_vma=False,
    )
```

```python
import math

import jax
import jax.numpy as jnp
from jax import lax
from jax.experimental import pallas as pl
from jax.experimental.pallas import tpu as pltpu
from jax.sharding import Mesh
from jax.sharding import PartitionSpec as P

ROPE_BASE = 10000.0
EPSILON = 1e-06


def product(left, right):
    return jnp.dot(left, right, preferred_element_type=jnp.float32)


def product_left(left, right):
    return lax.dot_general(
        left, right, (((0,), (0,)), ((), ())), preferred_element_type=jnp.float32
    )


def product_right(left, right):
    return lax.dot_general(
        left, right, (((1,), (1,)), ((), ())), preferred_element_type=jnp.float32
    )


def rotate_halves(value_rows, cosine_table, sine_table):
    middle_at = value_rows.shape[-1] // 2
    first = value_rows[..., :middle_at]
    second = value_rows[..., middle_at:]
    return jnp.concatenate(
        [first * cosine_table - second * sine_table, second * cosine_table + first * sine_table],
        axis=-1,
    )


def norm_scale(value_rows):
    return lax.rsqrt(jnp.mean(value_rows * value_rows, axis=-1, keepdims=True) + EPSILON)


def norm_back(value_rows, scale, gain, grad):
    normed = value_rows * scale
    inner = grad * gain
    back = scale * (inner - normed * jnp.mean(inner * normed, axis=-1, keepdims=True))
    return (back, jnp.sum(grad * normed, axis=0))


WIDE = ("zh", "zl", "x", "c")
GROUP = ("zl", "c")


def other(value, axis):
    return lax.ppermute(value, axis, [(0, 1), (1, 0)])


def low(value):
    return value.astype(jnp.bfloat16)


def after(value, *earlier):
    return lax.optimization_barrier((value, *earlier))[0]


def gather_group(own):
    core = other(own, "c")
    across = other(own, "zl")
    far = other(across, "c")
    return jnp.concatenate([own, core, across, far], axis=0)


def sum_core(partial, rows):
    sent = low(jnp.concatenate([partial[rows : 2 * rows], partial[3 * rows :]], axis=0))
    core = other(sent, "c").astype(jnp.float32)
    return partial[:rows] + core[:rows], low(partial[2 * rows : 3 * rows] + core[rows:])


def sum_low_z(own, across, *earlier):
    return low(own + after(other(across, "zl"), *earlier).astype(jnp.float32))


def sum_pair(mine, *earlier):
    return mine.astype(jnp.float32) + after(other(mine, "y"), *earlier).astype(jnp.float32)


def sum_narrow(partial):
    mine = low(partial)
    return mine.astype(jnp.float32) + other(mine, "y").astype(jnp.float32)


def deal(weight):
    features, hidden = weight.shape
    parts = weight.reshape(features, 4, hidden // 4).transpose(1, 0, 2)
    parts = lax.all_to_all(parts, GROUP, split_axis=0, concat_axis=0, tiled=True)
    return parts.reshape(1, 2, 1, 2 * features, hidden // 4)


def fetch_first(own):
    if lax.axis_size("zh") == 2:
        return own, other(own, "zh"), other(own, "x")
    every = lax.all_gather(own, "zh", axis=0, tiled=True)
    return every, None, None


def fetch_last(pieces, *earlier):
    own, far, near = pieces
    high = lax.axis_size("zh")
    at_x = lax.axis_index("x")
    whole = jnp.zeros((high, *own.shape[1:2], 2, *own.shape[3:]), jnp.bfloat16)
    if high == 2:
        at_high = lax.axis_index("zh")
        corner = other(after(far, *earlier), "x")
        placed = (
            (own, at_high, at_x),
            (far, 1 - at_high, at_x),
            (near, at_high, 1 - at_x),
            (corner, 1 - at_high, 1 - at_x),
        )
    else:
        placed = ((own, 0, at_x), (other(own, "x"), 0, 1 - at_x))
    return whole, placed


def assemble(whole_placed, *earlier):
    whole, placed = whole_placed
    for piece, high_place, x_place in placed:
        whole = lax.dynamic_update_slice(
            whole, after(piece, *earlier), (high_place, 0, x_place, 0, 0)
        )
    high, low_z, across, features, hidden = whole.shape
    return whole.reshape(high * low_z * across * features, hidden)


def split_half(grad, axis, position):
    at = lax.axis_index(axis)
    sent = lax.dynamic_slice_in_dim(grad, 1 - at, 1, position)
    kept = lax.dynamic_slice_in_dim(grad, at, 1, position)
    return kept, other(sent, axis)


def add_half(halves, *earlier):
    kept, came = halves
    return low(kept.astype(jnp.float32) + after(came, *earlier).astype(jnp.float32))


def collect_first(grad):
    high = lax.axis_size("zh")
    return split_half(grad.reshape(high, 2, 2, grad.shape[0] // (4 * high), grad.shape[1]), "x", 2)


def collect_second(halves, *earlier):
    summed = add_half(halves, *earlier)
    if lax.axis_size("zh") == 2:
        return split_half(summed, "zh", 0)
    return lax.psum_scatter(summed, "zh", scatter_dimension=0, tiled=True)


def collect_last(halves, *earlier):
    if lax.axis_size("zh") == 2:
        halves = add_half(halves, *earlier)
    features = halves.shape[3] // 2
    hidden = halves.shape[4]
    parts = halves.reshape(4, features, hidden)
    return lax.all_to_all(parts, GROUP, split_axis=0, concat_axis=0, tiled=True)


def collect_end(parts):
    count, features, hidden = parts.shape
    return parts.transpose(1, 0, 2).reshape(features, count * hidden).astype(jnp.float32)


def rotate_rows(value_rows, cosine, sine):
    return value_rows * cosine + pltpu.roll(value_rows, value_rows.shape[1] // 2, 1) * sine


def mask_bias(place_ref, begin, span):
    rows = place_ref.shape[1]
    key_index = begin + lax.broadcasted_iota(jnp.int32, (span, rows), 0)
    allowed = (key_index >= place_ref[0:1, :]) & (key_index <= place_ref[1:2, :])
    return jnp.where(allowed, 0.0, -1e30)


def turned(value):
    return value.astype(jnp.float32).T.astype(value.dtype)


def attend_kernel(
    bounds_ref, query_ref, cosine_ref, sine_ref, place_ref, pair_ref,
    rotated_ref, attended_ref, totals_ref, sums_ref,
):
    rows, wide = query_ref.shape
    head = cosine_ref.shape[1]
    factor = math.log2(math.e) / math.sqrt(head)
    cosine = cosine_ref[...]
    sine = sine_ref[...]
    for at in range(0, wide, head):
        rotated_ref[:, at : at + head] = low(
            rotate_rows(query_ref[:, at : at + head], cosine, sine)
        )
    sums_ref[...] = jnp.zeros_like(sums_ref)
    totals_ref[...] = jnp.zeros_like(totals_ref)

    def step(number, carry):
        begin = pl.multiple_of(number * rows, rows)
        keys = pair_ref[pl.ds(begin, rows), :head]
        values_turned = turned(pair_ref[pl.ds(begin, rows), head:])
        bias = mask_bias(place_ref, begin, rows)
        for order in range(wide // head):
            at = order * head
            scores = product_right(keys, rotated_ref[:, at : at + head])
            weights = jnp.exp2(scores * factor + bias)
            totals_ref[order : order + 1, :] += jnp.sum(weights, axis=0, keepdims=True)
            sums_ref[at : at + head, :] += product(values_turned, low(weights))
        return carry

    lax.fori_loop(bounds_ref[0], bounds_ref[1] + 1, step, 0)
    for order in range(wide // head):
        at = order * head
        attended_ref[:, at : at + head] = (
            sums_ref[at : at + head, :] / totals_ref[order : order + 1, :]
        ).T


def attend_back_kernel(
    bounds_ref, rotated_ref, grad_ref, attended_ref, totals_ref, cosine_ref, sine_ref, place_ref,
    pair_ref, grad_query_ref, grad_pair_ref, sums_ref, accum_ref, delta_ref,
):
    rows, wide = rotated_ref.shape
    head = cosine_ref.shape[1]
    scale = 1.0 / math.sqrt(head)
    factor = math.log2(math.e) * scale
    for order in range(wide // head):
        at = order * head
        totals = jnp.broadcast_to(totals_ref[order : order + 1, :], (head, rows)).T
        divided = grad_ref[:, at : at + head] / totals
        accum_ref[:, at : at + head] = low(divided)
        delta_ref[order : order + 1, :] = jnp.sum(
            (divided * attended_ref[:, at : at + head]).T, axis=0, keepdims=True
        )

    def clear(number, carry):
        begin = pl.multiple_of(number * rows, rows)
        grad_pair_ref[pl.ds(begin, rows), :] = jnp.zeros((rows, 2 * head), jnp.bfloat16)
        return carry

    lax.fori_loop(0, grad_pair_ref.shape[0] // rows, clear, 0)
    sums_ref[...] = jnp.zeros_like(sums_ref)

    def step(number, carry):
        begin = pl.multiple_of(number * rows, rows)
        keys = pair_ref[pl.ds(begin, rows), :head]
        values = pair_ref[pl.ds(begin, rows), head:]
        keys_turned = turned(keys)
        bias = mask_bias(place_ref, begin, rows)
        grad_keys = jnp.zeros((rows, head), jnp.float32)
        grad_values = jnp.zeros((rows, head), jnp.float32)
        for order in range(wide // head):
            at = order * head
            query = rotated_ref[:, at : at + head]
            accum = accum_ref[:, at : at + head]
            weights = jnp.exp2(product_right(keys, query) * factor + bias)
            grad_scores = low(
                weights * (product_right(values, accum) - delta_ref[order : order + 1, :])
            )
            grad_values += product(low(weights), accum)
            grad_keys += product(grad_scores, query)
            sums_ref[at : at + head, :] += product(keys_turned, grad_scores)
        grad_pair_ref[pl.ds(begin, rows), :head] = low(grad_keys * scale)
        grad_pair_ref[pl.ds(begin, rows), head:] = low(grad_values)
        return carry

    lax.fori_loop(bounds_ref[0], bounds_ref[1] + 1, step, 0)
    cosine = cosine_ref[...]
    sine = -sine_ref[...]
    for order in range(wide // head):
        at = order * head
        grad_query_ref[:, at : at + head] = low(
            rotate_rows(sums_ref[at : at + head, :].T * scale, cosine, sine)
        )


def in_vmem(count):
    return [pl.BlockSpec(memory_space=pltpu.SMEM)] + [
        pl.BlockSpec(memory_space=pltpu.VMEM) for _ in range(count)
    ]


def attend(bounds, query_pre, cosine, sine, place, pair):
    rows, wide = query_pre.shape
    return pl.pallas_call(
        attend_kernel,
        out_shape=(
            jax.ShapeDtypeStruct((rows, wide), jnp.bfloat16),
            jax.ShapeDtypeStruct((rows, wide), jnp.float32),
            jax.ShapeDtypeStruct((8 * -(-wide // cosine.shape[1] // 8), rows), jnp.float32),
        ),
        in_specs=in_vmem(5),
        out_specs=tuple(in_vmem(3)[1:]),
        scratch_shapes=[pltpu.VMEM((wide, rows), jnp.float32)],
        cost_estimate=pl.CostEstimate(
            flops=4 * 9 * rows * rows * wide, transcendentals=9 * rows * rows * 6, bytes_accessed=20 << 20
        ),
        name="attend",
    )(bounds, query_pre, cosine, sine, place, pair)


def attend_back(bounds, rotated, grad, attended, totals, cosine, sine, place, pair):
    rows, wide = rotated.shape
    return pl.pallas_call(
        attend_back_kernel,
        out_shape=(
            jax.ShapeDtypeStruct((rows, wide), jnp.bfloat16),
            jax.ShapeDtypeStruct(pair.shape, jnp.bfloat16),
        ),
        in_specs=in_vmem(8),
        out_specs=tuple(in_vmem(2)[1:]),
        scratch_shapes=[
            pltpu.VMEM((wide, rows), jnp.float32),
            pltpu.VMEM((rows, wide), jnp.bfloat16),
            pltpu.VMEM(totals.shape, jnp.float32),
        ],
        cost_estimate=pl.CostEstimate(
            flops=10 * 9 * rows * rows * wide, transcendentals=9 * rows * rows * 6, bytes_accessed=30 << 20
        ),
        name="attend_back",
    )(bounds, rotated, grad, attended, totals, cosine, sine, place, pair)


def local(
    tokens,
    lengths,
    norm1_gain,
    w_query,
    b_query,
    key_projection,
    key_bias_vector,
    value_projection,
    value_bias_vector,
    w_out,
    norm2_gain,
    w_gate,
    w_up,
    w_down,
    cotangent,
):
    rows, width = tokens.shape
    devices = lax.axis_size(WIDE)
    own_index = lax.axis_index(WIDE)
    first = own_index * rows
    index = first + jnp.arange(rows, dtype=jnp.int32)
    ends = jnp.cumsum(lengths, dtype=jnp.int32)
    starts = ends - lengths
    seq_start = jnp.max(jnp.where(starts[None, :] <= index[:, None], starts[None, :], 0), axis=1)
    lowest = jnp.min(seq_start)
    highest = first + rows - 1
    head = key_projection.shape[1]
    freq = 1.0 / ROPE_BASE ** (jnp.arange(head // 2, dtype=jnp.float32) * 2.0 / head)
    angle = (index - seq_start).astype(jnp.float32)[:, None] * freq[None, :]
    cosine_table = jnp.cos(angle)[:, None, :]
    sine_table = jnp.sin(angle)[:, None, :]
    cosine_head = jnp.concatenate([cosine_table[:, 0], cosine_table[:, 0]], axis=1)
    sine_head = jnp.concatenate([-sine_table[:, 0], sine_table[:, 0]], axis=1)
    place = jnp.concatenate([seq_start[None], index[None], jnp.zeros((6, rows), jnp.int32)], axis=0)
    bounds = jnp.stack([lowest // rows, highest // rows])
    features = w_query.shape[0]
    heads_width = w_query.shape[1]
    query_group = heads_width // head
    projected = heads_width + 2 * head

    piece = b_query.shape[1]
    small_parts = [norm1_gain, norm2_gain, b_query.reshape(-1), key_bias_vector.reshape(-1),
                   value_bias_vector.reshape(-1)]
    small_sizes = [part.shape[0] for part in small_parts]
    small_rows = -(-sum(small_sizes) // head)
    small = jnp.concatenate(small_parts)
    small = jnp.pad(small, (0, features * head - small.shape[0])).reshape(features, head)
    packed = jnp.concatenate([w_query, key_projection, value_projection, small, w_out.T], axis=1)
    gate_own = deal(w_gate)
    up_own = deal(w_up)
    w_packed = after(lax.all_gather(packed, WIDE, axis=0, tiled=True), gate_own, up_own)
    w_project = w_packed[:, : projected + head]
    w_out_all = w_packed[:, projected + head :]
    small_all = w_project[:, projected:].reshape(devices, features, head)[:, :small_rows]
    small_all = small_all.reshape(devices, small_rows * head).astype(jnp.float32)
    cuts = [0]
    for size in small_sizes:
        cuts.append(cuts[-1] + size)
    gain_one = small_all[:, cuts[0] : cuts[1]].reshape(-1)
    gain_two = small_all[:, cuts[1] : cuts[2]].reshape(-1)
    bias_query = small_all[:, cuts[2] : cuts[3]].reshape(devices, query_group, piece)
    bias_query = bias_query.transpose(1, 0, 2).reshape(-1)
    bias_key = small_all[:, cuts[3] : cuts[4]].reshape(-1)
    bias_value = small_all[:, cuts[4] : cuts[5]].reshape(-1)


    inputs = tokens.astype(jnp.float32)
    scale_one = norm_scale(inputs)
    normed_one = low(inputs * scale_one * gain_one)
    projections = product(normed_one, w_project)
    query_pre = projections[:, :heads_width] + bias_query
    key_pre = projections[:, heads_width : heads_width + head] + bias_key
    key_rows = low(
        rotate_halves(key_pre.reshape(rows, 1, head), cosine_table, sine_table).reshape(rows, head)
    )
    value_rows = low(projections[:, heads_width + head : projected] + bias_value)

    key_value = lax.all_gather(
        jnp.concatenate([key_rows, value_rows], axis=1), WIDE, axis=0, tiled=True
    )
    down_own = deal(w_down.T)
    cotangent_group = gather_group(cotangent)
    cotangent_turned = cotangent_group.T
    gate_own, up_own, down_own, key_value, cotangent_group, cotangent_turned = (
        lax.optimization_barrier(
            (gate_own, up_own, down_own, key_value, cotangent_group, cotangent_turned)
        )
    )
    gate_pieces = fetch_first(gate_own)
    up_pieces = fetch_first(up_own)
    down_pieces = fetch_first(down_own)
    query_rows, attended, totals = attend(
        bounds, query_pre, cosine_head, sine_head, place, key_value
    )
    attended_low = low(attended)
    attention = product_right(attended_low, w_out_all)
    gate_pieces = fetch_last(gate_pieces, attention)
    middle = inputs + sum_narrow(attention)
    scale_two = norm_scale(middle)
    normed_two = low(middle * scale_two * gain_two)
    up_pieces = fetch_last(up_pieces, normed_two)
    normed_group = gather_group(normed_two)
    normed_turned = lax.optimization_barrier(normed_group.T)
    gate_all = assemble(gate_pieces, attention)
    gate = product(normed_group, gate_all)
    up_all = assemble(up_pieces, normed_two)
    down_pieces = fetch_last(down_pieces, normed_group)
    up_part = product(normed_group, up_all)
    sigmoid_gate = jax.nn.sigmoid(gate)
    silu_gate = gate * sigmoid_gate
    hidden = low(silu_gate * up_part)
    grad_down = low(product(cotangent_turned, hidden))
    down_halves = collect_first(grad_down)
    down_all = assemble(down_pieces, normed_group)
    grad_hidden = product(after(cotangent_group, grad_down), down_all)
    grad_gate = low(grad_hidden * up_part * sigmoid_gate * (1.0 + gate * (1.0 - sigmoid_gate)))
    grad_up = low(grad_hidden * silu_gate)
    grad_normed_part = product_right(grad_gate, gate_all) + product_right(grad_up, up_all)
    grad_normed_own, grad_normed_across = sum_core(grad_normed_part, rows)
    grad_gate_all = low(
        product(normed_turned, after(grad_gate, grad_normed_across, down_halves[1]))
    )
    down_halves = collect_second(down_halves, grad_normed_across)
    gate_halves = collect_first(grad_gate_all)
    grad_up_all = low(product(normed_turned, after(grad_up, grad_gate_all, down_halves[0])))
    up_halves = collect_first(grad_up_all)
    grad_normed_mine = sum_low_z(grad_normed_own, grad_normed_across, grad_up_all)
    down_part = product_right(after(hidden, grad_normed_mine), down_all)
    down_mine, down_across = sum_core(down_part, rows)
    grad_normed_two = sum_pair(grad_normed_mine, down_across, gate_halves[1])
    down_mine = sum_low_z(down_mine, down_across, grad_normed_two)
    result = low(middle + sum_pair(down_mine))
    down_parts = collect_last(down_halves, grad_normed_two)
    gate_halves = collect_second(gate_halves, grad_normed_two)

    back_two, grad_gain_two = norm_back(middle, scale_two, gain_two, grad_normed_two)
    grad_middle = cotangent.astype(jnp.float32) + back_two
    grad_att = low(grad_middle)
    grad_out_all = product_left(attended_low, grad_att).T
    grad_attended = product(grad_att, w_out_all)
    up_halves = collect_second(up_halves, gate_halves[0])
    grad_query_pre, buffer = attend_back(
        bounds, query_rows, after(grad_attended, up_halves[0], down_halves[1]), attended, totals,
        cosine_head, sine_head, place, key_value,
    )
    key_value_grads = lax.psum_scatter(buffer, WIDE, scatter_dimension=0, tiled=True)
    gate_parts = collect_last(gate_halves, buffer)
    square_grads = low(
        jnp.concatenate([product_left(grad_query_pre, normed_one).T, grad_out_all], axis=1)
    )
    up_parts = collect_last(up_halves, gate_parts)
    key_value_grads = after(
        key_value_grads, square_grads, gate_parts, down_parts, up_parts
    ).astype(jnp.float32)
    square_grads = lax.psum_scatter(square_grads, WIDE, scatter_dimension=0, tiled=True)
    grad_key_pre = low(
        rotate_halves(key_value_grads[:, :head].reshape(rows, 1, head), cosine_table, -sine_table)
    ).reshape(rows, head)
    grad_value_pre = low(key_value_grads[:, head:])
    grad_pair = jnp.concatenate([grad_key_pre, grad_value_pre], axis=1)
    grad_project = jnp.concatenate([grad_query_pre, grad_pair], axis=1)
    grad_bias = jnp.sum(grad_project.astype(jnp.float32), axis=0)
    grad_normed_one = sum_narrow(product_right(grad_project, w_project[:, :projected]))
    back_one, grad_gain_one = norm_back(inputs, scale_one, gain_one, grad_normed_one)
    grad_tokens = low(grad_middle + back_one)

    small_grads = jnp.concatenate(
        [
            grad_gain_one.reshape(devices, -1),
            grad_gain_two.reshape(devices, -1),
            grad_bias[:heads_width]
            .reshape(query_group, devices, piece)
            .transpose(1, 0, 2)
            .reshape(devices, -1),
            grad_bias[heads_width : heads_width + head].reshape(devices, -1),
            grad_bias[heads_width + head :].reshape(devices, -1),
        ],
        axis=1,
    )
    small_grads = jnp.pad(small_grads, ((0, 0), (0, features * head - small_grads.shape[1])))
    packed_grads = low(
        jnp.concatenate(
            [product_left(grad_pair, normed_one).T, small_grads.reshape(devices * features, head)],
            axis=1,
        )
    )
    packed_grads = lax.psum_scatter(packed_grads, WIDE, scatter_dimension=0, tiled=True).astype(
        jnp.float32
    )
    small_own = packed_grads[:, 2 * head :].reshape(-1)
    square_grads = square_grads.astype(jnp.float32)
    grad_w_out = square_grads[:, heads_width:].T
    grad_w_down = collect_end(down_parts).T
    grad_w_gate = collect_end(gate_parts)
    grad_w_up = collect_end(up_parts)
    return (
        result,
        grad_tokens,
        small_own[cuts[0] : cuts[1]],
        square_grads[:, :heads_width],
        small_own[cuts[2] : cuts[3]].reshape(query_group, piece),
        packed_grads[:, :head],
        small_own[cuts[3] : cuts[4]].reshape(1, piece),
        packed_grads[:, head : 2 * head],
        small_own[cuts[4] : cuts[5]].reshape(1, piece),
        grad_w_out,
        small_own[cuts[1] : cuts[2]],
        grad_w_gate,
        grad_w_up,
        grad_w_down,
    )


def solution(mesh):
    wide, narrow = mesh.devices.shape
    grouped = Mesh(mesh.devices.reshape(wide // 8, 2, 2, 2, narrow), WIDE + ("y",))
    rows = P(WIDE, None)
    vector = P(WIDE)
    columns = P(WIDE, "y")
    lines = P("y", WIDE)
    return jax.shard_map(
        local,
        mesh=grouped,
        in_specs=(rows, P(), vector, columns, lines, columns, lines, columns, lines, lines,
                  vector, columns, columns, lines, rows),
        out_specs=(rows, rows, vector, columns, lines, columns, lines, columns, lines, lines,
                   vector, columns, columns, lines),
        check_vma=False,
    )
```

```python
import math

import jax
import jax.numpy as jnp
from jax import lax
from jax.experimental import pallas as pl
from jax.experimental.pallas import tpu as pltpu
from jax.sharding import Mesh
from jax.sharding import PartitionSpec as P

ROPE_BASE = 10000.0
EPSILON = 1e-06


def product(left, right):
    return jnp.dot(left, right, preferred_element_type=jnp.float32)


def product_left(left, right):
    return lax.dot_general(
        left, right, (((0,), (0,)), ((), ())), preferred_element_type=jnp.float32
    )


def product_right(left, right):
    return lax.dot_general(
        left, right, (((1,), (1,)), ((), ())), preferred_element_type=jnp.float32
    )


def rotate_halves(value_rows, cosine_table, sine_table):
    middle_at = value_rows.shape[-1] // 2
    first = value_rows[..., :middle_at]
    second = value_rows[..., middle_at:]
    return jnp.concatenate(
        [first * cosine_table - second * sine_table, second * cosine_table + first * sine_table],
        axis=-1,
    )


def norm_scale(value_rows):
    return lax.rsqrt(jnp.mean(value_rows * value_rows, axis=-1, keepdims=True) + EPSILON)


def norm_back(value_rows, scale, gain, grad):
    normed = value_rows * scale
    inner = grad * gain
    back = scale * (inner - normed * jnp.mean(inner * normed, axis=-1, keepdims=True))
    return (back, jnp.sum(grad * normed, axis=0))


WIDE = ("z", "x", "c")
GROUP = ("x", "c")


def other(value, axis):
    return lax.ppermute(value, axis, [(0, 1), (1, 0)])


def low(value):
    return value.astype(jnp.bfloat16)


def after(value, *earlier):
    return lax.optimization_barrier((value, *earlier))[0]


def gather_group(own):
    core = other(own, "c")
    across = other(own, "x")
    far = other(across, "c")
    return jnp.concatenate([own, core, across, far], axis=0)


def sum_core(partial, rows):
    sent = low(jnp.concatenate([partial[rows : 2 * rows], partial[3 * rows :]], axis=0))
    core = other(sent, "c").astype(jnp.float32)
    return partial[:rows] + core[:rows], low(partial[2 * rows : 3 * rows] + core[rows:])


def sum_across(own, across, *earlier):
    return low(own + after(other(across, "x"), *earlier).astype(jnp.float32))


def sum_pair(mine, *earlier):
    return mine.astype(jnp.float32) + after(other(mine, "y"), *earlier).astype(jnp.float32)


def sum_narrow(partial):
    mine = low(partial)
    return mine.astype(jnp.float32) + other(mine, "y").astype(jnp.float32)


def deal(weight):
    features, hidden = weight.shape
    parts = weight.reshape(features, 4, hidden // 4).transpose(1, 0, 2)
    parts = lax.all_to_all(parts, GROUP, split_axis=0, concat_axis=0, tiled=True)
    return parts.reshape(4 * features, hidden // 4)


def gather_z(own):
    return lax.all_gather(own, "z", axis=0, tiled=True)


def scatter_z(whole):
    return lax.psum_scatter(whole, "z", scatter_dimension=0, tiled=True)


def undeal(grad):
    features = grad.shape[0] // 4
    parts = grad.reshape(4, features, grad.shape[1])
    return lax.all_to_all(parts, GROUP, split_axis=0, concat_axis=0, tiled=True)


def undeal_end(parts):
    count, features, hidden = parts.shape
    return parts.transpose(1, 0, 2).reshape(features, count * hidden).astype(jnp.float32)


def gather_rest(column, rows):
    own = column.reshape(-1, 1, 1, rows, column.shape[1])
    near = other(own, "x")
    at_x = lax.axis_index("x")
    at_c = lax.axis_index("c")
    whole = jnp.zeros((own.shape[0], 2, 2, *own.shape[3:]), column.dtype)
    for piece, x_place, c_place in (
        (own, at_x, at_c),
        (other(own, "c"), at_x, 1 - at_c),
        (near, 1 - at_x, at_c),
        (other(near, "c"), 1 - at_x, 1 - at_c),
    ):
        whole = lax.dynamic_update_slice(whole, piece, (0, x_place, c_place, 0, 0))
    return whole.reshape(-1, column.shape[1])


def halve(whole, axis, position):
    at = lax.axis_index(axis)
    sent = lax.dynamic_slice_in_dim(whole, 1 - at, 1, position)
    kept = lax.dynamic_slice_in_dim(whole, at, 1, position)
    return low(kept.astype(jnp.float32) + other(sent, axis).astype(jnp.float32))


def scatter_start(whole, rows):
    parts = whole.reshape(-1, 2, 2, rows, whole.shape[1])
    return halve(halve(parts, "c", 2), "x", 1).reshape(-1, whole.shape[1])


def rotate_rows(value_rows, cosine, sine):
    return value_rows * cosine + pltpu.roll(value_rows, value_rows.shape[1] // 2, 1) * sine


def mask_bias(place_ref, begin, span):
    rows = place_ref.shape[1]
    key_index = begin + lax.broadcasted_iota(jnp.int32, (span, rows), 0)
    allowed = (key_index >= place_ref[0:1, :]) & (key_index <= place_ref[1:2, :])
    return jnp.where(allowed, 0.0, -1e30)


def turned(value):
    return value.astype(jnp.float32).T.astype(value.dtype)


def attend_kernel(
    bounds_ref, query_ref, cosine_ref, sine_ref, place_ref, pair_ref,
    rotated_ref, attended_ref, totals_ref, sums_ref,
):
    rows, wide = query_ref.shape
    head = cosine_ref.shape[1]
    factor = math.log2(math.e) / math.sqrt(head)
    cosine = cosine_ref[...]
    sine = sine_ref[...]
    for at in range(0, wide, head):
        rotated_ref[:, at : at + head] = low(
            rotate_rows(query_ref[:, at : at + head], cosine, sine)
        )
    sums_ref[...] = jnp.zeros_like(sums_ref)
    totals_ref[...] = jnp.zeros_like(totals_ref)

    def step(number, carry):
        begin = pl.multiple_of(number * rows, rows)
        keys = pair_ref[pl.ds(begin, rows), :head]
        values_turned = turned(pair_ref[pl.ds(begin, rows), head:])
        bias = mask_bias(place_ref, begin, rows)
        for order in range(wide // head):
            at = order * head
            scores = product_right(keys, rotated_ref[:, at : at + head])
            weights = jnp.exp2(scores * factor + bias)
            totals_ref[order : order + 1, :] += jnp.sum(weights, axis=0, keepdims=True)
            sums_ref[at : at + head, :] += product(values_turned, low(weights))
        return carry

    lax.fori_loop(bounds_ref[0], bounds_ref[1] + 1, step, 0)
    for order in range(wide // head):
        at = order * head
        attended_ref[:, at : at + head] = (
            sums_ref[at : at + head, :] / totals_ref[order : order + 1, :]
        ).T


def attend_back_kernel(
    bounds_ref, rotated_ref, grad_ref, attended_ref, totals_ref, cosine_ref, sine_ref, place_ref,
    pair_ref, grad_query_ref, grad_pair_ref, sums_ref, accum_ref, delta_ref,
):
    rows, wide = rotated_ref.shape
    head = cosine_ref.shape[1]
    scale = 1.0 / math.sqrt(head)
    factor = math.log2(math.e) * scale
    for order in range(wide // head):
        at = order * head
        totals = jnp.broadcast_to(totals_ref[order : order + 1, :], (head, rows)).T
        divided = grad_ref[:, at : at + head] / totals
        accum_ref[:, at : at + head] = low(divided)
        delta_ref[order : order + 1, :] = jnp.sum(
            (divided * attended_ref[:, at : at + head]).T, axis=0, keepdims=True
        )

    def clear(number, carry):
        begin = pl.multiple_of(number * rows, rows)
        grad_pair_ref[pl.ds(begin, rows), :] = jnp.zeros((rows, 2 * head), jnp.bfloat16)
        return carry

    lax.fori_loop(0, grad_pair_ref.shape[0] // rows, clear, 0)
    sums_ref[...] = jnp.zeros_like(sums_ref)

    def step(number, carry):
        begin = pl.multiple_of(number * rows, rows)
        keys = pair_ref[pl.ds(begin, rows), :head]
        values = pair_ref[pl.ds(begin, rows), head:]
        keys_turned = turned(keys)
        bias = mask_bias(place_ref, begin, rows)
        grad_keys = jnp.zeros((rows, head), jnp.float32)
        grad_values = jnp.zeros((rows, head), jnp.float32)
        for order in range(wide // head):
            at = order * head
            query = rotated_ref[:, at : at + head]
            accum = accum_ref[:, at : at + head]
            weights = jnp.exp2(product_right(keys, query) * factor + bias)
            grad_scores = low(
                weights * (product_right(values, accum) - delta_ref[order : order + 1, :])
            )
            grad_values += product(low(weights), accum)
            grad_keys += product(grad_scores, query)
            sums_ref[at : at + head, :] += product(keys_turned, grad_scores)
        grad_pair_ref[pl.ds(begin, rows), :head] = low(grad_keys * scale)
        grad_pair_ref[pl.ds(begin, rows), head:] = low(grad_values)
        return carry

    lax.fori_loop(bounds_ref[0], bounds_ref[1] + 1, step, 0)
    cosine = cosine_ref[...]
    sine = -sine_ref[...]
    for order in range(wide // head):
        at = order * head
        grad_query_ref[:, at : at + head] = low(
            rotate_rows(sums_ref[at : at + head, :].T * scale, cosine, sine)
        )


def in_vmem(count):
    return [pl.BlockSpec(memory_space=pltpu.SMEM)] + [
        pl.BlockSpec(memory_space=pltpu.VMEM) for _ in range(count)
    ]


def attend(bounds, query_pre, cosine, sine, place, pair):
    rows, wide = query_pre.shape
    return pl.pallas_call(
        attend_kernel,
        out_shape=(
            jax.ShapeDtypeStruct((rows, wide), jnp.bfloat16),
            jax.ShapeDtypeStruct((rows, wide), jnp.float32),
            jax.ShapeDtypeStruct((8 * -(-wide // cosine.shape[1] // 8), rows), jnp.float32),
        ),
        in_specs=in_vmem(5),
        out_specs=tuple(in_vmem(3)[1:]),
        scratch_shapes=[pltpu.VMEM((wide, rows), jnp.float32)],
        cost_estimate=pl.CostEstimate(
            flops=4 * 9 * rows * rows * wide, transcendentals=9 * rows * rows * 6, bytes_accessed=20 << 20
        ),
        name="attend",
    )(bounds, query_pre, cosine, sine, place, pair)


def attend_back(bounds, rotated, grad, attended, totals, cosine, sine, place, pair):
    rows, wide = rotated.shape
    return pl.pallas_call(
        attend_back_kernel,
        out_shape=(
            jax.ShapeDtypeStruct((rows, wide), jnp.bfloat16),
            jax.ShapeDtypeStruct(pair.shape, jnp.bfloat16),
        ),
        in_specs=in_vmem(8),
        out_specs=tuple(in_vmem(2)[1:]),
        scratch_shapes=[
            pltpu.VMEM((wide, rows), jnp.float32),
            pltpu.VMEM((rows, wide), jnp.bfloat16),
            pltpu.VMEM(totals.shape, jnp.float32),
        ],
        cost_estimate=pl.CostEstimate(
            flops=10 * 9 * rows * rows * wide, transcendentals=9 * rows * rows * 6, bytes_accessed=30 << 20
        ),
        name="attend_back",
    )(bounds, rotated, grad, attended, totals, cosine, sine, place, pair)


def local(
    tokens,
    lengths,
    norm1_gain,
    w_query,
    b_query,
    key_projection,
    key_bias_vector,
    value_projection,
    value_bias_vector,
    w_out,
    norm2_gain,
    w_gate,
    w_up,
    w_down,
    cotangent,
):
    rows, width = tokens.shape
    devices = lax.axis_size(WIDE)
    own_index = lax.axis_index(WIDE)
    first = own_index * rows
    index = first + jnp.arange(rows, dtype=jnp.int32)
    ends = jnp.cumsum(lengths, dtype=jnp.int32)
    starts = ends - lengths
    seq_start = jnp.max(jnp.where(starts[None, :] <= index[:, None], starts[None, :], 0), axis=1)
    lowest = jnp.min(seq_start)
    highest = first + rows - 1
    head = key_projection.shape[1]
    freq = 1.0 / ROPE_BASE ** (jnp.arange(head // 2, dtype=jnp.float32) * 2.0 / head)
    angle = (index - seq_start).astype(jnp.float32)[:, None] * freq[None, :]
    cosine_table = jnp.cos(angle)[:, None, :]
    sine_table = jnp.sin(angle)[:, None, :]
    cosine_head = jnp.concatenate([cosine_table[:, 0], cosine_table[:, 0]], axis=1)
    sine_head = jnp.concatenate([-sine_table[:, 0], sine_table[:, 0]], axis=1)
    place = jnp.concatenate([seq_start[None], index[None], jnp.zeros((6, rows), jnp.int32)], axis=0)
    bounds = jnp.stack([lowest // rows, highest // rows])
    features = w_query.shape[0]
    heads_width = w_query.shape[1]
    query_group = heads_width // head
    projected = heads_width + 2 * head

    piece = b_query.shape[1]
    small_parts = [norm1_gain, norm2_gain, b_query.reshape(-1), key_bias_vector.reshape(-1),
                   value_bias_vector.reshape(-1)]
    small_sizes = [part.shape[0] for part in small_parts]
    small_rows = -(-sum(small_sizes) // head)
    small = jnp.concatenate(small_parts)
    small = jnp.pad(small, (0, features * head - small.shape[0])).reshape(features, head)
    pair_column = gather_z(
        jnp.concatenate([key_projection, value_projection, small], axis=1)
    )
    square_column = gather_z(
        after(jnp.concatenate([w_query, w_out.T], axis=1), small)
    )
    gate_own = deal(w_gate)
    w_pair = gather_rest(pair_column, features)
    small_all = w_pair[:, 2 * head :].reshape(devices, features, head)[:, :small_rows]
    small_all = small_all.reshape(devices, small_rows * head).astype(jnp.float32)
    cuts = [0]
    for size in small_sizes:
        cuts.append(cuts[-1] + size)
    gain_one = small_all[:, cuts[0] : cuts[1]].reshape(-1)
    gain_two = small_all[:, cuts[1] : cuts[2]].reshape(-1)
    bias_query = small_all[:, cuts[2] : cuts[3]].reshape(devices, query_group, piece)
    bias_query = bias_query.transpose(1, 0, 2).reshape(-1)
    bias_key = small_all[:, cuts[3] : cuts[4]].reshape(-1)
    bias_value = small_all[:, cuts[4] : cuts[5]].reshape(-1)


    inputs = tokens.astype(jnp.float32)
    scale_one = norm_scale(inputs)
    normed_one = low(inputs * scale_one * gain_one)
    projections = product(normed_one, w_pair[:, : 2 * head])
    key_pre = projections[:, :head] + bias_key
    key_rows = low(
        rotate_halves(key_pre.reshape(rows, 1, head), cosine_table, sine_table).reshape(rows, head)
    )
    value_rows = low(projections[:, head:] + bias_value)
    key_value = jnp.concatenate([key_rows, value_rows], axis=1)
    key_value, gate_own = lax.optimization_barrier((key_value, gate_own))
    key_value_column = gather_z(key_value)
    up_own = deal(after(w_up, key_value))
    w_square = gather_rest(square_column, features)
    w_query_all = w_square[:, :heads_width]
    w_out_all = w_square[:, heads_width:]
    query_pre = product(normed_one, w_query_all) + bias_query
    key_value_column = after(key_value_column, up_own)
    gate_all = gather_z(after(gate_own, key_value_column))
    up_all = gather_z(after(up_own, key_value_column))
    key_value = gather_rest(key_value_column, rows)
    down_own = deal(after(w_down, key_value_column).T)
    down_all = gather_z(down_own)
    cotangent_group = gather_group(after(cotangent, key_value))
    cotangent_turned = lax.optimization_barrier(cotangent_group.T)
    query_rows, attended, totals = attend(
        bounds, query_pre, cosine_head, sine_head, place, key_value
    )
    attended_low = low(attended)
    middle = inputs + sum_narrow(product_right(attended_low, w_out_all))
    scale_two = norm_scale(middle)
    normed_two = low(middle * scale_two * gain_two)
    normed_group = gather_group(normed_two)
    normed_turned = lax.optimization_barrier(normed_group.T)
    gate = product(normed_group, gate_all)
    up_part = product(normed_group, up_all)
    sigmoid_gate = jax.nn.sigmoid(gate)
    silu_gate = gate * sigmoid_gate
    hidden = low(silu_gate * up_part)
    grad_down = low(product(cotangent_turned, hidden))
    down_sums = scatter_z(grad_down)
    grad_hidden = product(after(cotangent_group, grad_down), down_all)
    grad_gate = low(grad_hidden * up_part * sigmoid_gate * (1.0 + gate * (1.0 - sigmoid_gate)))
    grad_up = low(grad_hidden * silu_gate)
    grad_normed_part = product_right(grad_gate, gate_all) + product_right(grad_up, up_all)
    grad_normed_own, grad_normed_across = sum_core(grad_normed_part, rows)
    grad_gate_all = low(product(normed_turned, after(grad_gate, grad_normed_across)))
    gate_sums = scatter_z(grad_gate_all)
    grad_up_all = low(product(normed_turned, after(grad_up, grad_gate_all)))
    up_sums = scatter_z(grad_up_all)
    grad_normed_mine = sum_across(grad_normed_own, grad_normed_across, grad_up_all)
    down_part = product_right(after(hidden, grad_normed_mine), down_all)
    down_mine, down_across = sum_core(down_part, rows)
    grad_normed_two = sum_pair(grad_normed_mine, down_across)
    down_mine = sum_across(down_mine, down_across, grad_normed_two)
    result = low(middle + sum_pair(down_mine))

    back_two, grad_gain_two = norm_back(middle, scale_two, gain_two, grad_normed_two)
    grad_middle = cotangent.astype(jnp.float32) + back_two
    grad_att = low(grad_middle)
    grad_out_all = product_left(attended_low, grad_att).T
    grad_attended = product(grad_att, w_out_all)
    grad_query_pre, buffer = attend_back(
        bounds, query_rows, grad_attended, attended, totals,
        cosine_head, sine_head, place, key_value,
    )
    key_value_grads = scatter_z(scatter_start(buffer, rows))
    square_grads = low(
        jnp.concatenate([product_left(grad_query_pre, normed_one).T, grad_out_all], axis=1)
    )
    square_grads = scatter_start(square_grads, features)
    down_parts = undeal(after(down_sums, buffer))
    gate_parts = undeal(after(gate_sums, buffer))
    grad_query_part = product_right(grad_query_pre, w_query_all)
    key_value_grads = after(
        key_value_grads, square_grads, down_parts, gate_parts, grad_query_part
    ).astype(jnp.float32)
    square_grads = scatter_z(square_grads)
    grad_key_pre = low(
        rotate_halves(key_value_grads[:, :head].reshape(rows, 1, head), cosine_table, -sine_table)
    ).reshape(rows, head)
    grad_value_pre = low(key_value_grads[:, head:])
    grad_pair = jnp.concatenate([grad_key_pre, grad_value_pre], axis=1)
    grad_project = jnp.concatenate([grad_query_pre, grad_pair], axis=1)
    grad_bias = jnp.sum(grad_project.astype(jnp.float32), axis=0)
    up_parts = undeal(after(up_sums, grad_pair))
    grad_normed_one = sum_pair(
        low(grad_query_part + product_right(grad_pair, w_pair[:, : 2 * head])), up_parts
    )
    back_one, grad_gain_one = norm_back(inputs, scale_one, gain_one, grad_normed_one)
    grad_tokens = low(grad_middle + back_one)

    small_grads = jnp.concatenate(
        [
            grad_gain_one.reshape(devices, -1),
            grad_gain_two.reshape(devices, -1),
            grad_bias[:heads_width]
            .reshape(query_group, devices, piece)
            .transpose(1, 0, 2)
            .reshape(devices, -1),
            grad_bias[heads_width : heads_width + head].reshape(devices, -1),
            grad_bias[heads_width + head :].reshape(devices, -1),
        ],
        axis=1,
    )
    small_grads = jnp.pad(small_grads, ((0, 0), (0, features * head - small_grads.shape[1])))
    packed_grads = low(
        jnp.concatenate(
            [product_left(grad_pair, normed_one).T, small_grads.reshape(devices * features, head)],
            axis=1,
        )
    )
    packed_grads = scatter_z(scatter_start(packed_grads, features)).astype(jnp.float32)
    small_own = packed_grads[:, 2 * head :].reshape(-1)
    square_grads = square_grads.astype(jnp.float32)
    grad_w_out = square_grads[:, heads_width:].T
    grad_w_down = undeal_end(down_parts).T
    grad_w_gate = undeal_end(gate_parts)
    grad_w_up = undeal_end(up_parts)
    return (
        result,
        grad_tokens,
        small_own[cuts[0] : cuts[1]],
        square_grads[:, :heads_width],
        small_own[cuts[2] : cuts[3]].reshape(query_group, piece),
        packed_grads[:, :head],
        small_own[cuts[3] : cuts[4]].reshape(1, piece),
        packed_grads[:, head : 2 * head],
        small_own[cuts[4] : cuts[5]].reshape(1, piece),
        grad_w_out,
        small_own[cuts[1] : cuts[2]],
        grad_w_gate,
        grad_w_up,
        grad_w_down,
    )


def solution(mesh):
    wide, narrow = mesh.devices.shape
    grouped = Mesh(mesh.devices.reshape(wide // 4, 2, 2, narrow), WIDE + ("y",))
    rows = P(WIDE, None)
    vector = P(WIDE)
    columns = P(WIDE, "y")
    lines = P("y", WIDE)
    return jax.shard_map(
        local,
        mesh=grouped,
        in_specs=(rows, P(), vector, columns, lines, columns, lines, columns, lines, lines,
                  vector, columns, columns, lines, rows),
        out_specs=(rows, rows, vector, columns, lines, columns, lines, columns, lines, lines,
                   vector, columns, columns, lines),
        check_vma=False,
    )
```

```python
import math

import jax
import jax.numpy as jnp
from jax import lax
from jax.experimental import pallas as pl
from jax.experimental.layout import Layout, with_layout_constraint
from jax.experimental.pallas import tpu as pltpu
from jax.sharding import Mesh
from jax.sharding import PartitionSpec as P

ROPE_BASE = 10000.0
EPSILON = 1e-06


def product(left, right):
    return jnp.dot(left, right, preferred_element_type=jnp.float32)


def product_left(left, right):
    return lax.dot_general(
        left, right, (((0,), (0,)), ((), ())), preferred_element_type=jnp.float32
    )


def product_right(left, right):
    return lax.dot_general(
        left, right, (((1,), (1,)), ((), ())), preferred_element_type=jnp.float32
    )


def rotate_halves(value_rows, cosine_table, sine_table):
    middle_at = value_rows.shape[-1] // 2
    first = value_rows[..., :middle_at]
    second = value_rows[..., middle_at:]
    return jnp.concatenate(
        [first * cosine_table - second * sine_table, second * cosine_table + first * sine_table],
        axis=-1,
    )


def norm_scale(value_rows):
    return lax.rsqrt(jnp.mean(value_rows * value_rows, axis=-1, keepdims=True) + EPSILON)


def norm_back(value_rows, scale, gain, grad):
    normed = value_rows * scale
    inner = grad * gain
    back = scale * (inner - normed * jnp.mean(inner * normed, axis=-1, keepdims=True))
    return (back, jnp.sum(grad * normed, axis=0))


WIDE = ("z", "x", "c")
GROUP = ("x", "c")


def other(value, axis):
    return lax.ppermute(value, axis, [(0, 1), (1, 0)])


def low(value):
    return value.astype(jnp.bfloat16)


def after(value, *earlier):
    return lax.optimization_barrier((value, *earlier))[0]


def row_major(value):
    return with_layout_constraint(value, Layout(major_to_minor=(0, 1)))


def gather_group(own):
    core = other(own, "c")
    across = other(own, "x")
    far = other(across, "c")
    return jnp.concatenate([own, core, across, far], axis=0)


def sum_core(partial, rows):
    sent = low(jnp.concatenate([partial[rows : 2 * rows], partial[3 * rows :]], axis=0))
    core = other(sent, "c").astype(jnp.float32)
    return partial[:rows] + core[:rows], low(partial[2 * rows : 3 * rows] + core[rows:])


def sum_narrow(partial):
    mine = low(partial)
    return mine.astype(jnp.float32) + other(mine, "y").astype(jnp.float32)


def deal(weight):
    features, hidden = weight.shape
    parts = weight.reshape(features, 4, hidden // 4).transpose(1, 0, 2)
    parts = lax.all_to_all(parts, GROUP, split_axis=0, concat_axis=0, tiled=True)
    return parts.reshape(4 * features, hidden // 4)


def gather_z(own):
    return lax.all_gather(own, "z", axis=0, tiled=True)


def scatter_z(whole):
    return lax.psum_scatter(whole, "z", scatter_dimension=0, tiled=True)


def undeal(grad):
    features = grad.shape[0] // 4
    parts = grad.reshape(4, features, grad.shape[1])
    return lax.all_to_all(parts, GROUP, split_axis=0, concat_axis=0, tiled=True)


def undeal_end(parts):
    count, features, hidden = parts.shape
    return parts.transpose(1, 0, 2).reshape(features, count * hidden).astype(jnp.float32)


def gather_rest(column, rows):
    own = column.reshape(-1, 1, 1, rows, column.shape[1])
    near = other(own, "x")
    at_x = lax.axis_index("x")
    at_c = lax.axis_index("c")
    whole = jnp.zeros((own.shape[0], 2, 2, *own.shape[3:]), column.dtype)
    for piece, x_place, c_place in (
        (own, at_x, at_c),
        (other(own, "c"), at_x, 1 - at_c),
        (near, 1 - at_x, at_c),
        (other(near, "c"), 1 - at_x, 1 - at_c),
    ):
        whole = lax.dynamic_update_slice(whole, piece, (0, x_place, c_place, 0, 0))
    return whole.reshape(-1, column.shape[1])


def halve(whole, axis, position):
    at = lax.axis_index(axis)
    sent = lax.dynamic_slice_in_dim(whole, 1 - at, 1, position)
    kept = lax.dynamic_slice_in_dim(whole, at, 1, position)
    return low(kept.astype(jnp.float32) + other(sent, axis).astype(jnp.float32))


def scatter_start(whole, rows):
    parts = whole.reshape(-1, 2, 2, rows, whole.shape[1])
    return halve(halve(parts, "c", 2), "x", 1).reshape(-1, whole.shape[1])


def rotate_rows(value_rows, cosine, sine):
    return value_rows * cosine + pltpu.roll(value_rows, value_rows.shape[1] // 2, 1) * sine


def mask_bias(place_ref, begin, span):
    rows = place_ref.shape[1]
    key_index = begin + lax.broadcasted_iota(jnp.int32, (span, rows), 0)
    allowed = (key_index >= place_ref[0:1, :]) & (key_index <= place_ref[1:2, :])
    return jnp.where(allowed, 0.0, -1e30)


def turned(value):
    return value.astype(jnp.float32).T.astype(value.dtype)


def attend_kernel(
    bounds_ref, query_ref, cosine_ref, sine_ref, place_ref, pair_ref,
    rotated_ref, attended_ref, totals_ref, sums_ref,
):
    rows, wide = query_ref.shape
    head = cosine_ref.shape[1]
    factor = math.log2(math.e) / math.sqrt(head)
    cosine = cosine_ref[...]
    sine = sine_ref[...]
    for at in range(0, wide, head):
        rotated_ref[:, at : at + head] = low(
            rotate_rows(query_ref[:, at : at + head], cosine, sine)
        )
    sums_ref[...] = jnp.zeros_like(sums_ref)
    totals_ref[...] = jnp.zeros_like(totals_ref)

    def step(number, carry):
        begin = pl.multiple_of(number * rows, rows)
        keys = pair_ref[pl.ds(begin, rows), :head]
        values_turned = turned(pair_ref[pl.ds(begin, rows), head:])
        bias = mask_bias(place_ref, begin, rows)
        for order in range(wide // head):
            at = order * head
            scores = product_right(keys, rotated_ref[:, at : at + head])
            weights = jnp.exp2(scores * factor + bias)
            totals_ref[order : order + 1, :] += jnp.sum(weights, axis=0, keepdims=True)
            sums_ref[at : at + head, :] += product(values_turned, low(weights))
        return carry

    lax.fori_loop(bounds_ref[0], bounds_ref[1] + 1, step, 0)
    for order in range(wide // head):
        at = order * head
        attended_ref[:, at : at + head] = (
            sums_ref[at : at + head, :] / totals_ref[order : order + 1, :]
        ).T


def attend_back_kernel(
    bounds_ref, rotated_ref, grad_ref, attended_ref, totals_ref, cosine_ref, sine_ref, place_ref,
    pair_ref, grad_query_ref, grad_pair_ref, sums_ref, accum_ref, delta_ref,
):
    rows, wide = rotated_ref.shape
    head = cosine_ref.shape[1]
    scale = 1.0 / math.sqrt(head)
    factor = math.log2(math.e) * scale
    for order in range(wide // head):
        at = order * head
        totals = jnp.broadcast_to(totals_ref[order : order + 1, :], (head, rows)).T
        divided = grad_ref[:, at : at + head] / totals
        accum_ref[:, at : at + head] = low(divided)
        delta_ref[order : order + 1, :] = jnp.sum(
            (divided * attended_ref[:, at : at + head]).T, axis=0, keepdims=True
        )

    def clear(number, carry):
        begin = pl.multiple_of(number * rows, rows)
        grad_pair_ref[pl.ds(begin, rows), :] = jnp.zeros((rows, 2 * head), jnp.bfloat16)
        return carry

    lax.fori_loop(0, grad_pair_ref.shape[0] // rows, clear, 0)
    sums_ref[...] = jnp.zeros_like(sums_ref)

    def step(number, carry):
        begin = pl.multiple_of(number * rows, rows)
        keys = pair_ref[pl.ds(begin, rows), :head]
        values = pair_ref[pl.ds(begin, rows), head:]
        keys_turned = turned(keys)
        bias = mask_bias(place_ref, begin, rows)
        grad_keys = jnp.zeros((rows, head), jnp.float32)
        grad_values = jnp.zeros((rows, head), jnp.float32)
        for order in range(wide // head):
            at = order * head
            query = rotated_ref[:, at : at + head]
            accum = accum_ref[:, at : at + head]
            weights = jnp.exp2(product_right(keys, query) * factor + bias)
            grad_scores = low(
                weights * (product_right(values, accum) - delta_ref[order : order + 1, :])
            )
            grad_values += product(low(weights), accum)
            grad_keys += product(grad_scores, query)
            sums_ref[at : at + head, :] += product(keys_turned, grad_scores)
        grad_pair_ref[pl.ds(begin, rows), :head] = low(grad_keys * scale)
        grad_pair_ref[pl.ds(begin, rows), head:] = low(grad_values)
        return carry

    lax.fori_loop(bounds_ref[0], bounds_ref[1] + 1, step, 0)
    cosine = cosine_ref[...]
    sine = -sine_ref[...]
    for order in range(wide // head):
        at = order * head
        grad_query_ref[:, at : at + head] = low(
            rotate_rows(sums_ref[at : at + head, :].T * scale, cosine, sine)
        )


def in_vmem(count):
    return [pl.BlockSpec(memory_space=pltpu.SMEM)] + [
        pl.BlockSpec(memory_space=pltpu.VMEM) for _ in range(count)
    ]


def attend(bounds, query_pre, cosine, sine, place, pair):
    rows, wide = query_pre.shape
    return pl.pallas_call(
        attend_kernel,
        out_shape=(
            jax.ShapeDtypeStruct((rows, wide), jnp.bfloat16),
            jax.ShapeDtypeStruct((rows, wide), jnp.float32),
            jax.ShapeDtypeStruct((8 * -(-wide // cosine.shape[1] // 8), rows), jnp.float32),
        ),
        in_specs=in_vmem(5),
        out_specs=tuple(in_vmem(3)[1:]),
        scratch_shapes=[pltpu.VMEM((wide, rows), jnp.float32)],
        cost_estimate=pl.CostEstimate(
            flops=4 * 9 * rows * rows * wide, transcendentals=9 * rows * rows * 6, bytes_accessed=20 << 20
        ),
        name="attend",
    )(bounds, query_pre, cosine, sine, place, pair)


def attend_back(bounds, rotated, grad, attended, totals, cosine, sine, place, pair):
    rows, wide = rotated.shape
    return pl.pallas_call(
        attend_back_kernel,
        out_shape=(
            jax.ShapeDtypeStruct((rows, wide), jnp.bfloat16),
            jax.ShapeDtypeStruct(pair.shape, jnp.bfloat16),
        ),
        in_specs=in_vmem(8),
        out_specs=tuple(in_vmem(2)[1:]),
        scratch_shapes=[
            pltpu.VMEM((wide, rows), jnp.float32),
            pltpu.VMEM((rows, wide), jnp.bfloat16),
            pltpu.VMEM(totals.shape, jnp.float32),
        ],
        cost_estimate=pl.CostEstimate(
            flops=10 * 9 * rows * rows * wide, transcendentals=9 * rows * rows * 6, bytes_accessed=30 << 20
        ),
        name="attend_back",
    )(bounds, rotated, grad, attended, totals, cosine, sine, place, pair)


def local(
    tokens,
    lengths,
    norm1_gain,
    w_query,
    b_query,
    key_projection,
    key_bias_vector,
    value_projection,
    value_bias_vector,
    w_out,
    norm2_gain,
    w_gate,
    w_up,
    w_down,
    cotangent,
):
    rows, width = tokens.shape
    devices = lax.axis_size(WIDE)
    own_index = lax.axis_index(WIDE)
    first = own_index * rows
    index = first + jnp.arange(rows, dtype=jnp.int32)
    ends = jnp.cumsum(lengths, dtype=jnp.int32)
    starts = ends - lengths
    seq_start = jnp.max(jnp.where(starts[None, :] <= index[:, None], starts[None, :], 0), axis=1)
    lowest = jnp.min(seq_start)
    highest = first + rows - 1
    head = key_projection.shape[1]
    freq = 1.0 / ROPE_BASE ** (jnp.arange(head // 2, dtype=jnp.float32) * 2.0 / head)
    angle = (index - seq_start).astype(jnp.float32)[:, None] * freq[None, :]
    cosine_table = jnp.cos(angle)[:, None, :]
    sine_table = jnp.sin(angle)[:, None, :]
    cosine_head = jnp.concatenate([cosine_table[:, 0], cosine_table[:, 0]], axis=1)
    sine_head = jnp.concatenate([-sine_table[:, 0], sine_table[:, 0]], axis=1)
    place = jnp.concatenate([seq_start[None], index[None], jnp.zeros((6, rows), jnp.int32)], axis=0)
    bounds = jnp.stack([lowest // rows, highest // rows])
    features = w_query.shape[0]
    heads_width = w_query.shape[1]
    query_group = heads_width // head
    projected = heads_width + 2 * head

    piece = b_query.shape[1]
    small_parts = [norm1_gain, norm2_gain, b_query.reshape(-1), key_bias_vector.reshape(-1),
                   value_bias_vector.reshape(-1)]
    small_sizes = [part.shape[0] for part in small_parts]
    small_rows = -(-sum(small_sizes) // head)
    small = jnp.concatenate(small_parts)
    small = jnp.pad(small, (0, features * head - small.shape[0])).reshape(features, head)
    square_pack = jnp.concatenate([w_query, w_out.T], axis=1)
    square_column = gather_z(square_pack)
    pair_pack = jnp.concatenate([key_projection, value_projection, small], axis=1)
    pair_column = gather_z(after(pair_pack, square_pack))
    gate_own = deal(after(w_gate, pair_column))
    w_pair = gather_rest(pair_column, features)
    small_all = w_pair[:, 2 * head :].reshape(devices, features, head)[:, :small_rows]
    small_all = small_all.reshape(devices, small_rows * head).astype(jnp.float32)
    cuts = [0]
    for size in small_sizes:
        cuts.append(cuts[-1] + size)
    gain_one = small_all[:, cuts[0] : cuts[1]].reshape(-1)
    gain_two = small_all[:, cuts[1] : cuts[2]].reshape(-1)
    bias_query = small_all[:, cuts[2] : cuts[3]].reshape(devices, query_group, piece)
    bias_query = bias_query.transpose(1, 0, 2).reshape(-1)
    bias_key = small_all[:, cuts[3] : cuts[4]].reshape(-1)
    bias_value = small_all[:, cuts[4] : cuts[5]].reshape(-1)


    inputs = tokens.astype(jnp.float32)
    scale_one = norm_scale(inputs)
    normed_one = low(inputs * scale_one * gain_one)
    projections = product(normed_one, w_pair[:, : 2 * head])
    key_pre = projections[:, :head] + bias_key
    key_rows = low(
        rotate_halves(key_pre.reshape(rows, 1, head), cosine_table, sine_table).reshape(rows, head)
    )
    value_rows = low(projections[:, head:] + bias_value)
    key_value = jnp.concatenate([key_rows, value_rows], axis=1)
    gate_all = gather_z(gate_own)
    key_value_column = gather_z(after(key_value, gate_own, square_column))
    up_own = deal(after(w_up, key_value))
    w_square = gather_rest(square_column, features)
    w_query_all = w_square[:, :heads_width]
    w_out_all = w_square[:, heads_width:]
    query_pre = product(normed_one, w_query_all) + bias_query
    key_value_column = after(key_value_column, up_own)
    up_all = gather_z(up_own)
    key_value = gather_rest(key_value_column, rows)
    down_own = deal(after(w_down, key_value_column).T)
    down_all = gather_z(down_own)
    cotangent_group = gather_group(after(cotangent, key_value))
    cotangent_turned = lax.optimization_barrier(cotangent_group.T)
    query_rows, attended, totals = attend(
        bounds, query_pre, cosine_head, sine_head, place, key_value
    )
    attended_low = low(attended)
    middle = inputs + sum_narrow(product_right(attended_low, w_out_all))
    scale_two = norm_scale(middle)
    normed_two = low(middle * scale_two * gain_two)
    normed_group = gather_group(normed_two)
    normed_turned = lax.optimization_barrier(normed_group.T)
    gate = product(normed_group, gate_all)
    up_part = product(normed_group, up_all)
    sigmoid_gate = jax.nn.sigmoid(gate)
    silu_gate = gate * sigmoid_gate
    hidden = low(silu_gate * up_part)
    grad_down = row_major(low(product(cotangent_turned, hidden)))
    down_sums = scatter_z(grad_down)
    grad_hidden = product(after(cotangent_group, grad_down), down_all)
    grad_gate = low(grad_hidden * up_part * sigmoid_gate * (1.0 + gate * (1.0 - sigmoid_gate)))
    grad_up = low(grad_hidden * silu_gate)
    grad_normed_part = product_right(grad_gate, gate_all) + product_right(grad_up, up_all)
    grad_normed_own, grad_normed_across = sum_core(grad_normed_part, rows)
    normed_came = other(grad_normed_across, "x")
    grad_gate_all = row_major(low(product(normed_turned, after(grad_gate, grad_normed_across))))
    gate_sums = scatter_z(grad_gate_all)
    grad_up_all = row_major(low(product(normed_turned, after(grad_up, grad_gate_all))))
    up_sums = scatter_z(grad_up_all)
    down_part = product_right(after(hidden, grad_up_all), down_all)
    normed_came = after(normed_came, down_part)
    grad_normed_mine = low(grad_normed_own + normed_came.astype(jnp.float32))
    normed_pair = other(grad_normed_mine, "y")
    down_parts = undeal(after(down_sums, grad_normed_mine))
    normed_pair = after(normed_pair, down_parts)
    grad_normed_two = grad_normed_mine.astype(jnp.float32) + normed_pair.astype(jnp.float32)
    down_own, down_across = sum_core(after(down_part, normed_pair), rows)
    down_came = other(down_across, "x")

    back_two, grad_gain_two = norm_back(middle, scale_two, gain_two, grad_normed_two)
    grad_middle = cotangent.astype(jnp.float32) + back_two
    grad_att = low(grad_middle)
    grad_out_all = product_left(attended_low, grad_att).T
    grad_attended = product(grad_att, w_out_all)
    grad_query_pre, buffer = attend_back(
        bounds, query_rows, grad_attended, attended, totals,
        cosine_head, sine_head, place, key_value,
    )
    key_value_sums = scatter_start(buffer, rows)
    key_value_grads = scatter_z(key_value_sums)
    down_mine = low(down_own + after(down_came, key_value_sums).astype(jnp.float32))
    down_pair = other(down_mine, "y")
    square_grads = low(
        jnp.concatenate(
            [product_left(grad_query_pre, normed_one).T, grad_out_all], axis=1
        )
    )
    square_grads = scatter_start(after(square_grads, key_value_sums), features)
    gate_parts = undeal(after(gate_sums, key_value_sums))
    grad_query_part = product_right(grad_query_pre, w_query_all)
    key_value_grads = after(key_value_grads, square_grads, grad_query_part).astype(jnp.float32)
    square_grads = scatter_z(square_grads)
    grad_key_pre = low(
        rotate_halves(key_value_grads[:, :head].reshape(rows, 1, head), cosine_table, -sine_table)
    ).reshape(rows, head)
    grad_value_pre = low(key_value_grads[:, head:])
    grad_pair = jnp.concatenate([grad_key_pre, grad_value_pre], axis=1)
    grad_project = jnp.concatenate([grad_query_pre, grad_pair], axis=1)
    grad_bias = jnp.sum(grad_project.astype(jnp.float32), axis=0)
    grad_normed_mine = low(grad_query_part + product_right(grad_pair, w_pair[:, : 2 * head]))
    normed_pair = after(other(grad_normed_mine, "y"), gate_parts, down_pair)
    result = low(
        middle + down_mine.astype(jnp.float32) + after(down_pair, grad_pair).astype(jnp.float32)
    )
    up_parts = undeal(after(up_sums, grad_normed_mine))
    grad_normed_one = grad_normed_mine.astype(jnp.float32) + normed_pair.astype(jnp.float32)
    back_one, grad_gain_one = norm_back(inputs, scale_one, gain_one, grad_normed_one)
    grad_tokens = low(grad_middle + back_one)

    small_grads = jnp.concatenate(
        [
            grad_gain_one.reshape(devices, -1),
            grad_gain_two.reshape(devices, -1),
            grad_bias[:heads_width]
            .reshape(query_group, devices, piece)
            .transpose(1, 0, 2)
            .reshape(devices, -1),
            grad_bias[heads_width : heads_width + head].reshape(devices, -1),
            grad_bias[heads_width + head :].reshape(devices, -1),
        ],
        axis=1,
    )
    small_grads = jnp.pad(small_grads, ((0, 0), (0, features * head - small_grads.shape[1])))
    packed_grads = low(
        jnp.concatenate(
            [product_left(grad_pair, normed_one).T, small_grads.reshape(devices * features, head)],
            axis=1,
        )
    )
    packed_grads = scatter_z(scatter_start(packed_grads, features)).astype(jnp.float32)
    small_own = packed_grads[:, 2 * head :].reshape(-1)
    square_grads = square_grads.astype(jnp.float32)
    grad_w_out = square_grads[:, heads_width:].T
    grad_w_down = undeal_end(down_parts).T
    grad_w_gate = undeal_end(gate_parts)
    grad_w_up = undeal_end(up_parts)
    return (
        result,
        grad_tokens,
        small_own[cuts[0] : cuts[1]],
        square_grads[:, :heads_width],
        small_own[cuts[2] : cuts[3]].reshape(query_group, piece),
        packed_grads[:, :head],
        small_own[cuts[3] : cuts[4]].reshape(1, piece),
        packed_grads[:, head : 2 * head],
        small_own[cuts[4] : cuts[5]].reshape(1, piece),
        grad_w_out,
        small_own[cuts[1] : cuts[2]],
        grad_w_gate,
        grad_w_up,
        grad_w_down,
    )


def solution(mesh):
    wide, narrow = mesh.devices.shape
    grouped = Mesh(mesh.devices.reshape(wide // 4, 2, 2, narrow), WIDE + ("y",))
    rows = P(WIDE, None)
    vector = P(WIDE)
    columns = P(WIDE, "y")
    lines = P("y", WIDE)
    return jax.shard_map(
        local,
        mesh=grouped,
        in_specs=(rows, P(), vector, columns, lines, columns, lines, columns, lines, lines,
                  vector, columns, columns, lines, rows),
        out_specs=(rows, rows, vector, columns, lines, columns, lines, columns, lines, lines,
                   vector, columns, columns, lines),
        check_vma=False,
    )
```

```python
import math

import jax
import jax.numpy as jnp
from jax import lax
from jax.experimental import pallas as pl
from jax.experimental.layout import Layout, with_layout_constraint
from jax.experimental.pallas import tpu as pltpu
from jax.sharding import Mesh
from jax.sharding import PartitionSpec as P

ROPE_BASE = 10000.0
EPSILON = 1e-06


def product(left, right):
    return jnp.dot(left, right, preferred_element_type=jnp.float32)


def product_left(left, right):
    return lax.dot_general(
        left, right, (((0,), (0,)), ((), ())), preferred_element_type=jnp.float32
    )


def product_right(left, right):
    return lax.dot_general(
        left, right, (((1,), (1,)), ((), ())), preferred_element_type=jnp.float32
    )


def rotate_halves(value_rows, cosine_table, sine_table):
    middle_at = value_rows.shape[-1] // 2
    first = value_rows[..., :middle_at]
    second = value_rows[..., middle_at:]
    return jnp.concatenate(
        [first * cosine_table - second * sine_table, second * cosine_table + first * sine_table],
        axis=-1,
    )


def norm_scale(value_rows):
    return lax.rsqrt(jnp.mean(value_rows * value_rows, axis=-1, keepdims=True) + EPSILON)


def norm_back(value_rows, scale, gain, grad):
    normed = value_rows * scale
    inner = grad * gain
    back = scale * (inner - normed * jnp.mean(inner * normed, axis=-1, keepdims=True))
    return (back, jnp.sum(grad * normed, axis=0))


WIDE = ("z", "x", "c")
GROUP = ("x", "c")


def other(value, axis):
    return lax.ppermute(value, axis, [(0, 1), (1, 0)])


def low(value):
    return value.astype(jnp.bfloat16)


def after(value, *earlier):
    return lax.optimization_barrier((value, *earlier))[0]


def row_major(value):
    return with_layout_constraint(value, Layout(major_to_minor=(0, 1)))


def gather_group(own):
    core = other(own, "c")
    across = other(own, "x")
    far = other(across, "c")
    return jnp.concatenate([own, core, across, far], axis=0)


def sum_core(partial, rows):
    sent = low(jnp.concatenate([partial[rows : 2 * rows], partial[3 * rows :]], axis=0))
    core = other(sent, "c").astype(jnp.float32)
    return partial[:rows] + core[:rows], low(partial[2 * rows : 3 * rows] + core[rows:])


def sum_narrow(partial):
    mine = low(partial)
    return mine.astype(jnp.float32) + other(mine, "y").astype(jnp.float32)


def deal(weight):
    features, hidden = weight.shape
    parts = weight.reshape(features, 4, hidden // 4).transpose(1, 0, 2)
    parts = lax.all_to_all(parts, GROUP, split_axis=0, concat_axis=0, tiled=True)
    return parts.reshape(4 * features, hidden // 4)


def gather_z(own):
    return lax.all_gather(own, "z", axis=0, tiled=True)


def scatter_z(whole):
    return lax.psum_scatter(whole, "z", scatter_dimension=0, tiled=True)


def undeal(grad):
    features = grad.shape[0] // 4
    parts = grad.reshape(4, features, grad.shape[1])
    return lax.all_to_all(parts, GROUP, split_axis=0, concat_axis=0, tiled=True)


def undeal_end(parts):
    count, features, hidden = parts.shape
    return parts.transpose(1, 0, 2).reshape(features, count * hidden).astype(jnp.float32)


def gather_rest(column, rows):
    own = column.reshape(-1, 1, 1, rows, column.shape[1])
    near = other(own, "x")
    at_x = lax.axis_index("x")
    at_c = lax.axis_index("c")
    whole = jnp.zeros((own.shape[0], 2, 2, *own.shape[3:]), column.dtype)
    for piece, x_place, c_place in (
        (own, at_x, at_c),
        (other(own, "c"), at_x, 1 - at_c),
        (near, 1 - at_x, at_c),
        (other(near, "c"), 1 - at_x, 1 - at_c),
    ):
        whole = lax.dynamic_update_slice(whole, piece, (0, x_place, c_place, 0, 0))
    return whole.reshape(-1, column.shape[1])


def halve(whole, axis, position):
    at = lax.axis_index(axis)
    sent = lax.dynamic_slice_in_dim(whole, 1 - at, 1, position)
    kept = lax.dynamic_slice_in_dim(whole, at, 1, position)
    return low(kept.astype(jnp.float32) + other(sent, axis).astype(jnp.float32))


def other_half(whole, axis, position):
    at = lax.axis_index(axis)
    sent = lax.dynamic_slice_in_dim(whole, 1 - at, 1, position)
    return lax.dynamic_slice_in_dim(whole, at, 1, position), other(sent, axis)


def halve_z(column, rows):
    high = lax.axis_size("z")
    at_z = lax.axis_index("z")
    step = 1
    while step < high:
        parts = column.reshape(-1, 2, rows, column.shape[1])
        at = (at_z // step) % 2
        sent = lax.dynamic_slice_in_dim(parts, 1 - at, 1, 1)
        kept = lax.dynamic_slice_in_dim(parts, at, 1, 1)
        came = lax.ppermute(sent, "z", [(number, number ^ step) for number in range(high)])
        column = kept.astype(jnp.float32) + came.astype(jnp.float32)
        column = column.reshape(-1, column.shape[3])
        step *= 2
        column = low(column) if step < high else column
    return column


def scatter_start(whole, rows):
    parts = whole.reshape(-1, 2, 2, rows, whole.shape[1])
    return halve(halve(parts, "c", 2), "x", 1).reshape(-1, whole.shape[1])


def rotate_rows(value_rows, cosine, sine):
    return value_rows * cosine + pltpu.roll(value_rows, value_rows.shape[1] // 2, 1) * sine


def mask_bias(place_ref, begin, span):
    rows = place_ref.shape[1]
    key_index = begin + lax.broadcasted_iota(jnp.int32, (span, rows), 0)
    allowed = (key_index >= place_ref[0:1, :]) & (key_index <= place_ref[1:2, :])
    return jnp.where(allowed, 0.0, -1e30)


def turned(value):
    return value.astype(jnp.float32).T.astype(value.dtype)


def attend_kernel(
    bounds_ref, query_ref, cosine_ref, sine_ref, place_ref, pair_ref,
    rotated_ref, attended_ref, totals_ref, sums_ref,
):
    rows, wide = query_ref.shape
    head = cosine_ref.shape[1]
    factor = math.log2(math.e) / math.sqrt(head)
    cosine = cosine_ref[...]
    sine = sine_ref[...]
    for at in range(0, wide, head):
        rotated_ref[:, at : at + head] = low(
            rotate_rows(query_ref[:, at : at + head], cosine, sine)
        )
    sums_ref[...] = jnp.zeros_like(sums_ref)
    totals_ref[...] = jnp.zeros_like(totals_ref)

    def step(number, carry):
        begin = pl.multiple_of(number * rows, rows)
        keys = pair_ref[pl.ds(begin, rows), :head]
        values_turned = turned(pair_ref[pl.ds(begin, rows), head:])
        bias = mask_bias(place_ref, begin, rows)
        for order in range(wide // head):
            at = order * head
            scores = product_right(keys, rotated_ref[:, at : at + head])
            weights = jnp.exp2(scores * factor + bias)
            totals_ref[order : order + 1, :] += jnp.sum(weights, axis=0, keepdims=True)
            sums_ref[at : at + head, :] += product(values_turned, low(weights))
        return carry

    lax.fori_loop(bounds_ref[0], bounds_ref[1] + 1, step, 0)
    for order in range(wide // head):
        at = order * head
        attended_ref[:, at : at + head] = (
            sums_ref[at : at + head, :] / totals_ref[order : order + 1, :]
        ).T


def attend_back_kernel(
    bounds_ref, rotated_ref, grad_ref, attended_ref, totals_ref, cosine_ref, sine_ref, place_ref,
    pair_ref, grad_query_ref, grad_pair_ref, sums_ref, accum_ref, delta_ref,
):
    rows, wide = rotated_ref.shape
    head = cosine_ref.shape[1]
    scale = 1.0 / math.sqrt(head)
    factor = math.log2(math.e) * scale
    for order in range(wide // head):
        at = order * head
        totals = jnp.broadcast_to(totals_ref[order : order + 1, :], (head, rows)).T
        divided = grad_ref[:, at : at + head] / totals
        accum_ref[:, at : at + head] = low(divided)
        delta_ref[order : order + 1, :] = jnp.sum(
            (divided * attended_ref[:, at : at + head]).T, axis=0, keepdims=True
        )

    def clear(number, carry):
        begin = pl.multiple_of(number * rows, rows)
        grad_pair_ref[pl.ds(begin, rows), :] = jnp.zeros((rows, 2 * head), jnp.bfloat16)
        return carry

    lax.fori_loop(0, grad_pair_ref.shape[0] // rows, clear, 0)
    sums_ref[...] = jnp.zeros_like(sums_ref)

    def step(number, carry):
        begin = pl.multiple_of(number * rows, rows)
        keys = pair_ref[pl.ds(begin, rows), :head]
        values = pair_ref[pl.ds(begin, rows), head:]
        keys_turned = turned(keys)
        bias = mask_bias(place_ref, begin, rows)
        grad_keys = jnp.zeros((rows, head), jnp.float32)
        grad_values = jnp.zeros((rows, head), jnp.float32)
        for order in range(wide // head):
            at = order * head
            query = rotated_ref[:, at : at + head]
            accum = accum_ref[:, at : at + head]
            weights = jnp.exp2(product_right(keys, query) * factor + bias)
            grad_scores = low(
                weights * (product_right(values, accum) - delta_ref[order : order + 1, :])
            )
            grad_values += product(low(weights), accum)
            grad_keys += product(grad_scores, query)
            sums_ref[at : at + head, :] += product(keys_turned, grad_scores)
        grad_pair_ref[pl.ds(begin, rows), :head] = low(grad_keys * scale)
        grad_pair_ref[pl.ds(begin, rows), head:] = low(grad_values)
        return carry

    lax.fori_loop(bounds_ref[0], bounds_ref[1] + 1, step, 0)
    cosine = cosine_ref[...]
    sine = -sine_ref[...]
    for order in range(wide // head):
        at = order * head
        grad_query_ref[:, at : at + head] = low(
            rotate_rows(sums_ref[at : at + head, :].T * scale, cosine, sine)
        )


def in_vmem(count):
    return [pl.BlockSpec(memory_space=pltpu.SMEM)] + [
        pl.BlockSpec(memory_space=pltpu.VMEM) for _ in range(count)
    ]


def attend(bounds, query_pre, cosine, sine, place, pair):
    rows, wide = query_pre.shape
    return pl.pallas_call(
        attend_kernel,
        out_shape=(
            jax.ShapeDtypeStruct((rows, wide), jnp.bfloat16),
            jax.ShapeDtypeStruct((rows, wide), jnp.float32),
            jax.ShapeDtypeStruct((8 * -(-wide // cosine.shape[1] // 8), rows), jnp.float32),
        ),
        in_specs=in_vmem(5),
        out_specs=tuple(in_vmem(3)[1:]),
        scratch_shapes=[pltpu.VMEM((wide, rows), jnp.float32)],
        cost_estimate=pl.CostEstimate(
            flops=4 * 9 * rows * rows * wide, transcendentals=9 * rows * rows * 6, bytes_accessed=20 << 20
        ),
        name="attend",
    )(bounds, query_pre, cosine, sine, place, pair)


def attend_back(bounds, rotated, grad, attended, totals, cosine, sine, place, pair):
    rows, wide = rotated.shape
    return pl.pallas_call(
        attend_back_kernel,
        out_shape=(
            jax.ShapeDtypeStruct((rows, wide), jnp.bfloat16),
            jax.ShapeDtypeStruct(pair.shape, jnp.bfloat16),
        ),
        in_specs=in_vmem(8),
        out_specs=tuple(in_vmem(2)[1:]),
        scratch_shapes=[
            pltpu.VMEM((wide, rows), jnp.float32),
            pltpu.VMEM((rows, wide), jnp.bfloat16),
            pltpu.VMEM(totals.shape, jnp.float32),
        ],
        cost_estimate=pl.CostEstimate(
            flops=rows * wide, transcendentals=0, bytes_accessed=rows * wide
        ),
        name="attend_back",
    )(bounds, rotated, grad, attended, totals, cosine, sine, place, pair)


def local(
    tokens,
    lengths,
    norm1_gain,
    w_query,
    b_query,
    key_projection,
    key_bias_vector,
    value_projection,
    value_bias_vector,
    w_out,
    norm2_gain,
    w_gate,
    w_up,
    w_down,
    cotangent,
):
    rows, width = tokens.shape
    devices = lax.axis_size(WIDE)
    own_index = lax.axis_index(WIDE)
    first = own_index * rows
    index = first + jnp.arange(rows, dtype=jnp.int32)
    ends = jnp.cumsum(lengths, dtype=jnp.int32)
    starts = ends - lengths
    seq_start = jnp.max(jnp.where(starts[None, :] <= index[:, None], starts[None, :], 0), axis=1)
    lowest = jnp.min(seq_start)
    highest = first + rows - 1
    head = key_projection.shape[1]
    freq = 1.0 / ROPE_BASE ** (jnp.arange(head // 2, dtype=jnp.float32) * 2.0 / head)
    angle = (index - seq_start).astype(jnp.float32)[:, None] * freq[None, :]
    cosine_table = jnp.cos(angle)[:, None, :]
    sine_table = jnp.sin(angle)[:, None, :]
    cosine_head = jnp.concatenate([cosine_table[:, 0], cosine_table[:, 0]], axis=1)
    sine_head = jnp.concatenate([-sine_table[:, 0], sine_table[:, 0]], axis=1)
    place = jnp.concatenate([seq_start[None], index[None], jnp.zeros((6, rows), jnp.int32)], axis=0)
    bounds = jnp.stack([lowest // rows, highest // rows])
    features = w_query.shape[0]
    heads_width = w_query.shape[1]
    query_group = heads_width // head
    projected = heads_width + 2 * head

    piece = b_query.shape[1]
    small_parts = [norm1_gain, norm2_gain, b_query.reshape(-1), key_bias_vector.reshape(-1),
                   value_bias_vector.reshape(-1)]
    small_sizes = [part.shape[0] for part in small_parts]
    small_rows = -(-sum(small_sizes) // head)
    small = jnp.concatenate(small_parts)
    small = jnp.pad(small, (0, features * head - small.shape[0])).reshape(features, head)
    square_pack = jnp.concatenate([w_query, w_out.T], axis=1)
    square_column = gather_z(square_pack)
    pair_pack = jnp.concatenate([key_projection, value_projection, small], axis=1)
    pair_column = gather_z(after(pair_pack, square_pack))
    gate_own = deal(after(w_gate, pair_column))
    w_pair = gather_rest(pair_column, features)
    small_all = w_pair[:, 2 * head :].reshape(devices, features, head)[:, :small_rows]
    small_all = small_all.reshape(devices, small_rows * head).astype(jnp.float32)
    cuts = [0]
    for size in small_sizes:
        cuts.append(cuts[-1] + size)
    gain_one = small_all[:, cuts[0] : cuts[1]].reshape(-1)
    gain_two = small_all[:, cuts[1] : cuts[2]].reshape(-1)
    bias_query = small_all[:, cuts[2] : cuts[3]].reshape(devices, query_group, piece)
    bias_query = bias_query.transpose(1, 0, 2).reshape(-1)
    bias_key = small_all[:, cuts[3] : cuts[4]].reshape(-1)
    bias_value = small_all[:, cuts[4] : cuts[5]].reshape(-1)


    inputs = tokens.astype(jnp.float32)
    scale_one = norm_scale(inputs)
    normed_one = low(inputs * scale_one * gain_one)
    projections = product(normed_one, w_pair[:, : 2 * head])
    key_pre = projections[:, :head] + bias_key
    key_rows = low(
        rotate_halves(key_pre.reshape(rows, 1, head), cosine_table, sine_table).reshape(rows, head)
    )
    value_rows = low(projections[:, head:] + bias_value)
    key_value = jnp.concatenate([key_rows, value_rows], axis=1)
    gate_all = gather_z(gate_own)
    key_value_column = gather_z(after(key_value, gate_own, square_column))
    up_own = deal(after(w_up, key_value))
    w_square = gather_rest(square_column, features)
    w_query_all = w_square[:, :heads_width]
    w_out_all = w_square[:, heads_width:]
    query_pre = product(normed_one, w_query_all) + bias_query
    key_value_column = after(key_value_column, up_own)
    up_all = gather_z(up_own)
    down_own = deal(after(w_down, key_value_column).T)
    down_all = gather_z(down_own)
    key_value = after(gather_rest(key_value_column, rows), down_own)
    cotangent_group = gather_group(after(cotangent, key_value))
    cotangent_turned = lax.optimization_barrier(cotangent_group.T)
    query_rows, attended, totals = attend(
        bounds, query_pre, cosine_head, sine_head, place, key_value
    )
    attended_low = low(attended)
    middle = inputs + sum_narrow(product_right(attended_low, w_out_all))
    scale_two = norm_scale(middle)
    normed_two = low(middle * scale_two * gain_two)
    normed_group = gather_group(normed_two)
    normed_turned = lax.optimization_barrier(normed_group.T)
    gate = product(normed_group, gate_all)
    up_part = product(normed_group, up_all)
    sigmoid_gate = jax.nn.sigmoid(gate)
    silu_gate = gate * sigmoid_gate
    hidden = low(silu_gate * up_part)
    grad_down = row_major(low(product(cotangent_turned, hidden)))
    down_sums = scatter_z(grad_down)
    grad_hidden = product(after(cotangent_group, grad_down), down_all)
    grad_gate = low(grad_hidden * up_part * sigmoid_gate * (1.0 + gate * (1.0 - sigmoid_gate)))
    grad_up = low(grad_hidden * silu_gate)
    grad_normed_part = product_right(grad_gate, gate_all) + product_right(grad_up, up_all)
    grad_normed_own, grad_normed_across = sum_core(grad_normed_part, rows)
    normed_came = other(grad_normed_across, "x")
    grad_gate_all = row_major(low(product(normed_turned, after(grad_gate, grad_normed_across))))
    gate_sums = scatter_z(grad_gate_all)
    grad_up_all = row_major(low(product(normed_turned, after(grad_up, grad_gate_all))))
    up_sums = scatter_z(grad_up_all)
    down_part = product_right(after(hidden, grad_up_all, down_sums), down_all)
    normed_came = after(normed_came, down_part)
    grad_normed_mine = low(grad_normed_own + normed_came.astype(jnp.float32))
    normed_pair = other(grad_normed_mine, "y")
    down_parts = undeal(after(down_sums, grad_normed_mine))
    normed_pair = after(normed_pair, down_parts)
    grad_normed_two = grad_normed_mine.astype(jnp.float32) + normed_pair.astype(jnp.float32)
    down_own, down_across = sum_core(after(down_part, normed_pair), rows)
    down_came = other(down_across, "x")

    back_two, grad_gain_two = norm_back(middle, scale_two, gain_two, grad_normed_two)
    grad_middle = cotangent.astype(jnp.float32) + back_two
    grad_att = low(grad_middle)
    grad_out_all = product_left(attended_low, grad_att).T
    grad_attended = product(grad_att, w_out_all)
    grad_query_pre, buffer = attend_back(
        bounds, query_rows, grad_attended, attended, totals,
        cosine_head, sine_head, place, key_value,
    )
    key_value_half = halve(buffer.reshape(-1, 2, 2, rows, 2 * head), "c", 2)
    key_value_kept, key_value_came = other_half(key_value_half, "x", 1)
    key_value_came = after(key_value_came, gate_sums, down_came)
    key_value_sums = low(
        key_value_kept.astype(jnp.float32) + key_value_came.astype(jnp.float32)
    ).reshape(-1, 2 * head)
    key_value_grads = halve_z(key_value_sums, rows)
    square_grads = low(
        jnp.concatenate(
            [product_left(grad_query_pre, normed_one).T, grad_out_all], axis=1
        )
    )
    square_half = halve(
        after(square_grads, key_value_sums).reshape(-1, 2, 2, features, 2 * heads_width), "c", 2
    )
    square_sent = other_half(square_half, "x", 1)
    gate_parts = undeal(after(gate_sums, key_value_sums))
    grad_query_part = product_right(grad_query_pre, w_query_all)
    key_value_grads = after(key_value_grads, square_half, grad_query_part, up_sums, gate_parts)
    grad_key_pre = low(
        rotate_halves(key_value_grads[:, :head].reshape(rows, 1, head), cosine_table, -sine_table)
    ).reshape(rows, head)
    grad_value_pre = low(key_value_grads[:, head:])
    grad_pair = jnp.concatenate([grad_key_pre, grad_value_pre], axis=1)
    grad_project = jnp.concatenate([grad_query_pre, grad_pair], axis=1)
    grad_bias = jnp.sum(grad_project.astype(jnp.float32), axis=0)
    grad_normed_mine = low(grad_query_part + product_right(grad_pair, w_pair[:, : 2 * head]))
    normed_pair = other(grad_normed_mine, "y")
    square_sums = low(
        square_sent[0].astype(jnp.float32)
        + after(square_sent[1], grad_normed_mine).astype(jnp.float32)
    )
    square_grads = scatter_z(square_sums.reshape(-1, 2 * heads_width))
    normed_pair = after(normed_pair, square_sums)
    up_parts = undeal(after(up_sums, normed_pair))
    down_mine = low(down_own + after(down_came, normed_pair).astype(jnp.float32))
    result = low(
        middle + down_mine.astype(jnp.float32) + other(down_mine, "y").astype(jnp.float32)
    )
    grad_normed_one = grad_normed_mine.astype(jnp.float32) + normed_pair.astype(jnp.float32)
    back_one, grad_gain_one = norm_back(inputs, scale_one, gain_one, grad_normed_one)
    grad_tokens = low(grad_middle + back_one)

    small_grads = jnp.concatenate(
        [
            grad_gain_one.reshape(devices, -1),
            grad_gain_two.reshape(devices, -1),
            grad_bias[:heads_width]
            .reshape(query_group, devices, piece)
            .transpose(1, 0, 2)
            .reshape(devices, -1),
            grad_bias[heads_width : heads_width + head].reshape(devices, -1),
            grad_bias[heads_width + head :].reshape(devices, -1),
        ],
        axis=1,
    )
    small_grads = jnp.pad(small_grads, ((0, 0), (0, features * head - small_grads.shape[1])))
    packed_grads = low(
        jnp.concatenate(
            [product_left(grad_pair, normed_one).T, small_grads.reshape(devices * features, head)],
            axis=1,
        )
    )
    packed_grads = after(scatter_start(packed_grads, features), square_grads)
    packed_grads = scatter_z(packed_grads).astype(jnp.float32)
    small_own = packed_grads[:, 2 * head :].reshape(-1)
    square_grads = square_grads.astype(jnp.float32)
    grad_w_out = square_grads[:, heads_width:].T
    grad_w_down = undeal_end(down_parts).T
    grad_w_gate = undeal_end(gate_parts)
    grad_w_up = undeal_end(up_parts)
    return (
        result,
        grad_tokens,
        small_own[cuts[0] : cuts[1]],
        square_grads[:, :heads_width],
        small_own[cuts[2] : cuts[3]].reshape(query_group, piece),
        packed_grads[:, :head],
        small_own[cuts[3] : cuts[4]].reshape(1, piece),
        packed_grads[:, head : 2 * head],
        small_own[cuts[4] : cuts[5]].reshape(1, piece),
        grad_w_out,
        small_own[cuts[1] : cuts[2]],
        grad_w_gate,
        grad_w_up,
        grad_w_down,
    )


def solution(mesh):
    wide, narrow = mesh.devices.shape
    grouped = Mesh(mesh.devices.reshape(wide // 4, 2, 2, narrow), WIDE + ("y",))
    rows = P(WIDE, None)
    vector = P(WIDE)
    columns = P(WIDE, "y")
    lines = P("y", WIDE)
    return jax.shard_map(
        local,
        mesh=grouped,
        in_specs=(rows, P(), vector, columns, lines, columns, lines, columns, lines, lines,
                  vector, columns, columns, lines, rows),
        out_specs=(rows, rows, vector, columns, lines, columns, lines, columns, lines, lines,
                   vector, columns, columns, lines),
        check_vma=False,
    )
```

```python
import math

import jax
import jax.numpy as jnp
from jax import lax
from jax.experimental import pallas as pl
from jax.experimental.layout import Layout, with_layout_constraint
from jax.experimental.pallas import tpu as pltpu
from jax.sharding import Mesh
from jax.sharding import PartitionSpec as P

ROPE_BASE = 10000.0
EPSILON = 1e-06


def product(left, right):
    return jnp.dot(left, right, preferred_element_type=jnp.float32)


def product_left(left, right):
    return lax.dot_general(
        left, right, (((0,), (0,)), ((), ())), preferred_element_type=jnp.float32
    )


def product_right(left, right):
    return lax.dot_general(
        left, right, (((1,), (1,)), ((), ())), preferred_element_type=jnp.float32
    )


def rotate_halves(value_rows, cosine_table, sine_table):
    middle_at = value_rows.shape[-1] // 2
    first = value_rows[..., :middle_at]
    second = value_rows[..., middle_at:]
    return jnp.concatenate(
        [first * cosine_table - second * sine_table, second * cosine_table + first * sine_table],
        axis=-1,
    )


def norm_scale(value_rows):
    return lax.rsqrt(jnp.mean(value_rows * value_rows, axis=-1, keepdims=True) + EPSILON)


def norm_back(value_rows, scale, gain, grad):
    normed = value_rows * scale
    inner = grad * gain
    back = scale * (inner - normed * jnp.mean(inner * normed, axis=-1, keepdims=True))
    return (back, jnp.sum(grad * normed, axis=0))


WIDE = ("z", "x", "c")
GROUP = ("x", "c")


def other(value, axis):
    return lax.ppermute(value, axis, [(0, 1), (1, 0)])


def low(value):
    return value.astype(jnp.bfloat16)


def after(value, *earlier):
    return lax.optimization_barrier((value, *earlier))[0]


def row_major(value):
    return with_layout_constraint(value, Layout(major_to_minor=(0, 1)))


def in_order(own, came):
    first = lax.axis_index("y") == 0
    return jnp.concatenate([jnp.where(first, own, came), jnp.where(first, came, own)], axis=1)


def gather_group(own):
    core = other(own, "c")
    across = other(own, "x")
    far = other(across, "c")
    return jnp.concatenate([own, core, across, far], axis=0)


def sum_core(partial, rows):
    sent = low(jnp.concatenate([partial[rows : 2 * rows], partial[3 * rows :]], axis=0))
    core = other(sent, "c").astype(jnp.float32)
    return partial[:rows] + core[:rows], low(partial[2 * rows : 3 * rows] + core[rows:])


def sum_narrow(partial):
    mine = low(partial)
    return mine.astype(jnp.float32) + other(mine, "y").astype(jnp.float32)


def deal(weight):
    features, hidden = weight.shape
    parts = weight.reshape(features, 4, hidden // 4).transpose(1, 0, 2)
    parts = lax.all_to_all(parts, GROUP, split_axis=0, concat_axis=0, tiled=True)
    return parts.reshape(4 * features, hidden // 4)


def gather_z(own):
    return lax.all_gather(own, "z", axis=0, tiled=True)


def scatter_z(whole):
    return lax.psum_scatter(whole, "z", scatter_dimension=0, tiled=True)


def undeal(grad):
    features = grad.shape[0] // 4
    parts = grad.reshape(4, features, grad.shape[1])
    return lax.all_to_all(parts, GROUP, split_axis=0, concat_axis=0, tiled=True)


def undeal_end(parts):
    count, features, hidden = parts.shape
    return parts.transpose(1, 0, 2).reshape(features, count * hidden).astype(jnp.float32)


def gather_rest(column, rows):
    own = column.reshape(-1, 1, 1, rows, column.shape[1])
    near = other(own, "x")
    at_x = lax.axis_index("x")
    at_c = lax.axis_index("c")
    whole = jnp.zeros((own.shape[0], 2, 2, *own.shape[3:]), column.dtype)
    for piece, x_place, c_place in (
        (own, at_x, at_c),
        (other(own, "c"), at_x, 1 - at_c),
        (near, 1 - at_x, at_c),
        (other(near, "c"), 1 - at_x, 1 - at_c),
    ):
        whole = lax.dynamic_update_slice(whole, piece, (0, x_place, c_place, 0, 0))
    return whole.reshape(-1, column.shape[1])


def other_half(whole, axis, position):
    at = lax.axis_index(axis)
    sent = lax.dynamic_slice_in_dim(whole, 1 - at, 1, position)
    return lax.dynamic_slice_in_dim(whole, at, 1, position), other(sent, axis)


def halve_z(column, rows, early, late):
    high = lax.axis_size("z")
    at_z = lax.axis_index("z")
    step = 1
    while step < high:
        parts = column.reshape(-1, 2, rows, column.shape[1])
        at = (at_z // step) % 2
        sent = lax.dynamic_slice_in_dim(parts, 1 - at, 1, 1)
        kept = lax.dynamic_slice_in_dim(parts, at, 1, 1)
        came = lax.ppermute(sent, "z", [(number, number ^ step) for number in range(high)])
        came = after(came, early if step == 1 else late)
        column = kept.astype(jnp.float32) + came.astype(jnp.float32)
        column = column.reshape(-1, column.shape[3])
        step *= 2
        column = low(column) if step < high else column
    return column


def add_half(halves, *earlier):
    kept, came = halves
    return low(kept.astype(jnp.float32) + after(came, *earlier).astype(jnp.float32))


def scatter_core(whole, rows, *earlier):
    parts = whole.reshape(-1, 2, 2, rows, whole.shape[1])
    return other_half(add_half(other_half(parts, "c", 2), *earlier), "x", 1)


def scatter_across(halves, *earlier):
    summed = add_half(halves, *earlier)
    return summed.reshape(-1, summed.shape[4])


def rotate_rows(value_rows, cosine, sine):
    return value_rows * cosine + pltpu.roll(value_rows, value_rows.shape[1] // 2, 1) * sine


def mask_bias(place_ref, begin, span):
    rows = place_ref.shape[1]
    key_index = begin + lax.broadcasted_iota(jnp.int32, (span, rows), 0)
    allowed = (key_index >= place_ref[0:1, :]) & (key_index <= place_ref[1:2, :])
    return jnp.where(allowed, 0.0, -1e30)


def turned(value):
    return value.astype(jnp.float32).T.astype(value.dtype)


def attend_kernel(
    bounds_ref, query_ref, cosine_ref, sine_ref, place_ref, pair_ref,
    rotated_ref, attended_ref, totals_ref, sums_ref,
):
    rows, wide = query_ref.shape
    head = cosine_ref.shape[1]
    factor = math.log2(math.e) / math.sqrt(head)
    cosine = cosine_ref[...]
    sine = sine_ref[...]
    for at in range(0, wide, head):
        rotated_ref[:, at : at + head] = low(
            rotate_rows(query_ref[:, at : at + head], cosine, sine)
        )
    sums_ref[...] = jnp.zeros_like(sums_ref)
    totals_ref[...] = jnp.zeros_like(totals_ref)

    def step(number, carry):
        begin = pl.multiple_of(number * rows, rows)
        keys = pair_ref[pl.ds(begin, rows), :head]
        values_turned = turned(pair_ref[pl.ds(begin, rows), head:])
        bias = mask_bias(place_ref, begin, rows)
        for order in range(wide // head):
            at = order * head
            scores = product_right(keys, rotated_ref[:, at : at + head])
            weights = jnp.exp2(scores * factor + bias)
            totals_ref[order : order + 1, :] += jnp.sum(weights, axis=0, keepdims=True)
            sums_ref[at : at + head, :] += product(values_turned, low(weights))
        return carry

    lax.fori_loop(bounds_ref[0], bounds_ref[1] + 1, step, 0)
    for order in range(wide // head):
        at = order * head
        attended_ref[:, at : at + head] = (
            sums_ref[at : at + head, :] / totals_ref[order : order + 1, :]
        ).T


def attend_back_kernel(
    bounds_ref, rotated_ref, grad_ref, attended_ref, totals_ref, cosine_ref, sine_ref, place_ref,
    pair_ref, grad_query_ref, grad_pair_ref, sums_ref, accum_ref, delta_ref,
):
    rows, wide = rotated_ref.shape
    head = cosine_ref.shape[1]
    scale = 1.0 / math.sqrt(head)
    factor = math.log2(math.e) * scale
    for order in range(wide // head):
        at = order * head
        totals = jnp.broadcast_to(totals_ref[order : order + 1, :], (head, rows)).T
        divided = grad_ref[:, at : at + head] / totals
        accum_ref[:, at : at + head] = low(divided)
        delta_ref[order : order + 1, :] = jnp.sum(
            (divided * attended_ref[:, at : at + head]).T, axis=0, keepdims=True
        )

    def clear(number, carry):
        begin = pl.multiple_of(number * rows, rows)
        grad_pair_ref[pl.ds(begin, rows), :] = jnp.zeros((rows, 2 * head), jnp.bfloat16)
        return carry

    lax.fori_loop(0, grad_pair_ref.shape[0] // rows, clear, 0)
    sums_ref[...] = jnp.zeros_like(sums_ref)

    def step(number, carry):
        begin = pl.multiple_of(number * rows, rows)
        keys = pair_ref[pl.ds(begin, rows), :head]
        values = pair_ref[pl.ds(begin, rows), head:]
        keys_turned = turned(keys)
        bias = mask_bias(place_ref, begin, rows)
        grad_keys = jnp.zeros((rows, head), jnp.float32)
        grad_values = jnp.zeros((rows, head), jnp.float32)
        for order in range(wide // head):
            at = order * head
            query = rotated_ref[:, at : at + head]
            accum = accum_ref[:, at : at + head]
            weights = jnp.exp2(product_right(keys, query) * factor + bias)
            grad_scores = low(
                weights * (product_right(values, accum) - delta_ref[order : order + 1, :])
            )
            grad_values += product(low(weights), accum)
            grad_keys += product(grad_scores, query)
            sums_ref[at : at + head, :] += product(keys_turned, grad_scores)
        grad_pair_ref[pl.ds(begin, rows), :head] = low(grad_keys * scale)
        grad_pair_ref[pl.ds(begin, rows), head:] = low(grad_values)
        return carry

    lax.fori_loop(bounds_ref[0], bounds_ref[1] + 1, step, 0)
    cosine = cosine_ref[...]
    sine = -sine_ref[...]
    for order in range(wide // head):
        at = order * head
        grad_query_ref[:, at : at + head] = low(
            rotate_rows(sums_ref[at : at + head, :].T * scale, cosine, sine)
        )


def in_vmem(count):
    return [pl.BlockSpec(memory_space=pltpu.SMEM)] + [
        pl.BlockSpec(memory_space=pltpu.VMEM) for _ in range(count)
    ]


def attend(bounds, query_pre, cosine, sine, place, pair):
    rows, wide = query_pre.shape
    return pl.pallas_call(
        attend_kernel,
        out_shape=(
            jax.ShapeDtypeStruct((rows, wide), jnp.bfloat16),
            jax.ShapeDtypeStruct((rows, wide), jnp.float32),
            jax.ShapeDtypeStruct((8 * -(-wide // cosine.shape[1] // 8), rows), jnp.float32),
        ),
        in_specs=in_vmem(5),
        out_specs=tuple(in_vmem(3)[1:]),
        scratch_shapes=[pltpu.VMEM((wide, rows), jnp.float32)],
        cost_estimate=pl.CostEstimate(
            flops=4 * 9 * rows * rows * wide, transcendentals=9 * rows * rows * 6, bytes_accessed=20 << 20
        ),
        name="attend",
    )(bounds, query_pre, cosine, sine, place, pair)


def attend_back(bounds, rotated, grad, attended, totals, cosine, sine, place, pair):
    rows, wide = rotated.shape
    return pl.pallas_call(
        attend_back_kernel,
        out_shape=(
            jax.ShapeDtypeStruct((rows, wide), jnp.bfloat16),
            jax.ShapeDtypeStruct(pair.shape, jnp.bfloat16),
        ),
        in_specs=in_vmem(8),
        out_specs=tuple(in_vmem(2)[1:]),
        scratch_shapes=[
            pltpu.VMEM((wide, rows), jnp.float32),
            pltpu.VMEM((rows, wide), jnp.bfloat16),
            pltpu.VMEM(totals.shape, jnp.float32),
        ],
        cost_estimate=pl.CostEstimate(
            flops=10 * 9 * rows * rows * wide, transcendentals=9 * rows * rows * 6, bytes_accessed=30 << 20
        ),
        name="attend_back",
    )(bounds, rotated, grad, attended, totals, cosine, sine, place, pair)


def local(
    tokens,
    lengths,
    norm1_gain,
    w_query,
    b_query,
    key_projection,
    key_bias_vector,
    value_projection,
    value_bias_vector,
    w_out,
    norm2_gain,
    w_gate,
    w_up,
    w_down,
    cotangent,
):
    rows, width = tokens.shape
    devices = lax.axis_size(WIDE)
    own_index = lax.axis_index(WIDE)
    first = own_index * rows
    index = first + jnp.arange(rows, dtype=jnp.int32)
    ends = jnp.cumsum(lengths, dtype=jnp.int32)
    starts = ends - lengths
    seq_start = jnp.max(jnp.where(starts[None, :] <= index[:, None], starts[None, :], 0), axis=1)
    lowest = jnp.min(seq_start)
    highest = first + rows - 1
    head = key_projection.shape[1]
    freq = 1.0 / ROPE_BASE ** (jnp.arange(head // 2, dtype=jnp.float32) * 2.0 / head)
    angle = (index - seq_start).astype(jnp.float32)[:, None] * freq[None, :]
    cosine_table = jnp.cos(angle)[:, None, :]
    sine_table = jnp.sin(angle)[:, None, :]
    cosine_head = jnp.concatenate([cosine_table[:, 0], cosine_table[:, 0]], axis=1)
    sine_head = jnp.concatenate([-sine_table[:, 0], sine_table[:, 0]], axis=1)
    place = jnp.concatenate([seq_start[None], index[None], jnp.zeros((6, rows), jnp.int32)], axis=0)
    bounds = jnp.stack([lowest // rows, highest // rows])
    features = w_query.shape[0]
    heads_width = w_query.shape[1]
    query_group = heads_width // head
    projected = heads_width + 2 * head

    piece = b_query.shape[1]
    small_parts = [norm1_gain, norm2_gain, b_query.reshape(-1), key_bias_vector.reshape(-1),
                   value_bias_vector.reshape(-1)]
    small_sizes = [part.shape[0] for part in small_parts]
    small_rows = -(-sum(small_sizes) // head)
    small = jnp.concatenate(small_parts)
    small = jnp.pad(small, (0, features * head - small.shape[0])).reshape(features, head)
    square_pack = jnp.concatenate([w_query, w_out.T], axis=1)
    square_column = gather_z(square_pack)
    pair_pack = jnp.concatenate([key_projection, value_projection, small], axis=1)
    pair_column = gather_z(after(pair_pack, square_pack))
    gate_own = deal(after(w_gate, pair_column))
    w_pair = gather_rest(pair_column, features)
    pair_weights_came = other(w_pair[:, : 2 * head], "y")
    small_all = w_pair[:, 2 * head :].reshape(devices, features, head)[:, :small_rows]
    small_all = small_all.reshape(devices, small_rows * head).astype(jnp.float32)
    cuts = [0]
    for size in small_sizes:
        cuts.append(cuts[-1] + size)
    gain_one = small_all[:, cuts[0] : cuts[1]].reshape(-1)
    gain_two = small_all[:, cuts[1] : cuts[2]].reshape(-1)
    bias_query = small_all[:, cuts[2] : cuts[3]].reshape(devices, query_group, piece)
    bias_query = bias_query.transpose(1, 0, 2).reshape(-1)
    bias_key = small_all[:, cuts[3] : cuts[4]].reshape(-1)
    bias_value = small_all[:, cuts[4] : cuts[5]].reshape(-1)


    inputs = tokens.astype(jnp.float32)
    scale_one = norm_scale(inputs)
    normed_one = low(inputs * scale_one * gain_one)
    projections = product(normed_one, w_pair[:, : 2 * head])
    key_pre = projections[:, :head] + bias_key
    key_rows = low(
        rotate_halves(key_pre.reshape(rows, 1, head), cosine_table, sine_table).reshape(rows, head)
    )
    value_rows = low(projections[:, head:] + bias_value)
    key_value = jnp.concatenate([key_rows, value_rows], axis=1)
    gate_all = gather_z(gate_own)
    key_value_column = gather_z(after(key_value, gate_own, square_column))
    up_own = deal(after(w_up, key_value))
    w_square = gather_rest(square_column, features)
    w_query_all = w_square[:, :heads_width]
    w_out_all = w_square[:, heads_width:]
    query_pre = product(normed_one, w_query_all) + bias_query
    key_value_column = after(key_value_column, up_own)
    up_all = gather_z(up_own)
    down_own = deal(after(w_down, key_value_column).T)
    down_all = gather_z(down_own)
    key_value = after(gather_rest(key_value_column, rows), down_own)
    cotangent_group = gather_group(after(cotangent, key_value))
    cotangent_turned = lax.optimization_barrier(cotangent_group.T)
    query_rows, attended, totals = attend(
        bounds, query_pre, cosine_head, sine_head, place, key_value
    )
    attended_low = low(attended)
    attention = low(product_right(attended_low, w_out_all))
    attention_came = after(
        other(attention, "y"), cotangent_group, cotangent_turned, pair_weights_came
    )
    middle = inputs + (attention.astype(jnp.float32) + attention_came.astype(jnp.float32))
    scale_two = norm_scale(middle)
    normed_two = low(middle * scale_two * gain_two)
    normed_group = gather_group(normed_two)
    normed_turned = lax.optimization_barrier(normed_group.T)
    gate = product(normed_group, gate_all)
    up_part = product(normed_group, up_all)
    sigmoid_gate = jax.nn.sigmoid(gate)
    silu_gate = gate * sigmoid_gate
    hidden = low(silu_gate * up_part)
    grad_down = row_major(low(product(cotangent_turned, hidden)))
    down_sums = scatter_z(grad_down)
    grad_hidden = product(after(cotangent_group, grad_down), down_all)
    grad_gate = low(grad_hidden * up_part * sigmoid_gate * (1.0 + gate * (1.0 - sigmoid_gate)))
    grad_up = low(grad_hidden * silu_gate)
    grad_normed_part = product_right(grad_gate, gate_all) + product_right(grad_up, up_all)
    grad_normed_own, grad_normed_across = sum_core(grad_normed_part, rows)
    normed_came = other(grad_normed_across, "x")
    grad_gate_all = row_major(low(product(normed_turned, after(grad_gate, grad_normed_across))))
    gate_sums = scatter_z(grad_gate_all)
    grad_up_all = row_major(low(product(normed_turned, after(grad_up, grad_gate_all))))
    up_sums = scatter_z(grad_up_all)
    down_part = product_right(after(hidden, grad_up_all, down_sums), down_all)
    normed_came = after(normed_came, down_part)
    grad_normed_mine = low(grad_normed_own + normed_came.astype(jnp.float32))
    normed_pair = other(grad_normed_mine, "y")
    down_parts = undeal(after(down_sums, grad_normed_mine))
    normed_pair = after(normed_pair, down_parts)
    grad_normed_two = grad_normed_mine.astype(jnp.float32) + normed_pair.astype(jnp.float32)

    back_two, grad_gain_two = norm_back(middle, scale_two, gain_two, grad_normed_two)
    grad_middle = cotangent.astype(jnp.float32) + back_two
    grad_att = low(grad_middle)
    grad_out_all = product_left(attended_low, grad_att).T
    grad_attended = product(grad_att, w_out_all)
    grad_query_pre, buffer = attend_back(
        bounds, query_rows, grad_attended, attended, totals,
        cosine_head, sine_head, place, key_value,
    )
    grad_query_mine = low(product_right(grad_query_pre, w_query_all))
    query_came = other(grad_query_mine, "y")
    key_value_halves = scatter_core(buffer, rows)
    square_grads = row_major(
        low(jnp.concatenate([product_left(grad_query_pre, normed_one).T, grad_out_all], axis=1))
    )
    key_value_sums = scatter_across(key_value_halves, gate_sums, square_grads, grad_query_mine)
    gate_parts = undeal(after(gate_sums, key_value_sums))
    square_halves = scatter_core(after(square_grads, key_value_sums), features)
    key_value_grads = halve_z(key_value_sums, rows, key_value_sums, query_came)
    square_sums = scatter_across(square_halves, gate_parts)
    down_own, down_across = sum_core(after(down_part, key_value_sums), rows)
    key_value_grads = after(key_value_grads, gate_parts, up_sums, down_across)
    down_came = other(after(down_across, square_sums), "x")
    square_grads = scatter_z(square_sums)
    grad_key_pre = low(
        rotate_halves(key_value_grads[:, :head].reshape(rows, 1, head), cosine_table, -sine_table)
    ).reshape(rows, head)
    grad_value_pre = low(key_value_grads[:, head:])
    grad_pair = jnp.concatenate([grad_key_pre, grad_value_pre], axis=1)
    grad_project = jnp.concatenate([grad_query_pre, grad_pair], axis=1)
    grad_bias = jnp.sum(grad_project.astype(jnp.float32), axis=0)
    pair_both = in_order(grad_pair, other(grad_pair, "y"))
    query_came = after(query_came, grad_pair)
    grad_normed_one = (
        grad_query_mine.astype(jnp.float32) + query_came.astype(jnp.float32)
    ) + product_right(
        pair_both, in_order(w_pair[:, : 2 * head], pair_weights_came)
    )
    down_mine = low(down_own + after(down_came, pair_both).astype(jnp.float32))
    down_pair = other(down_mine, "y")
    result = low(middle + down_mine.astype(jnp.float32) + down_pair.astype(jnp.float32))
    back_one, grad_gain_one = norm_back(inputs, scale_one, gain_one, grad_normed_one)
    grad_tokens = low(grad_middle + back_one)

    small_grads = jnp.concatenate(
        [
            grad_gain_one.reshape(devices, -1),
            grad_gain_two.reshape(devices, -1),
            grad_bias[:heads_width]
            .reshape(query_group, devices, piece)
            .transpose(1, 0, 2)
            .reshape(devices, -1),
            grad_bias[heads_width : heads_width + head].reshape(devices, -1),
            grad_bias[heads_width + head :].reshape(devices, -1),
        ],
        axis=1,
    )
    small_grads = jnp.pad(small_grads, ((0, 0), (0, features * head - small_grads.shape[1])))
    packed_grads = low(
        jnp.concatenate(
            [product_left(grad_pair, normed_one).T, small_grads.reshape(devices * features, head)],
            axis=1,
        )
    )
    up_parts = undeal(after(up_sums, grad_pair))
    packed_grads = scatter_across(
        scatter_core(packed_grads, features, square_sums), up_parts, down_came
    )
    packed_grads = scatter_z(packed_grads).astype(jnp.float32)
    small_own = packed_grads[:, 2 * head :].reshape(-1)
    square_grads = square_grads.astype(jnp.float32)
    grad_w_out = square_grads[:, heads_width:].T
    grad_w_down = undeal_end(down_parts).T
    grad_w_gate = undeal_end(gate_parts)
    grad_w_up = undeal_end(up_parts)
    return (
        result,
        grad_tokens,
        small_own[cuts[0] : cuts[1]],
        square_grads[:, :heads_width],
        small_own[cuts[2] : cuts[3]].reshape(query_group, piece),
        packed_grads[:, :head],
        small_own[cuts[3] : cuts[4]].reshape(1, piece),
        packed_grads[:, head : 2 * head],
        small_own[cuts[4] : cuts[5]].reshape(1, piece),
        grad_w_out,
        small_own[cuts[1] : cuts[2]],
        grad_w_gate,
        grad_w_up,
        grad_w_down,
    )


def solution(mesh):
    wide, narrow = mesh.devices.shape
    grouped = Mesh(mesh.devices.reshape(wide // 4, 2, 2, narrow), WIDE + ("y",))
    rows = P(WIDE, None)
    vector = P(WIDE)
    columns = P(WIDE, "y")
    lines = P("y", WIDE)
    return jax.shard_map(
        local,
        mesh=grouped,
        in_specs=(rows, P(), vector, columns, lines, columns, lines, columns, lines, lines,
                  vector, columns, columns, lines, rows),
        out_specs=(rows, rows, vector, columns, lines, columns, lines, columns, lines, lines,
                   vector, columns, columns, lines),
        check_vma=False,
    )
```

```python
import math

import jax
import jax.numpy as jnp
from jax import lax
from jax.experimental import pallas as pl
from jax.experimental.layout import Layout, with_layout_constraint
from jax.experimental.pallas import tpu as pltpu
from jax.sharding import Mesh
from jax.sharding import PartitionSpec as P

ROPE_BASE = 10000.0
EPSILON = 1e-06


def product(left, right):
    return jnp.dot(left, right, preferred_element_type=jnp.float32)


def product_left(left, right):
    return lax.dot_general(
        left, right, (((0,), (0,)), ((), ())), preferred_element_type=jnp.float32
    )


def product_right(left, right):
    return lax.dot_general(
        left, right, (((1,), (1,)), ((), ())), preferred_element_type=jnp.float32
    )


def rotate_halves(value_rows, cosine_table, sine_table):
    middle_at = value_rows.shape[-1] // 2
    first = value_rows[..., :middle_at]
    second = value_rows[..., middle_at:]
    return jnp.concatenate(
        [first * cosine_table - second * sine_table, second * cosine_table + first * sine_table],
        axis=-1,
    )


def norm_scale(value_rows):
    return lax.rsqrt(jnp.mean(value_rows * value_rows, axis=-1, keepdims=True) + EPSILON)


def norm_back(value_rows, scale, gain, grad):
    normed = value_rows * scale
    inner = grad * gain
    back = scale * (inner - normed * jnp.mean(inner * normed, axis=-1, keepdims=True))
    return (back, jnp.sum(grad * normed, axis=0))


WIDE = ("z", "x", "c")
GROUP = ("x", "c")


def other(value, axis):
    return lax.ppermute(value, axis, [(0, 1), (1, 0)])


def low(value):
    return value.astype(jnp.bfloat16)


def after(value, *earlier):
    return lax.optimization_barrier((value, *earlier))[0]


def row_major(value):
    return with_layout_constraint(value, Layout(major_to_minor=(0, 1)))


def in_order(own, came):
    first = lax.axis_index("y") == 0
    return jnp.concatenate([jnp.where(first, own, came), jnp.where(first, came, own)], axis=1)


def gather_group(own):
    core = other(own, "c")
    across = other(own, "x")
    far = other(across, "c")
    return jnp.concatenate([own, core, across, far], axis=0)


def sum_core(partial, rows):
    sent = low(jnp.concatenate([partial[rows : 2 * rows], partial[3 * rows :]], axis=0))
    core = other(sent, "c").astype(jnp.float32)
    return partial[:rows] + core[:rows], low(partial[2 * rows : 3 * rows] + core[rows:])


def sum_narrow(partial):
    mine = low(partial)
    return mine.astype(jnp.float32) + other(mine, "y").astype(jnp.float32)


def deal(weight):
    features, hidden = weight.shape
    parts = weight.reshape(features, 4, hidden // 4).transpose(1, 0, 2)
    parts = lax.all_to_all(parts, GROUP, split_axis=0, concat_axis=0, tiled=True)
    return parts.reshape(4 * features, hidden // 4)


def gather_z(own):
    return lax.all_gather(own, "z", axis=0, tiled=True)


def scatter_z(whole):
    return lax.psum_scatter(whole, "z", scatter_dimension=0, tiled=True)


def undeal(grad):
    features = grad.shape[0] // 4
    parts = grad.reshape(4, features, grad.shape[1])
    return lax.all_to_all(parts, GROUP, split_axis=0, concat_axis=0, tiled=True)


def undeal_end(parts):
    count, features, hidden = parts.shape
    return parts.transpose(1, 0, 2).reshape(features, count * hidden).astype(jnp.float32)


def gather_rest(column, rows):
    own = column.reshape(-1, 1, 1, rows, column.shape[1])
    near = other(own, "x")
    at_x = lax.axis_index("x")
    at_c = lax.axis_index("c")
    whole = jnp.zeros((own.shape[0], 2, 2, *own.shape[3:]), column.dtype)
    for piece, x_place, c_place in (
        (own, at_x, at_c),
        (other(own, "c"), at_x, 1 - at_c),
        (near, 1 - at_x, at_c),
        (other(near, "c"), 1 - at_x, 1 - at_c),
    ):
        whole = lax.dynamic_update_slice(whole, piece, (0, x_place, c_place, 0, 0))
    return whole.reshape(-1, column.shape[1])


def other_half(whole, axis, position):
    at = lax.axis_index(axis)
    sent = lax.dynamic_slice_in_dim(whole, 1 - at, 1, position)
    return lax.dynamic_slice_in_dim(whole, at, 1, position), other(sent, axis)


def halve_z(column, rows, early, late):
    high = lax.axis_size("z")
    at_z = lax.axis_index("z")
    step = 1
    while step < high:
        parts = column.reshape(-1, 2, rows, column.shape[1])
        at = (at_z // step) % 2
        sent = lax.dynamic_slice_in_dim(parts, 1 - at, 1, 1)
        kept = lax.dynamic_slice_in_dim(parts, at, 1, 1)
        came = lax.ppermute(sent, "z", [(number, number ^ step) for number in range(high)])
        came = after(came, early if step == 1 else late)
        column = kept.astype(jnp.float32) + came.astype(jnp.float32)
        column = column.reshape(-1, column.shape[3])
        step *= 2
        column = low(column) if step < high else column
    return column


def add_half(halves, *earlier):
    kept, came = halves
    return low(kept.astype(jnp.float32) + after(came, *earlier).astype(jnp.float32))


def scatter_core(whole, rows, *earlier):
    parts = whole.reshape(-1, 2, 2, rows, whole.shape[1])
    return other_half(add_half(other_half(parts, "c", 2), *earlier), "x", 1)


def scatter_across(halves, *earlier):
    summed = add_half(halves, *earlier)
    return summed.reshape(-1, summed.shape[4])


def rotate_rows(value_rows, cosine, sine):
    return value_rows * cosine + pltpu.roll(value_rows, value_rows.shape[1] // 2, 1) * sine


def mask_bias(place_ref, begin, span):
    rows = place_ref.shape[1]
    key_index = begin + lax.broadcasted_iota(jnp.int32, (span, rows), 0)
    allowed = (key_index >= place_ref[0:1, :]) & (key_index <= place_ref[1:2, :])
    return jnp.where(allowed, 0.0, -1e30)


def turned(value):
    return value.astype(jnp.float32).T.astype(value.dtype)


def attend_kernel(
    bounds_ref, query_ref, cosine_ref, sine_ref, place_ref, pair_ref,
    rotated_ref, attended_ref, totals_ref, sums_ref,
):
    rows, wide = query_ref.shape
    head = cosine_ref.shape[1]
    factor = math.log2(math.e) / math.sqrt(head)
    cosine = cosine_ref[...]
    sine = sine_ref[...]
    for at in range(0, wide, head):
        rotated_ref[:, at : at + head] = low(
            rotate_rows(query_ref[:, at : at + head], cosine, sine)
        )
    sums_ref[...] = jnp.zeros_like(sums_ref)
    totals_ref[...] = jnp.zeros_like(totals_ref)

    def step(number, carry):
        begin = pl.multiple_of(number * rows, rows)
        keys = pair_ref[pl.ds(begin, rows), :head]
        values_turned = turned(pair_ref[pl.ds(begin, rows), head:])
        bias = mask_bias(place_ref, begin, rows)
        for order in range(wide // head):
            at = order * head
            scores = product_right(keys, rotated_ref[:, at : at + head])
            weights = jnp.exp2(scores * factor + bias)
            totals_ref[order : order + 1, :] += jnp.sum(weights, axis=0, keepdims=True)
            sums_ref[at : at + head, :] += product(values_turned, low(weights))
        return carry

    lax.fori_loop(bounds_ref[0], bounds_ref[1] + 1, step, 0)
    for order in range(wide // head):
        at = order * head
        attended_ref[:, at : at + head] = (
            sums_ref[at : at + head, :] / totals_ref[order : order + 1, :]
        ).T


def attend_back_kernel(
    bounds_ref, rotated_ref, grad_ref, attended_ref, totals_ref, cosine_ref, sine_ref, place_ref,
    pair_ref, grad_query_ref, grad_pair_ref, sums_ref, accum_ref, delta_ref,
):
    rows, wide = rotated_ref.shape
    head = cosine_ref.shape[1]
    scale = 1.0 / math.sqrt(head)
    factor = math.log2(math.e) * scale
    for order in range(wide // head):
        at = order * head
        totals = jnp.broadcast_to(totals_ref[order : order + 1, :], (head, rows)).T
        divided = grad_ref[:, at : at + head] / totals
        accum_ref[:, at : at + head] = low(divided)
        delta_ref[order : order + 1, :] = jnp.sum(
            (divided * attended_ref[:, at : at + head]).T, axis=0, keepdims=True
        )

    def clear(number, carry):
        begin = pl.multiple_of(number * rows, rows)
        grad_pair_ref[pl.ds(begin, rows), :] = jnp.zeros((rows, 2 * head), jnp.bfloat16)
        return carry

    lax.fori_loop(0, grad_pair_ref.shape[0] // rows, clear, 0)
    sums_ref[...] = jnp.zeros_like(sums_ref)

    def step(number, carry):
        begin = pl.multiple_of(number * rows, rows)
        keys = pair_ref[pl.ds(begin, rows), :head]
        values = pair_ref[pl.ds(begin, rows), head:]
        keys_turned = turned(keys)
        bias = mask_bias(place_ref, begin, rows)
        grad_keys = jnp.zeros((rows, head), jnp.float32)
        grad_values = jnp.zeros((rows, head), jnp.float32)
        for order in range(wide // head):
            at = order * head
            query = rotated_ref[:, at : at + head]
            accum = accum_ref[:, at : at + head]
            weights = jnp.exp2(product_right(keys, query) * factor + bias)
            grad_scores = low(
                weights * (product_right(values, accum) - delta_ref[order : order + 1, :])
            )
            grad_values += product(low(weights), accum)
            grad_keys += product(grad_scores, query)
            sums_ref[at : at + head, :] += product(keys_turned, grad_scores)
        grad_pair_ref[pl.ds(begin, rows), :head] = low(grad_keys * scale)
        grad_pair_ref[pl.ds(begin, rows), head:] = low(grad_values)
        return carry

    lax.fori_loop(bounds_ref[0], bounds_ref[1] + 1, step, 0)
    cosine = cosine_ref[...]
    sine = -sine_ref[...]
    for order in range(wide // head):
        at = order * head
        grad_query_ref[:, at : at + head] = low(
            rotate_rows(sums_ref[at : at + head, :].T * scale, cosine, sine)
        )


def in_vmem(count):
    return [pl.BlockSpec(memory_space=pltpu.SMEM)] + [
        pl.BlockSpec(memory_space=pltpu.VMEM) for _ in range(count)
    ]


def attend(bounds, query_pre, cosine, sine, place, pair):
    rows, wide = query_pre.shape
    return pl.pallas_call(
        attend_kernel,
        out_shape=(
            jax.ShapeDtypeStruct((rows, wide), jnp.bfloat16),
            jax.ShapeDtypeStruct((rows, wide), jnp.float32),
            jax.ShapeDtypeStruct((8 * -(-wide // cosine.shape[1] // 8), rows), jnp.float32),
        ),
        in_specs=in_vmem(5),
        out_specs=tuple(in_vmem(3)[1:]),
        scratch_shapes=[pltpu.VMEM((wide, rows), jnp.float32)],
        cost_estimate=pl.CostEstimate(
            flops=4 * 9 * rows * rows * wide, transcendentals=9 * rows * rows * 6, bytes_accessed=20 << 20
        ),
        name="attend",
    )(bounds, query_pre, cosine, sine, place, pair)


def attend_back(bounds, rotated, grad, attended, totals, cosine, sine, place, pair):
    rows, wide = rotated.shape
    return pl.pallas_call(
        attend_back_kernel,
        out_shape=(
            jax.ShapeDtypeStruct((rows, wide), jnp.bfloat16),
            jax.ShapeDtypeStruct(pair.shape, jnp.bfloat16),
        ),
        in_specs=in_vmem(8),
        out_specs=tuple(in_vmem(2)[1:]),
        scratch_shapes=[
            pltpu.VMEM((wide, rows), jnp.float32),
            pltpu.VMEM((rows, wide), jnp.bfloat16),
            pltpu.VMEM(totals.shape, jnp.float32),
        ],
        cost_estimate=pl.CostEstimate(
            flops=rows * wide, transcendentals=0, bytes_accessed=rows * wide
        ),
        name="attend_back",
    )(bounds, rotated, grad, attended, totals, cosine, sine, place, pair)


def local(
    tokens,
    lengths,
    norm1_gain,
    w_query,
    b_query,
    key_projection,
    key_bias_vector,
    value_projection,
    value_bias_vector,
    w_out,
    norm2_gain,
    w_gate,
    w_up,
    w_down,
    cotangent,
):
    rows, width = tokens.shape
    devices = lax.axis_size(WIDE)
    own_index = lax.axis_index(WIDE)
    first = own_index * rows
    index = first + jnp.arange(rows, dtype=jnp.int32)
    ends = jnp.cumsum(lengths, dtype=jnp.int32)
    starts = ends - lengths
    seq_start = jnp.max(jnp.where(starts[None, :] <= index[:, None], starts[None, :], 0), axis=1)
    lowest = jnp.min(seq_start)
    highest = first + rows - 1
    head = key_projection.shape[1]
    freq = 1.0 / ROPE_BASE ** (jnp.arange(head // 2, dtype=jnp.float32) * 2.0 / head)
    angle = (index - seq_start).astype(jnp.float32)[:, None] * freq[None, :]
    cosine_table = jnp.cos(angle)[:, None, :]
    sine_table = jnp.sin(angle)[:, None, :]
    cosine_head = jnp.concatenate([cosine_table[:, 0], cosine_table[:, 0]], axis=1)
    sine_head = jnp.concatenate([-sine_table[:, 0], sine_table[:, 0]], axis=1)
    place = jnp.concatenate([seq_start[None], index[None], jnp.zeros((6, rows), jnp.int32)], axis=0)
    bounds = jnp.stack([lowest // rows, highest // rows])
    features = w_query.shape[0]
    heads_width = w_query.shape[1]
    query_group = heads_width // head
    projected = heads_width + 2 * head

    piece = b_query.shape[1]
    small_parts = [norm1_gain, norm2_gain, b_query.reshape(-1), key_bias_vector.reshape(-1),
                   value_bias_vector.reshape(-1)]
    small_sizes = [part.shape[0] for part in small_parts]
    small_rows = -(-sum(small_sizes) // head)
    small = jnp.concatenate(small_parts)
    small = jnp.pad(small, (0, features * head - small.shape[0])).reshape(features, head)
    square_pack = jnp.concatenate([w_query, w_out.T], axis=1)
    square_column = gather_z(square_pack)
    pair_pack = jnp.concatenate([key_projection, value_projection, small], axis=1)
    pair_column = gather_z(after(pair_pack, square_pack))
    gate_own = deal(after(w_gate, pair_column))
    w_pair = gather_rest(pair_column, features)
    pair_weights_came = other(w_pair[:, : 2 * head], "y")
    small_all = w_pair[:, 2 * head :].reshape(devices, features, head)[:, :small_rows]
    small_all = small_all.reshape(devices, small_rows * head).astype(jnp.float32)
    cuts = [0]
    for size in small_sizes:
        cuts.append(cuts[-1] + size)
    gain_one = small_all[:, cuts[0] : cuts[1]].reshape(-1)
    gain_two = small_all[:, cuts[1] : cuts[2]].reshape(-1)
    bias_query = small_all[:, cuts[2] : cuts[3]].reshape(devices, query_group, piece)
    bias_query = bias_query.transpose(1, 0, 2).reshape(-1)
    bias_key = small_all[:, cuts[3] : cuts[4]].reshape(-1)
    bias_value = small_all[:, cuts[4] : cuts[5]].reshape(-1)


    inputs = tokens.astype(jnp.float32)
    scale_one = norm_scale(inputs)
    normed_one = low(inputs * scale_one * gain_one)
    projections = product(normed_one, w_pair[:, : 2 * head])
    key_pre = projections[:, :head] + bias_key
    key_rows = low(
        rotate_halves(key_pre.reshape(rows, 1, head), cosine_table, sine_table).reshape(rows, head)
    )
    value_rows = low(projections[:, head:] + bias_value)
    key_value = jnp.concatenate([key_rows, value_rows], axis=1)
    gate_all = gather_z(gate_own)
    key_value_column = gather_z(after(key_value, gate_own, square_column))
    up_own = deal(after(w_up, key_value))
    w_square = gather_rest(square_column, features)
    w_query_all = w_square[:, :heads_width]
    w_out_all = w_square[:, heads_width:]
    query_pre = product(normed_one, w_query_all) + bias_query
    key_value_column = after(key_value_column, up_own)
    up_all = gather_z(up_own)
    down_own = deal(after(w_down, key_value_column).T)
    down_all = gather_z(down_own)
    key_value = after(gather_rest(key_value_column, rows), down_own, pair_weights_came)
    cotangent_group = gather_group(after(cotangent, key_value))
    cotangent_turned = lax.optimization_barrier(cotangent_group.T)
    query_rows, attended, totals = attend(
        bounds, query_pre, cosine_head, sine_head, place, key_value
    )
    attended_low = low(attended)
    attention = low(product_right(attended_low, w_out_all))
    attention_came = after(
        other(attention, "y"), cotangent_group, cotangent_turned
    )
    middle = inputs + (attention.astype(jnp.float32) + attention_came.astype(jnp.float32))
    scale_two = norm_scale(middle)
    normed_two = low(middle * scale_two * gain_two)
    normed_group = gather_group(normed_two)
    normed_turned = lax.optimization_barrier(normed_group.T)
    gate = product(normed_group, gate_all)
    up_all = after(up_all, normed_turned)
    up_part = product(normed_group, up_all)
    sigmoid_gate = jax.nn.sigmoid(gate)
    silu_gate = gate * sigmoid_gate
    hidden = low(silu_gate * up_part)
    grad_down = row_major(low(product(cotangent_turned, hidden)))
    down_sums = scatter_z(grad_down)
    grad_hidden = product(after(cotangent_group, grad_down), down_all)
    grad_gate = low(grad_hidden * up_part * sigmoid_gate * (1.0 + gate * (1.0 - sigmoid_gate)))
    grad_up = low(grad_hidden * silu_gate)
    grad_normed_part = product_right(grad_gate, gate_all) + product_right(grad_up, up_all)
    grad_normed_own, grad_normed_across = sum_core(grad_normed_part, rows)
    normed_came = other(grad_normed_across, "x")
    grad_gate_all = row_major(low(product(normed_turned, after(grad_gate, grad_normed_across))))
    gate_sums = scatter_z(grad_gate_all)
    grad_up_all = row_major(low(product(normed_turned, after(grad_up, grad_gate_all))))
    up_sums = scatter_z(grad_up_all)
    down_part = product_right(after(hidden, grad_up_all, down_sums), down_all)
    normed_came = after(normed_came, down_part)
    grad_normed_mine = low(grad_normed_own + normed_came.astype(jnp.float32))
    normed_pair = other(grad_normed_mine, "y")
    down_parts = undeal(after(down_sums, grad_normed_mine))
    normed_pair = after(normed_pair, down_parts)
    grad_normed_two = grad_normed_mine.astype(jnp.float32) + normed_pair.astype(jnp.float32)
    down_own, down_across = sum_core(after(down_part, normed_pair), rows)

    back_two, grad_gain_two = norm_back(middle, scale_two, gain_two, grad_normed_two)
    grad_middle = cotangent.astype(jnp.float32) + back_two
    grad_att = low(grad_middle)
    grad_out_all = product_left(attended_low, grad_att).T
    grad_attended = product(grad_att, w_out_all)
    grad_query_pre, buffer = attend_back(
        bounds, query_rows, grad_attended, attended, totals,
        cosine_head, sine_head, place, key_value,
    )
    grad_query_mine = low(product_right(grad_query_pre, w_query_all))
    query_came = other(grad_query_mine, "y")
    key_value_halves = scatter_core(buffer, rows)
    square_grads = row_major(
        low(jnp.concatenate([product_left(grad_query_pre, normed_one).T, grad_out_all], axis=1))
    )
    key_value_sums = scatter_across(
        key_value_halves, gate_sums, square_grads, grad_query_mine, down_across
    )
    gate_parts = undeal(after(gate_sums, key_value_sums))
    square_halves = scatter_core(after(square_grads, key_value_sums), features)
    key_value_grads = halve_z(key_value_sums, rows, key_value_sums, query_came)
    square_sums = scatter_across(square_halves)
    key_value_grads = after(key_value_grads, up_sums)
    down_came = other(after(down_across, key_value_sums), "x")
    grad_key_pre = low(
        rotate_halves(key_value_grads[:, :head].reshape(rows, 1, head), cosine_table, -sine_table)
    ).reshape(rows, head)
    grad_value_pre = low(key_value_grads[:, head:])
    grad_pair = jnp.concatenate([grad_key_pre, grad_value_pre], axis=1)
    grad_project = jnp.concatenate([grad_query_pre, grad_pair], axis=1)
    grad_bias = jnp.sum(grad_project.astype(jnp.float32), axis=0)
    pair_both = in_order(grad_pair, other(grad_pair, "y"))
    query_came = after(query_came, grad_pair, down_came)
    grad_normed_one = (
        grad_query_mine.astype(jnp.float32) + query_came.astype(jnp.float32)
    ) + product_right(
        pair_both, in_order(w_pair[:, : 2 * head], pair_weights_came)
    )
    down_mine = low(down_own + after(down_came, pair_both).astype(jnp.float32))
    down_pair = other(down_mine, "y")
    result = low(middle + down_mine.astype(jnp.float32) + down_pair.astype(jnp.float32))
    back_one, grad_gain_one = norm_back(inputs, scale_one, gain_one, grad_normed_one)
    grad_tokens = low(grad_middle + back_one)

    small_grads = jnp.concatenate(
        [
            grad_gain_one.reshape(devices, -1),
            grad_gain_two.reshape(devices, -1),
            grad_bias[:heads_width]
            .reshape(query_group, devices, piece)
            .transpose(1, 0, 2)
            .reshape(devices, -1),
            grad_bias[heads_width : heads_width + head].reshape(devices, -1),
            grad_bias[heads_width + head :].reshape(devices, -1),
        ],
        axis=1,
    )
    small_grads = jnp.pad(small_grads, ((0, 0), (0, features * head - small_grads.shape[1])))
    packed_grads = low(
        jnp.concatenate(
            [product_left(grad_pair, normed_one).T, small_grads.reshape(devices * features, head)],
            axis=1,
        )
    )
    up_parts = undeal(after(up_sums, grad_pair))
    packed_grads = scatter_across(
        scatter_core(packed_grads, features), gate_parts, square_sums
    )
    last_grads = scatter_z(jnp.concatenate([square_sums, packed_grads], axis=1)).astype(jnp.float32)
    square_grads = last_grads[:, : 2 * heads_width]
    packed_grads = last_grads[:, 2 * heads_width :]
    small_own = packed_grads[:, 2 * head :].reshape(-1)
    grad_w_out = square_grads[:, heads_width:].T
    grad_w_down = undeal_end(down_parts).T
    grad_w_gate = undeal_end(gate_parts)
    grad_w_up = undeal_end(up_parts)
    return (
        result,
        grad_tokens,
        small_own[cuts[0] : cuts[1]],
        square_grads[:, :heads_width],
        small_own[cuts[2] : cuts[3]].reshape(query_group, piece),
        packed_grads[:, :head],
        small_own[cuts[3] : cuts[4]].reshape(1, piece),
        packed_grads[:, head : 2 * head],
        small_own[cuts[4] : cuts[5]].reshape(1, piece),
        grad_w_out,
        small_own[cuts[1] : cuts[2]],
        grad_w_gate,
        grad_w_up,
        grad_w_down,
    )


def solution(mesh):
    wide, narrow = mesh.devices.shape
    grouped = Mesh(mesh.devices.reshape(wide // 4, 2, 2, narrow), WIDE + ("y",))
    rows = P(WIDE, None)
    vector = P(WIDE)
    columns = P(WIDE, "y")
    lines = P("y", WIDE)
    return jax.shard_map(
        local,
        mesh=grouped,
        in_specs=(rows, P(), vector, columns, lines, columns, lines, columns, lines, lines,
                  vector, columns, columns, lines, rows),
        out_specs=(rows, rows, vector, columns, lines, columns, lines, columns, lines, lines,
                   vector, columns, columns, lines),
        check_vma=False,
    )
```

```python
import math

import jax
import jax.numpy as jnp
from jax import lax
from jax.experimental import pallas as pl
from jax.experimental.layout import Layout, with_layout_constraint
from jax.experimental.pallas import tpu as pltpu
from jax.sharding import Mesh
from jax.sharding import PartitionSpec as P

ROPE_BASE = 10000.0
EPSILON = 1e-06


def product(left, right):
    return jnp.dot(left, right, preferred_element_type=jnp.float32)


def product_left(left, right):
    return lax.dot_general(
        left, right, (((0,), (0,)), ((), ())), preferred_element_type=jnp.float32
    )


def product_right(left, right):
    return lax.dot_general(
        left, right, (((1,), (1,)), ((), ())), preferred_element_type=jnp.float32
    )


def rotate_halves(value_rows, cosine_table, sine_table):
    middle_at = value_rows.shape[-1] // 2
    first = value_rows[..., :middle_at]
    second = value_rows[..., middle_at:]
    return jnp.concatenate(
        [first * cosine_table - second * sine_table, second * cosine_table + first * sine_table],
        axis=-1,
    )


def norm_scale(value_rows):
    return lax.rsqrt(jnp.mean(value_rows * value_rows, axis=-1, keepdims=True) + EPSILON)


def norm_back(value_rows, scale, gain, grad):
    normed = value_rows * scale
    inner = grad * gain
    back = scale * (inner - normed * jnp.mean(inner * normed, axis=-1, keepdims=True))
    return (back, jnp.sum(grad * normed, axis=0))


WIDE = ("z", "x", "c")
GROUP = ("x", "c")


def other(value, axis):
    return lax.ppermute(value, axis, [(0, 1), (1, 0)])


def low(value):
    return value.astype(jnp.bfloat16)


def after(value, *earlier):
    return lax.optimization_barrier((value, *earlier))[0]


def row_major(value):
    return with_layout_constraint(value, Layout(major_to_minor=(0, 1)))


def in_order(own, came):
    first = lax.axis_index("y") == 0
    return jnp.concatenate([jnp.where(first, own, came), jnp.where(first, came, own)], axis=1)


def gather_group(own):
    core = other(own, "c")
    across = other(own, "x")
    far = other(across, "c")
    return jnp.concatenate([own, core, across, far], axis=0)


def sum_core(partial, rows):
    sent = low(jnp.concatenate([partial[rows : 2 * rows], partial[3 * rows :]], axis=0))
    core = other(sent, "c").astype(jnp.float32)
    return partial[:rows] + core[:rows], low(partial[2 * rows : 3 * rows] + core[rows:])


def sum_narrow(partial):
    mine = low(partial)
    return mine.astype(jnp.float32) + other(mine, "y").astype(jnp.float32)


def deal(weight):
    features, hidden = weight.shape
    parts = weight.reshape(features, 4, hidden // 4).transpose(1, 0, 2)
    parts = lax.all_to_all(parts, GROUP, split_axis=0, concat_axis=0, tiled=True)
    return parts.reshape(4 * features, hidden // 4)


def gather_z(own):
    return lax.all_gather(own, "z", axis=0, tiled=True)


def scatter_z(whole):
    return lax.psum_scatter(whole, "z", scatter_dimension=0, tiled=True)


def undeal(grad):
    features = grad.shape[0] // 4
    parts = grad.reshape(4, features, grad.shape[1])
    return lax.all_to_all(parts, GROUP, split_axis=0, concat_axis=0, tiled=True)


def undeal_end(parts):
    count, features, hidden = parts.shape
    return parts.transpose(1, 0, 2).reshape(features, count * hidden).astype(jnp.float32)


def gather_rest(column, rows):
    own = column.reshape(-1, 1, 1, rows, column.shape[1])
    near = other(own, "x")
    at_x = lax.axis_index("x")
    at_c = lax.axis_index("c")
    whole = jnp.zeros((own.shape[0], 2, 2, *own.shape[3:]), column.dtype)
    for piece, x_place, c_place in (
        (own, at_x, at_c),
        (other(own, "c"), at_x, 1 - at_c),
        (near, 1 - at_x, at_c),
        (other(near, "c"), 1 - at_x, 1 - at_c),
    ):
        whole = lax.dynamic_update_slice(whole, piece, (0, x_place, c_place, 0, 0))
    return whole.reshape(-1, column.shape[1])


def other_half(whole, axis, position):
    at = lax.axis_index(axis)
    sent = lax.dynamic_slice_in_dim(whole, 1 - at, 1, position)
    return lax.dynamic_slice_in_dim(whole, at, 1, position), other(sent, axis)


def halve_z(column, rows, early, late):
    high = lax.axis_size("z")
    at_z = lax.axis_index("z")
    step = 1
    while step < high:
        parts = column.reshape(-1, 2, rows, column.shape[1])
        at = (at_z // step) % 2
        sent = lax.dynamic_slice_in_dim(parts, 1 - at, 1, 1)
        kept = lax.dynamic_slice_in_dim(parts, at, 1, 1)
        came = lax.ppermute(sent, "z", [(number, number ^ step) for number in range(high)])
        came = after(came, *(early if step == 1 else late))
        column = kept.astype(jnp.float32) + came.astype(jnp.float32)
        column = column.reshape(-1, column.shape[3])
        step *= 2
        column = low(column) if step < high else column
    return column


def add_half(halves, *earlier):
    kept, came = halves
    return low(kept.astype(jnp.float32) + after(came, *earlier).astype(jnp.float32))


def scatter_core(whole, rows, *earlier):
    parts = whole.reshape(-1, 2, 2, rows, whole.shape[1])
    return other_half(add_half(other_half(parts, "c", 2), *earlier), "x", 1)


def scatter_across(halves, *earlier):
    summed = add_half(halves, *earlier)
    return summed.reshape(-1, summed.shape[4])


def rotate_rows(value_rows, cosine, sine):
    return value_rows * cosine + pltpu.roll(value_rows, value_rows.shape[1] // 2, 1) * sine


def mask_bias(place_ref, begin, span):
    rows = place_ref.shape[1]
    key_index = begin + lax.broadcasted_iota(jnp.int32, (span, rows), 0)
    allowed = (key_index >= place_ref[0:1, :]) & (key_index <= place_ref[1:2, :])
    return jnp.where(allowed, 0.0, -1e30)


def turned(value):
    return value.astype(jnp.float32).T.astype(value.dtype)


def attend_kernel(
    bounds_ref, query_ref, cosine_ref, sine_ref, place_ref, pair_ref,
    rotated_ref, attended_ref, totals_ref, sums_ref,
):
    rows, wide = query_ref.shape
    head = cosine_ref.shape[1]
    factor = math.log2(math.e) / math.sqrt(head)
    cosine = cosine_ref[...]
    sine = sine_ref[...]
    for at in range(0, wide, head):
        rotated_ref[:, at : at + head] = low(
            rotate_rows(query_ref[:, at : at + head], cosine, sine)
        )
    sums_ref[...] = jnp.zeros_like(sums_ref)
    totals_ref[...] = jnp.zeros_like(totals_ref)

    def step(number, carry):
        begin = pl.multiple_of(number * rows, rows)
        keys = pair_ref[pl.ds(begin, rows), :head]
        values_turned = turned(pair_ref[pl.ds(begin, rows), head:])
        bias = mask_bias(place_ref, begin, rows)
        for order in range(wide // head):
            at = order * head
            scores = product_right(keys, rotated_ref[:, at : at + head])
            weights = jnp.exp2(scores * factor + bias)
            totals_ref[order : order + 1, :] += jnp.sum(weights, axis=0, keepdims=True)
            sums_ref[at : at + head, :] += product(values_turned, low(weights))
        return carry

    lax.fori_loop(bounds_ref[0], bounds_ref[1] + 1, step, 0)
    for order in range(wide // head):
        at = order * head
        attended_ref[:, at : at + head] = (
            sums_ref[at : at + head, :] / totals_ref[order : order + 1, :]
        ).T


def attend_back_kernel(
    bounds_ref, rotated_ref, grad_ref, attended_ref, totals_ref, cosine_ref, sine_ref, place_ref,
    pair_ref, grad_query_ref, grad_pair_ref, sums_ref, accum_ref, delta_ref,
):
    rows, wide = rotated_ref.shape
    head = cosine_ref.shape[1]
    scale = 1.0 / math.sqrt(head)
    factor = math.log2(math.e) * scale
    for order in range(wide // head):
        at = order * head
        totals = jnp.broadcast_to(totals_ref[order : order + 1, :], (head, rows)).T
        divided = grad_ref[:, at : at + head] / totals
        accum_ref[:, at : at + head] = low(divided)
        delta_ref[order : order + 1, :] = jnp.sum(
            (divided * attended_ref[:, at : at + head]).T, axis=0, keepdims=True
        )

    def clear(number, carry):
        begin = pl.multiple_of(number * rows, rows)
        grad_pair_ref[pl.ds(begin, rows), :] = jnp.zeros((rows, 2 * head), jnp.bfloat16)
        return carry

    lax.fori_loop(0, grad_pair_ref.shape[0] // rows, clear, 0)
    sums_ref[...] = jnp.zeros_like(sums_ref)

    def step(number, carry):
        begin = pl.multiple_of(number * rows, rows)
        keys = pair_ref[pl.ds(begin, rows), :head]
        values = pair_ref[pl.ds(begin, rows), head:]
        keys_turned = turned(keys)
        bias = mask_bias(place_ref, begin, rows)
        grad_keys = jnp.zeros((rows, head), jnp.float32)
        grad_values = jnp.zeros((rows, head), jnp.float32)
        for order in range(wide // head):
            at = order * head
            query = rotated_ref[:, at : at + head]
            accum = accum_ref[:, at : at + head]
            weights = jnp.exp2(product_right(keys, query) * factor + bias)
            grad_scores = low(
                weights * (product_right(values, accum) - delta_ref[order : order + 1, :])
            )
            grad_values += product(low(weights), accum)
            grad_keys += product(grad_scores, query)
            sums_ref[at : at + head, :] += product(keys_turned, grad_scores)
        grad_pair_ref[pl.ds(begin, rows), :head] = low(grad_keys * scale)
        grad_pair_ref[pl.ds(begin, rows), head:] = low(grad_values)
        return carry

    lax.fori_loop(bounds_ref[0], bounds_ref[1] + 1, step, 0)
    cosine = cosine_ref[...]
    sine = -sine_ref[...]
    for order in range(wide // head):
        at = order * head
        grad_query_ref[:, at : at + head] = low(
            rotate_rows(sums_ref[at : at + head, :].T * scale, cosine, sine)
        )


def in_vmem(count):
    return [pl.BlockSpec(memory_space=pltpu.SMEM)] + [
        pl.BlockSpec(memory_space=pltpu.VMEM) for _ in range(count)
    ]


def attend(bounds, query_pre, cosine, sine, place, pair):
    rows, wide = query_pre.shape
    return pl.pallas_call(
        attend_kernel,
        out_shape=(
            jax.ShapeDtypeStruct((rows, wide), jnp.bfloat16),
            jax.ShapeDtypeStruct((rows, wide), jnp.float32),
            jax.ShapeDtypeStruct((8 * -(-wide // cosine.shape[1] // 8), rows), jnp.float32),
        ),
        in_specs=in_vmem(5),
        out_specs=tuple(in_vmem(3)[1:]),
        scratch_shapes=[pltpu.VMEM((wide, rows), jnp.float32)],
        cost_estimate=pl.CostEstimate(
            flops=4 * 9 * rows * rows * wide, transcendentals=9 * rows * rows * 6, bytes_accessed=20 << 20
        ),
        name="attend",
    )(bounds, query_pre, cosine, sine, place, pair)


def attend_back(bounds, rotated, grad, attended, totals, cosine, sine, place, pair):
    rows, wide = rotated.shape
    return pl.pallas_call(
        attend_back_kernel,
        out_shape=(
            jax.ShapeDtypeStruct((rows, wide), jnp.bfloat16),
            jax.ShapeDtypeStruct(pair.shape, jnp.bfloat16),
        ),
        in_specs=in_vmem(8),
        out_specs=tuple(in_vmem(2)[1:]),
        scratch_shapes=[
            pltpu.VMEM((wide, rows), jnp.float32),
            pltpu.VMEM((rows, wide), jnp.bfloat16),
            pltpu.VMEM(totals.shape, jnp.float32),
        ],
        cost_estimate=pl.CostEstimate(
            flops=rows * wide, transcendentals=0, bytes_accessed=rows * wide
        ),
        name="attend_back",
    )(bounds, rotated, grad, attended, totals, cosine, sine, place, pair)


def local(
    tokens,
    lengths,
    norm1_gain,
    w_query,
    b_query,
    key_projection,
    key_bias_vector,
    value_projection,
    value_bias_vector,
    w_out,
    norm2_gain,
    w_gate,
    w_up,
    w_down,
    cotangent,
):
    rows, width = tokens.shape
    devices = lax.axis_size(WIDE)
    own_index = lax.axis_index(WIDE)
    first = own_index * rows
    index = first + jnp.arange(rows, dtype=jnp.int32)
    ends = jnp.cumsum(lengths, dtype=jnp.int32)
    starts = ends - lengths
    seq_start = jnp.max(jnp.where(starts[None, :] <= index[:, None], starts[None, :], 0), axis=1)
    lowest = jnp.min(seq_start)
    highest = first + rows - 1
    head = key_projection.shape[1]
    freq = 1.0 / ROPE_BASE ** (jnp.arange(head // 2, dtype=jnp.float32) * 2.0 / head)
    angle = (index - seq_start).astype(jnp.float32)[:, None] * freq[None, :]
    cosine_table = jnp.cos(angle)[:, None, :]
    sine_table = jnp.sin(angle)[:, None, :]
    cosine_head = jnp.concatenate([cosine_table[:, 0], cosine_table[:, 0]], axis=1)
    sine_head = jnp.concatenate([-sine_table[:, 0], sine_table[:, 0]], axis=1)
    place = jnp.concatenate([seq_start[None], index[None], jnp.zeros((6, rows), jnp.int32)], axis=0)
    bounds = jnp.stack([lowest // rows, highest // rows])
    features = w_query.shape[0]
    heads_width = w_query.shape[1]
    query_group = heads_width // head
    projected = heads_width + 2 * head

    piece = b_query.shape[1]
    small_parts = [norm1_gain, norm2_gain, b_query.reshape(-1), key_bias_vector.reshape(-1),
                   value_bias_vector.reshape(-1)]
    small_sizes = [part.shape[0] for part in small_parts]
    small_rows = -(-sum(small_sizes) // head)
    small = jnp.concatenate(small_parts)
    small = jnp.pad(small, (0, features * head - small.shape[0])).reshape(features, head)
    square_pack = jnp.concatenate([w_query, w_out.T], axis=1)
    square_column = gather_z(square_pack)
    pair_pack = jnp.concatenate([key_projection, value_projection, small], axis=1)
    pair_column = gather_z(after(pair_pack, square_pack))
    gate_own = deal(after(w_gate, pair_column))
    w_pair = gather_rest(pair_column, features)
    pair_weights_came = other(w_pair[:, : 2 * head], "y")
    small_all = w_pair[:, 2 * head :].reshape(devices, features, head)[:, :small_rows]
    small_all = small_all.reshape(devices, small_rows * head).astype(jnp.float32)
    cuts = [0]
    for size in small_sizes:
        cuts.append(cuts[-1] + size)
    gain_one = small_all[:, cuts[0] : cuts[1]].reshape(-1)
    gain_two = small_all[:, cuts[1] : cuts[2]].reshape(-1)
    bias_query = small_all[:, cuts[2] : cuts[3]].reshape(devices, query_group, piece)
    bias_query = bias_query.transpose(1, 0, 2).reshape(-1)
    bias_key = small_all[:, cuts[3] : cuts[4]].reshape(-1)
    bias_value = small_all[:, cuts[4] : cuts[5]].reshape(-1)


    inputs = tokens.astype(jnp.float32)
    scale_one = norm_scale(inputs)
    normed_one = low(inputs * scale_one * gain_one)
    projections = product(normed_one, w_pair[:, : 2 * head])
    key_pre = projections[:, :head] + bias_key
    key_rows = low(
        rotate_halves(key_pre.reshape(rows, 1, head), cosine_table, sine_table).reshape(rows, head)
    )
    value_rows = low(projections[:, head:] + bias_value)
    key_value = jnp.concatenate([key_rows, value_rows], axis=1)
    gate_all = gather_z(gate_own)
    key_value_column = gather_z(after(key_value, gate_own, square_column))
    down_own = deal(after(w_down, key_value).T)
    w_square = gather_rest(square_column, features)
    w_query_all = w_square[:, :heads_width]
    w_out_all = w_square[:, heads_width:]
    query_pre = product(normed_one, w_query_all) + bias_query
    key_value_column = after(key_value_column, down_own)
    down_all = gather_z(down_own)
    up_own = deal(after(w_up, key_value_column))
    up_all = gather_z(up_own)
    key_value = after(gather_rest(key_value_column, rows), up_own, pair_weights_came)
    cotangent_group = gather_group(after(cotangent, key_value))
    cotangent_turned = lax.optimization_barrier(cotangent_group.T)
    query_rows, attended, totals = attend(
        bounds, query_pre, cosine_head, sine_head, place, key_value
    )
    attended_low = low(attended)
    attention = low(product_right(attended_low, w_out_all))
    attention_came = after(
        other(attention, "y"), cotangent_group, cotangent_turned
    )
    middle = inputs + (attention.astype(jnp.float32) + attention_came.astype(jnp.float32))
    scale_two = norm_scale(middle)
    normed_two = low(middle * scale_two * gain_two)
    normed_group = gather_group(normed_two)
    normed_turned = lax.optimization_barrier(normed_group.T)
    gate = product(normed_group, gate_all)
    grad_hidden = lax.optimization_barrier(product(cotangent_group, down_all))
    up_all = after(up_all, normed_turned, grad_hidden)
    up_part = product(normed_group, up_all)
    sigmoid_gate = jax.nn.sigmoid(gate)
    silu_gate = gate * sigmoid_gate
    hidden = low(silu_gate * up_part)
    grad_down = row_major(low(product(cotangent_turned, hidden)))
    down_sums = scatter_z(grad_down)
    grad_gate = low(grad_hidden * up_part * sigmoid_gate * (1.0 + gate * (1.0 - sigmoid_gate)))
    grad_up = low(grad_hidden * silu_gate)
    grad_normed_part = product_right(grad_gate, gate_all) + product_right(grad_up, up_all)
    grad_normed_own, grad_normed_across = sum_core(grad_normed_part, rows)
    normed_came = other(grad_normed_across, "x")
    grad_gate_all = row_major(low(product(normed_turned, after(grad_gate, grad_normed_across))))
    gate_sums = scatter_z(grad_gate_all)
    grad_up_all = row_major(low(product(normed_turned, after(grad_up, grad_gate_all))))
    up_sums = scatter_z(grad_up_all)
    down_part = product_right(after(hidden, grad_up_all, down_sums), down_all)
    normed_came = after(normed_came, down_part)
    grad_normed_mine = low(grad_normed_own + normed_came.astype(jnp.float32))
    normed_pair = other(grad_normed_mine, "y")
    down_parts = undeal(after(down_sums, grad_normed_mine))
    normed_pair = after(normed_pair, down_parts)
    grad_normed_two = grad_normed_mine.astype(jnp.float32) + normed_pair.astype(jnp.float32)
    down_own, down_across = sum_core(after(down_part, normed_pair), rows)

    back_two, grad_gain_two = norm_back(middle, scale_two, gain_two, grad_normed_two)
    grad_middle = cotangent.astype(jnp.float32) + back_two
    grad_att = low(grad_middle)
    grad_out_all = product_left(attended_low, grad_att).T
    grad_attended = product(grad_att, w_out_all)
    grad_query_pre, buffer = attend_back(
        bounds, query_rows, grad_attended, attended, totals,
        cosine_head, sine_head, place, key_value,
    )
    grad_query_mine = low(product_right(grad_query_pre, w_query_all))
    query_came = other(grad_query_mine, "y")
    key_value_halves = scatter_core(buffer, rows)
    square_grads = row_major(
        low(jnp.concatenate([product_left(grad_query_pre, normed_one).T, grad_out_all], axis=1))
    )
    key_value_sums = scatter_across(
        key_value_halves, gate_sums, square_grads, grad_query_mine, down_across
    )
    down_came = other(after(down_across, key_value_sums), "x")
    gate_parts = undeal(after(gate_sums, key_value_sums))
    square_halves = scatter_core(after(square_grads, key_value_sums), features)
    key_value_grads = halve_z(key_value_sums, rows, (key_value_sums,), (query_came, gate_parts, down_came))
    key_value_grads = after(key_value_grads, up_sums)
    grad_key_pre = low(
        rotate_halves(key_value_grads[:, :head].reshape(rows, 1, head), cosine_table, -sine_table)
    ).reshape(rows, head)
    grad_value_pre = low(key_value_grads[:, head:])
    grad_pair = jnp.concatenate([grad_key_pre, grad_value_pre], axis=1)
    grad_project = jnp.concatenate([grad_query_pre, grad_pair], axis=1)
    grad_bias = jnp.sum(grad_project.astype(jnp.float32), axis=0)
    pair_both = in_order(grad_pair, other(grad_pair, "y"))
    query_came = after(query_came, grad_pair, square_halves[0])
    grad_normed_one = (
        grad_query_mine.astype(jnp.float32) + query_came.astype(jnp.float32)
    ) + product_right(
        pair_both, in_order(w_pair[:, : 2 * head], pair_weights_came)
    )
    down_mine = low(down_own + after(down_came, key_value_sums).astype(jnp.float32))
    down_pair = other(down_mine, "y")
    result = low(middle + down_mine.astype(jnp.float32) + down_pair.astype(jnp.float32))
    back_one, grad_gain_one = norm_back(inputs, scale_one, gain_one, grad_normed_one)
    grad_tokens = low(grad_middle + back_one)

    small_grads = jnp.concatenate(
        [
            grad_gain_one.reshape(devices, -1),
            grad_gain_two.reshape(devices, -1),
            grad_bias[:heads_width]
            .reshape(query_group, devices, piece)
            .transpose(1, 0, 2)
            .reshape(devices, -1),
            grad_bias[heads_width : heads_width + head].reshape(devices, -1),
            grad_bias[heads_width + head :].reshape(devices, -1),
        ],
        axis=1,
    )
    small_grads = jnp.pad(small_grads, ((0, 0), (0, features * head - small_grads.shape[1])))
    packed_grads = low(
        jnp.concatenate(
            [product_left(grad_pair, normed_one).T, small_grads.reshape(devices * features, head)],
            axis=1,
        )
    )
    packed_halves = other_half(
        packed_grads.reshape(-1, 2, 2, features, packed_grads.shape[1]), "c", 2
    )
    square_sums = scatter_across(square_halves, packed_halves[1], down_pair)
    packed_grads = scatter_across(other_half(add_half(packed_halves), "x", 1))
    up_parts = undeal(after(up_sums, packed_halves[1]))
    last_grads = scatter_z(jnp.concatenate([square_sums, packed_grads], axis=1)).astype(jnp.float32)
    square_grads = last_grads[:, : 2 * heads_width]
    packed_grads = last_grads[:, 2 * heads_width :]
    small_own = packed_grads[:, 2 * head :].reshape(-1)
    grad_w_out = square_grads[:, heads_width:].T
    grad_w_down = undeal_end(down_parts).T
    grad_w_gate = undeal_end(gate_parts)
    grad_w_up = undeal_end(up_parts)
    return (
        result,
        grad_tokens,
        small_own[cuts[0] : cuts[1]],
        square_grads[:, :heads_width],
        small_own[cuts[2] : cuts[3]].reshape(query_group, piece),
        packed_grads[:, :head],
        small_own[cuts[3] : cuts[4]].reshape(1, piece),
        packed_grads[:, head : 2 * head],
        small_own[cuts[4] : cuts[5]].reshape(1, piece),
        grad_w_out,
        small_own[cuts[1] : cuts[2]],
        grad_w_gate,
        grad_w_up,
        grad_w_down,
    )


def solution(mesh):
    wide, narrow = mesh.devices.shape
    grouped = Mesh(mesh.devices.reshape(wide // 4, 2, 2, narrow), WIDE + ("y",))
    rows = P(WIDE, None)
    vector = P(WIDE)
    columns = P(WIDE, "y")
    lines = P("y", WIDE)
    return jax.shard_map(
        local,
        mesh=grouped,
        in_specs=(rows, P(), vector, columns, lines, columns, lines, columns, lines, lines,
                  vector, columns, columns, lines, rows),
        out_specs=(rows, rows, vector, columns, lines, columns, lines, columns, lines, lines,
                   vector, columns, columns, lines),
        check_vma=False,
    )
```

```python
import math

import jax
import jax.numpy as jnp
from jax import lax
from jax.experimental import pallas as pl
from jax.experimental.layout import Layout, with_layout_constraint
from jax.experimental.pallas import tpu as pltpu
from jax.sharding import Mesh
from jax.sharding import PartitionSpec as P

ROPE_BASE = 10000.0
EPSILON = 1e-06


def product(left, right):
    return jnp.dot(left, right, preferred_element_type=jnp.float32)


def product_left(left, right):
    return lax.dot_general(
        left, right, (((0,), (0,)), ((), ())), preferred_element_type=jnp.float32
    )


def product_right(left, right):
    return lax.dot_general(
        left, right, (((1,), (1,)), ((), ())), preferred_element_type=jnp.float32
    )


def rotate_halves(value_rows, cosine_table, sine_table):
    middle_at = value_rows.shape[-1] // 2
    first = value_rows[..., :middle_at]
    second = value_rows[..., middle_at:]
    return jnp.concatenate(
        [first * cosine_table - second * sine_table, second * cosine_table + first * sine_table],
        axis=-1,
    )


def norm_scale(value_rows):
    return lax.rsqrt(jnp.mean(value_rows * value_rows, axis=-1, keepdims=True) + EPSILON)


def norm_back(value_rows, scale, gain, grad):
    normed = value_rows * scale
    inner = grad * gain
    back = scale * (inner - normed * jnp.mean(inner * normed, axis=-1, keepdims=True))
    return (back, jnp.sum(grad * normed, axis=0))


WIDE = ("z", "x", "c")
GROUP = ("x", "c")


def other(value, axis):
    return lax.ppermute(value, axis, [(0, 1), (1, 0)])


def low(value):
    return value.astype(jnp.bfloat16)


def after(value, *earlier):
    return lax.optimization_barrier((value, *earlier))[0]


def row_major(value):
    return with_layout_constraint(value, Layout(major_to_minor=(0, 1)))


def in_order(own, came):
    first = lax.axis_index("y") == 0
    return jnp.concatenate([jnp.where(first, own, came), jnp.where(first, came, own)], axis=1)


def gather_group(own):
    core = other(own, "c")
    across = other(own, "x")
    far = other(across, "c")
    return jnp.concatenate([own, core, across, far], axis=0)


def sum_core(partial, rows):
    sent = low(jnp.concatenate([partial[rows : 2 * rows], partial[3 * rows :]], axis=0))
    core = other(sent, "c").astype(jnp.float32)
    return partial[:rows] + core[:rows], low(partial[2 * rows : 3 * rows] + core[rows:])


def sum_narrow(partial):
    mine = low(partial)
    return mine.astype(jnp.float32) + other(mine, "y").astype(jnp.float32)


def deal(weight):
    features, hidden = weight.shape
    parts = weight.reshape(features, 4, hidden // 4).transpose(1, 0, 2)
    parts = lax.all_to_all(parts, GROUP, split_axis=0, concat_axis=0, tiled=True)
    return parts.reshape(4 * features, hidden // 4)


def gather_z(own):
    return lax.all_gather(own, "z", axis=0, tiled=True)


def scatter_z(whole):
    return lax.psum_scatter(whole, "z", scatter_dimension=0, tiled=True)


def undeal(grad):
    features = grad.shape[0] // 4
    parts = grad.reshape(4, features, grad.shape[1])
    return lax.all_to_all(parts, GROUP, split_axis=0, concat_axis=0, tiled=True)


def undeal_end(parts):
    count, features, hidden = parts.shape
    return parts.transpose(1, 0, 2).reshape(features, count * hidden).astype(jnp.float32)


def gather_rest(column, rows):
    own = column.reshape(-1, 1, 1, rows, column.shape[1])
    near = other(own, "x")
    at_x = lax.axis_index("x")
    at_c = lax.axis_index("c")
    whole = jnp.zeros((own.shape[0], 2, 2, *own.shape[3:]), column.dtype)
    for piece, x_place, c_place in (
        (own, at_x, at_c),
        (other(own, "c"), at_x, 1 - at_c),
        (near, 1 - at_x, at_c),
        (other(near, "c"), 1 - at_x, 1 - at_c),
    ):
        whole = lax.dynamic_update_slice(whole, piece, (0, x_place, c_place, 0, 0))
    return whole.reshape(-1, column.shape[1])


def other_half(whole, axis, position):
    at = lax.axis_index(axis)
    sent = lax.dynamic_slice_in_dim(whole, 1 - at, 1, position)
    return lax.dynamic_slice_in_dim(whole, at, 1, position), other(sent, axis)


def halve_z(column, rows, early, late):
    high = lax.axis_size("z")
    at_z = lax.axis_index("z")
    step = 1
    while step < high:
        parts = column.reshape(-1, 2, rows, column.shape[1])
        at = (at_z // step) % 2
        sent = lax.dynamic_slice_in_dim(parts, 1 - at, 1, 1)
        kept = lax.dynamic_slice_in_dim(parts, at, 1, 1)
        came = lax.ppermute(sent, "z", [(number, number ^ step) for number in range(high)])
        came = after(came, *(early if step == 1 else late))
        column = kept.astype(jnp.float32) + came.astype(jnp.float32)
        column = column.reshape(-1, column.shape[3])
        step *= 2
        column = low(column) if step < high else column
    return column


def add_half(halves, *earlier):
    kept, came = halves
    return low(kept.astype(jnp.float32) + after(came, *earlier).astype(jnp.float32))


def scatter_core(whole, rows, *earlier):
    parts = whole.reshape(-1, 2, 2, rows, whole.shape[1])
    return other_half(add_half(other_half(parts, "c", 2), *earlier), "x", 1)


def scatter_across(halves, *earlier):
    summed = add_half(halves, *earlier)
    return summed.reshape(-1, summed.shape[4])


def rotate_rows(value_rows, cosine, sine):
    return value_rows * cosine + pltpu.roll(value_rows, value_rows.shape[1] // 2, 1) * sine


def mask_bias(place_ref, begin, span):
    rows = place_ref.shape[1]
    key_index = begin + lax.broadcasted_iota(jnp.int32, (span, rows), 0)
    allowed = (key_index >= place_ref[0:1, :]) & (key_index <= place_ref[1:2, :])
    return jnp.where(allowed, 0.0, -1e30)


def turned(value):
    return value.astype(jnp.float32).T.astype(value.dtype)


def attend_kernel(
    bounds_ref, query_ref, cosine_ref, sine_ref, place_ref, pair_ref,
    rotated_ref, attended_ref, totals_ref, sums_ref,
):
    rows, wide = query_ref.shape
    head = cosine_ref.shape[1]
    factor = math.log2(math.e) / math.sqrt(head)
    cosine = cosine_ref[...]
    sine = sine_ref[...]
    for at in range(0, wide, head):
        rotated_ref[:, at : at + head] = low(
            rotate_rows(query_ref[:, at : at + head], cosine, sine)
        )
    sums_ref[...] = jnp.zeros_like(sums_ref)
    totals_ref[...] = jnp.zeros_like(totals_ref)

    def step(number, carry):
        begin = pl.multiple_of(number * rows, rows)
        keys = pair_ref[pl.ds(begin, rows), :head]
        values_turned = turned(pair_ref[pl.ds(begin, rows), head:])
        bias = mask_bias(place_ref, begin, rows)
        for order in range(wide // head):
            at = order * head
            scores = product_right(keys, rotated_ref[:, at : at + head])
            weights = jnp.exp2(scores * factor + bias)
            totals_ref[order : order + 1, :] += jnp.sum(weights, axis=0, keepdims=True)
            sums_ref[at : at + head, :] += product(values_turned, low(weights))
        return carry

    lax.fori_loop(bounds_ref[0], bounds_ref[1] + 1, step, 0)
    for order in range(wide // head):
        at = order * head
        attended_ref[:, at : at + head] = (
            sums_ref[at : at + head, :] / totals_ref[order : order + 1, :]
        ).T


def attend_back_kernel(
    bounds_ref, rotated_ref, grad_ref, attended_ref, totals_ref, cosine_ref, sine_ref, place_ref,
    pair_ref, grad_query_ref, grad_pair_ref, sums_ref, accum_ref, delta_ref,
):
    rows, wide = rotated_ref.shape
    head = cosine_ref.shape[1]
    scale = 1.0 / math.sqrt(head)
    factor = math.log2(math.e) * scale
    for order in range(wide // head):
        at = order * head
        totals = jnp.broadcast_to(totals_ref[order : order + 1, :], (head, rows)).T
        divided = grad_ref[:, at : at + head] / totals
        accum_ref[:, at : at + head] = low(divided)
        delta_ref[order : order + 1, :] = jnp.sum(
            (divided * attended_ref[:, at : at + head]).T, axis=0, keepdims=True
        )

    def clear(number, carry):
        begin = pl.multiple_of(number * rows, rows)
        grad_pair_ref[pl.ds(begin, rows), :] = jnp.zeros((rows, 2 * head), jnp.bfloat16)
        return carry

    lax.fori_loop(0, grad_pair_ref.shape[0] // rows, clear, 0)
    sums_ref[...] = jnp.zeros_like(sums_ref)

    def step(number, carry):
        begin = pl.multiple_of(number * rows, rows)
        keys = pair_ref[pl.ds(begin, rows), :head]
        values = pair_ref[pl.ds(begin, rows), head:]
        keys_turned = turned(keys)
        bias = mask_bias(place_ref, begin, rows)
        grad_keys = jnp.zeros((rows, head), jnp.float32)
        grad_values = jnp.zeros((rows, head), jnp.float32)
        for order in range(wide // head):
            at = order * head
            query = rotated_ref[:, at : at + head]
            accum = accum_ref[:, at : at + head]
            weights = jnp.exp2(product_right(keys, query) * factor + bias)
            grad_scores = low(
                weights * (product_right(values, accum) - delta_ref[order : order + 1, :])
            )
            grad_values += product(low(weights), accum)
            grad_keys += product(grad_scores, query)
            sums_ref[at : at + head, :] += product(keys_turned, grad_scores)
        grad_pair_ref[pl.ds(begin, rows), :head] = low(grad_keys * scale)
        grad_pair_ref[pl.ds(begin, rows), head:] = low(grad_values)
        return carry

    lax.fori_loop(bounds_ref[0], bounds_ref[1] + 1, step, 0)
    cosine = cosine_ref[...]
    sine = -sine_ref[...]
    for order in range(wide // head):
        at = order * head
        grad_query_ref[:, at : at + head] = low(
            rotate_rows(sums_ref[at : at + head, :].T * scale, cosine, sine)
        )


def in_vmem(count):
    return [pl.BlockSpec(memory_space=pltpu.SMEM)] + [
        pl.BlockSpec(memory_space=pltpu.VMEM) for _ in range(count)
    ]


def attend(bounds, query_pre, cosine, sine, place, pair):
    rows, wide = query_pre.shape
    return pl.pallas_call(
        attend_kernel,
        out_shape=(
            jax.ShapeDtypeStruct((rows, wide), jnp.bfloat16),
            jax.ShapeDtypeStruct((rows, wide), jnp.float32),
            jax.ShapeDtypeStruct((8 * -(-wide // cosine.shape[1] // 8), rows), jnp.float32),
        ),
        in_specs=in_vmem(5),
        out_specs=tuple(in_vmem(3)[1:]),
        scratch_shapes=[pltpu.VMEM((wide, rows), jnp.float32)],
        cost_estimate=pl.CostEstimate(
            flops=4 * 9 * rows * rows * wide, transcendentals=9 * rows * rows * 6, bytes_accessed=20 << 20
        ),
        name="attend",
    )(bounds, query_pre, cosine, sine, place, pair)


def attend_back(bounds, rotated, grad, attended, totals, cosine, sine, place, pair):
    rows, wide = rotated.shape
    return pl.pallas_call(
        attend_back_kernel,
        out_shape=(
            jax.ShapeDtypeStruct((rows, wide), jnp.bfloat16),
            jax.ShapeDtypeStruct(pair.shape, jnp.bfloat16),
        ),
        in_specs=in_vmem(8),
        out_specs=tuple(in_vmem(2)[1:]),
        scratch_shapes=[
            pltpu.VMEM((wide, rows), jnp.float32),
            pltpu.VMEM((rows, wide), jnp.bfloat16),
            pltpu.VMEM(totals.shape, jnp.float32),
        ],
        cost_estimate=pl.CostEstimate(
            flops=rows * wide, transcendentals=0, bytes_accessed=rows * wide
        ),
        name="attend_back",
    )(bounds, rotated, grad, attended, totals, cosine, sine, place, pair)


def local(
    tokens,
    lengths,
    norm1_gain,
    w_query,
    b_query,
    key_projection,
    key_bias_vector,
    value_projection,
    value_bias_vector,
    w_out,
    norm2_gain,
    w_gate,
    w_up,
    w_down,
    cotangent,
):
    rows, width = tokens.shape
    devices = lax.axis_size(WIDE)
    own_index = lax.axis_index(WIDE)
    first = own_index * rows
    index = first + jnp.arange(rows, dtype=jnp.int32)
    ends = jnp.cumsum(lengths, dtype=jnp.int32)
    starts = ends - lengths
    seq_start = jnp.max(jnp.where(starts[None, :] <= index[:, None], starts[None, :], 0), axis=1)
    lowest = jnp.min(seq_start)
    highest = first + rows - 1
    head = key_projection.shape[1]
    freq = 1.0 / ROPE_BASE ** (jnp.arange(head // 2, dtype=jnp.float32) * 2.0 / head)
    angle = (index - seq_start).astype(jnp.float32)[:, None] * freq[None, :]
    cosine_table = jnp.cos(angle)[:, None, :]
    sine_table = jnp.sin(angle)[:, None, :]
    cosine_head = jnp.concatenate([cosine_table[:, 0], cosine_table[:, 0]], axis=1)
    sine_head = jnp.concatenate([-sine_table[:, 0], sine_table[:, 0]], axis=1)
    place = jnp.concatenate([seq_start[None], index[None], jnp.zeros((6, rows), jnp.int32)], axis=0)
    bounds = jnp.stack([lowest // rows, highest // rows])
    features = w_query.shape[0]
    heads_width = w_query.shape[1]
    query_group = heads_width // head
    projected = heads_width + 2 * head

    piece = b_query.shape[1]
    small_parts = [norm1_gain, norm2_gain, b_query.reshape(-1), key_bias_vector.reshape(-1),
                   value_bias_vector.reshape(-1)]
    small_sizes = [part.shape[0] for part in small_parts]
    small_rows = -(-sum(small_sizes) // head)
    small = jnp.concatenate(small_parts)
    small = jnp.pad(small, (0, features * head - small.shape[0])).reshape(features, head)
    square_pack = jnp.concatenate([w_query, w_out.T], axis=1)
    square_column = gather_z(square_pack)
    pair_pack = jnp.concatenate([key_projection, value_projection, small], axis=1)
    pair_column = gather_z(after(pair_pack, square_pack))
    down_own = deal(after(w_down, pair_column).T)
    w_pair = gather_rest(pair_column, features)
    pair_weights_came = other(w_pair[:, : 2 * head], "y")
    small_all = w_pair[:, 2 * head :].reshape(devices, features, head)[:, :small_rows]
    small_all = small_all.reshape(devices, small_rows * head).astype(jnp.float32)
    cuts = [0]
    for size in small_sizes:
        cuts.append(cuts[-1] + size)
    gain_one = small_all[:, cuts[0] : cuts[1]].reshape(-1)
    gain_two = small_all[:, cuts[1] : cuts[2]].reshape(-1)
    bias_query = small_all[:, cuts[2] : cuts[3]].reshape(devices, query_group, piece)
    bias_query = bias_query.transpose(1, 0, 2).reshape(-1)
    bias_key = small_all[:, cuts[3] : cuts[4]].reshape(-1)
    bias_value = small_all[:, cuts[4] : cuts[5]].reshape(-1)


    inputs = tokens.astype(jnp.float32)
    scale_one = norm_scale(inputs)
    normed_one = low(inputs * scale_one * gain_one)
    projections = product(normed_one, w_pair[:, : 2 * head])
    key_pre = projections[:, :head] + bias_key
    key_rows = low(
        rotate_halves(key_pre.reshape(rows, 1, head), cosine_table, sine_table).reshape(rows, head)
    )
    value_rows = low(projections[:, head:] + bias_value)
    key_value = jnp.concatenate([key_rows, value_rows], axis=1)
    down_all = gather_z(down_own)
    key_value_column = gather_z(after(key_value, down_own, square_column))
    gate_own = deal(after(w_gate, key_value))
    w_square = gather_rest(square_column, features)
    w_query_all = w_square[:, :heads_width]
    w_out_all = w_square[:, heads_width:]
    query_pre = product(normed_one, w_query_all) + bias_query
    key_value_column = after(key_value_column, gate_own)
    gate_all = gather_z(gate_own)
    up_own = deal(after(w_up, key_value_column))
    up_all = gather_z(up_own)
    key_value = after(gather_rest(key_value_column, rows), up_own, pair_weights_came)
    cotangent_group = gather_group(after(cotangent, key_value))
    cotangent_turned = lax.optimization_barrier(cotangent_group.T)
    query_rows, attended, totals = attend(
        bounds, query_pre, cosine_head, sine_head, place, key_value
    )
    attended_low = low(attended)
    attention = low(product_right(attended_low, w_out_all))
    attention_came = after(
        other(attention, "y"), cotangent_group, cotangent_turned
    )
    middle = inputs + (attention.astype(jnp.float32) + attention_came.astype(jnp.float32))
    scale_two = norm_scale(middle)
    normed_two = low(middle * scale_two * gain_two)
    normed_group = gather_group(normed_two)
    normed_turned = lax.optimization_barrier(normed_group.T)
    gate = product(normed_group, gate_all)
    grad_hidden = lax.optimization_barrier(product(cotangent_group, down_all))
    up_all = after(up_all, normed_turned, grad_hidden)
    up_part = product(normed_group, up_all)
    sigmoid_gate = jax.nn.sigmoid(gate)
    silu_gate = gate * sigmoid_gate
    hidden = low(silu_gate * up_part)
    grad_down = row_major(low(product(cotangent_turned, hidden)))
    down_sums = scatter_z(grad_down)
    grad_gate = low(grad_hidden * up_part * sigmoid_gate * (1.0 + gate * (1.0 - sigmoid_gate)))
    grad_up = low(grad_hidden * silu_gate)
    grad_normed_part = product_right(grad_gate, gate_all) + product_right(grad_up, up_all)
    grad_normed_own, grad_normed_across = sum_core(grad_normed_part, rows)
    normed_came = other(grad_normed_across, "x")
    grad_gate_all = row_major(low(product(normed_turned, after(grad_gate, grad_normed_across))))
    gate_sums = scatter_z(grad_gate_all)
    grad_up_all = row_major(low(product(normed_turned, after(grad_up, grad_gate_all))))
    up_sums = scatter_z(grad_up_all)
    down_part = product_right(after(hidden, grad_up_all, down_sums), down_all)
    normed_came = after(normed_came, down_part)
    grad_normed_mine = low(grad_normed_own + normed_came.astype(jnp.float32))
    normed_pair = other(grad_normed_mine, "y")
    down_parts = undeal(after(down_sums, grad_normed_mine))
    normed_pair = after(normed_pair, down_parts)
    grad_normed_two = grad_normed_mine.astype(jnp.float32) + normed_pair.astype(jnp.float32)
    down_own, down_across = sum_core(after(down_part, normed_pair), rows)

    back_two, grad_gain_two = norm_back(middle, scale_two, gain_two, grad_normed_two)
    grad_middle = cotangent.astype(jnp.float32) + back_two
    grad_att = low(grad_middle)
    grad_out_all = product_left(attended_low, grad_att).T
    grad_attended = product(grad_att, w_out_all)
    grad_query_pre, buffer = attend_back(
        bounds, query_rows, grad_attended, attended, totals,
        cosine_head, sine_head, place, key_value,
    )
    grad_query_mine = low(product_right(grad_query_pre, w_query_all))
    query_came = other(grad_query_mine, "y")
    key_value_halves = scatter_core(buffer, rows)
    square_grads = row_major(
        low(jnp.concatenate([product_left(grad_query_pre, normed_one).T, grad_out_all], axis=1))
    )
    key_value_sums = scatter_across(
        key_value_halves, gate_sums, square_grads, grad_query_mine, down_across
    )
    down_came = other(after(down_across, key_value_sums), "x")
    gate_parts = undeal(after(gate_sums, key_value_sums))
    square_halves = scatter_core(after(square_grads, key_value_sums), features)
    key_value_grads = halve_z(key_value_sums, rows, (key_value_sums,), (query_came, gate_parts, down_came))
    square_sums = scatter_across(square_halves)
    key_value_grads = after(key_value_grads, up_sums)
    grad_key_pre = low(
        rotate_halves(key_value_grads[:, :head].reshape(rows, 1, head), cosine_table, -sine_table)
    ).reshape(rows, head)
    grad_value_pre = low(key_value_grads[:, head:])
    grad_pair = jnp.concatenate([grad_key_pre, grad_value_pre], axis=1)
    grad_project = jnp.concatenate([grad_query_pre, grad_pair], axis=1)
    grad_bias = jnp.sum(grad_project.astype(jnp.float32), axis=0)
    pair_both = in_order(grad_pair, other(grad_pair, "y"))
    query_came = after(query_came, grad_pair, square_halves[0])
    grad_normed_one = (
        grad_query_mine.astype(jnp.float32) + query_came.astype(jnp.float32)
    ) + product_right(
        pair_both, in_order(w_pair[:, : 2 * head], pair_weights_came)
    )
    down_mine = low(down_own + after(down_came, key_value_sums).astype(jnp.float32))
    down_pair = other(down_mine, "y")
    result = low(middle + down_mine.astype(jnp.float32) + down_pair.astype(jnp.float32))
    back_one, grad_gain_one = norm_back(inputs, scale_one, gain_one, grad_normed_one)
    grad_tokens = low(grad_middle + back_one)

    small_grads = jnp.concatenate(
        [
            grad_gain_one.reshape(devices, -1),
            grad_gain_two.reshape(devices, -1),
            grad_bias[:heads_width]
            .reshape(query_group, devices, piece)
            .transpose(1, 0, 2)
            .reshape(devices, -1),
            grad_bias[heads_width : heads_width + head].reshape(devices, -1),
            grad_bias[heads_width + head :].reshape(devices, -1),
        ],
        axis=1,
    )
    small_grads = jnp.pad(small_grads, ((0, 0), (0, features * head - small_grads.shape[1])))
    packed_grads = low(
        jnp.concatenate(
            [product_left(grad_pair, normed_one).T, small_grads.reshape(devices * features, head)],
            axis=1,
        )
    )
    packed_halves = other_half(
        packed_grads.reshape(-1, 2, 2, features, packed_grads.shape[1]), "c", 2
    )
    packed_grads = scatter_across(other_half(add_half(packed_halves, square_sums), "x", 1))
    up_parts = undeal(after(up_sums, packed_halves[1]))
    last_grads = scatter_z(jnp.concatenate([square_sums, packed_grads], axis=1)).astype(jnp.float32)
    square_grads = last_grads[:, : 2 * heads_width]
    packed_grads = last_grads[:, 2 * heads_width :]
    small_own = packed_grads[:, 2 * head :].reshape(-1)
    grad_w_out = square_grads[:, heads_width:].T
    grad_w_down = undeal_end(down_parts).T
    grad_w_gate = undeal_end(gate_parts)
    grad_w_up = undeal_end(up_parts)
    return (
        result,
        grad_tokens,
        small_own[cuts[0] : cuts[1]],
        square_grads[:, :heads_width],
        small_own[cuts[2] : cuts[3]].reshape(query_group, piece),
        packed_grads[:, :head],
        small_own[cuts[3] : cuts[4]].reshape(1, piece),
        packed_grads[:, head : 2 * head],
        small_own[cuts[4] : cuts[5]].reshape(1, piece),
        grad_w_out,
        small_own[cuts[1] : cuts[2]],
        grad_w_gate,
        grad_w_up,
        grad_w_down,
    )


def solution(mesh):
    wide, narrow = mesh.devices.shape
    grouped = Mesh(mesh.devices.reshape(wide // 4, 2, 2, narrow), WIDE + ("y",))
    rows = P(WIDE, None)
    vector = P(WIDE)
    columns = P(WIDE, "y")
    lines = P("y", WIDE)
    return jax.shard_map(
        local,
        mesh=grouped,
        in_specs=(rows, P(), vector, columns, lines, columns, lines, columns, lines, lines,
                  vector, columns, columns, lines, rows),
        out_specs=(rows, rows, vector, columns, lines, columns, lines, columns, lines, lines,
                   vector, columns, columns, lines),
        check_vma=False,
    )
```

```python
import math

import jax
import jax.numpy as jnp
from jax import lax
from jax.experimental import pallas as pl
from jax.experimental.layout import Layout, with_layout_constraint
from jax.experimental.pallas import tpu as pltpu
from jax.sharding import Mesh
from jax.sharding import PartitionSpec as P

ROPE_BASE = 10000.0
EPSILON = 1e-06


def product(left, right):
    return jnp.dot(left, right, preferred_element_type=jnp.float32)


def product_left(left, right):
    return lax.dot_general(
        left, right, (((0,), (0,)), ((), ())), preferred_element_type=jnp.float32
    )


def product_right(left, right):
    return lax.dot_general(
        left, right, (((1,), (1,)), ((), ())), preferred_element_type=jnp.float32
    )


def rotate_halves(value_rows, cosine_table, sine_table):
    middle_at = value_rows.shape[-1] // 2
    first = value_rows[..., :middle_at]
    second = value_rows[..., middle_at:]
    return jnp.concatenate(
        [first * cosine_table - second * sine_table, second * cosine_table + first * sine_table],
        axis=-1,
    )


def norm_scale(value_rows):
    return lax.rsqrt(jnp.mean(value_rows * value_rows, axis=-1, keepdims=True) + EPSILON)


def norm_back(value_rows, scale, gain, grad):
    normed = value_rows * scale
    inner = grad * gain
    back = scale * (inner - normed * jnp.mean(inner * normed, axis=-1, keepdims=True))
    return (back, jnp.sum(grad * normed, axis=0))


WIDE = ("z", "x", "c")
GROUP = ("x", "c")


def other(value, axis):
    return lax.ppermute(value, axis, [(0, 1), (1, 0)])


def low(value):
    return value.astype(jnp.bfloat16)


def after(value, *earlier):
    return lax.optimization_barrier((value, *earlier))[0]


def row_major(value):
    return with_layout_constraint(value, Layout(major_to_minor=(0, 1)))


def in_order(own, came):
    first = lax.axis_index("y") == 0
    return jnp.concatenate([jnp.where(first, own, came), jnp.where(first, came, own)], axis=1)


def gather_group(own):
    core = other(own, "c")
    across = other(own, "x")
    far = other(across, "c")
    return jnp.concatenate([own, core, across, far], axis=0)


def sum_core(partial, rows):
    sent = low(jnp.concatenate([partial[rows : 2 * rows], partial[3 * rows :]], axis=0))
    core = other(sent, "c").astype(jnp.float32)
    return partial[:rows] + core[:rows], low(partial[2 * rows : 3 * rows] + core[rows:])


def sum_narrow(partial):
    mine = low(partial)
    return mine.astype(jnp.float32) + other(mine, "y").astype(jnp.float32)


def deal(weight):
    features, hidden = weight.shape
    parts = weight.reshape(features, 4, hidden // 4).transpose(1, 0, 2)
    parts = lax.all_to_all(parts, GROUP, split_axis=0, concat_axis=0, tiled=True)
    return parts.reshape(4 * features, hidden // 4)


def gather_z(own):
    return lax.all_gather(own, "z", axis=0, tiled=True)


def scatter_z(whole):
    return lax.psum_scatter(whole, "z", scatter_dimension=0, tiled=True)


def undeal(grad):
    features = grad.shape[0] // 4
    parts = grad.reshape(4, features, grad.shape[1])
    return lax.all_to_all(parts, GROUP, split_axis=0, concat_axis=0, tiled=True)


def undeal_end(parts):
    count, features, hidden = parts.shape
    return parts.transpose(1, 0, 2).reshape(features, count * hidden).astype(jnp.float32)


def gather_rest(column, rows):
    own = column.reshape(-1, 1, 1, rows, column.shape[1])
    near = other(own, "x")
    at_x = lax.axis_index("x")
    at_c = lax.axis_index("c")
    whole = jnp.zeros((own.shape[0], 2, 2, *own.shape[3:]), column.dtype)
    for piece, x_place, c_place in (
        (own, at_x, at_c),
        (other(own, "c"), at_x, 1 - at_c),
        (near, 1 - at_x, at_c),
        (other(near, "c"), 1 - at_x, 1 - at_c),
    ):
        whole = lax.dynamic_update_slice(whole, piece, (0, x_place, c_place, 0, 0))
    return whole.reshape(-1, column.shape[1])


def other_half(whole, axis, position):
    at = lax.axis_index(axis)
    sent = lax.dynamic_slice_in_dim(whole, 1 - at, 1, position)
    return lax.dynamic_slice_in_dim(whole, at, 1, position), other(sent, axis)


def halve_z(column, rows, early, late):
    high = lax.axis_size("z")
    at_z = lax.axis_index("z")
    step = 1
    while step < high:
        parts = column.reshape(-1, 2, rows, column.shape[1])
        at = (at_z // step) % 2
        sent = lax.dynamic_slice_in_dim(parts, 1 - at, 1, 1)
        kept = lax.dynamic_slice_in_dim(parts, at, 1, 1)
        came = lax.ppermute(sent, "z", [(number, number ^ step) for number in range(high)])
        came = after(came, *(early if step == 1 else late))
        column = kept.astype(jnp.float32) + came.astype(jnp.float32)
        column = column.reshape(-1, column.shape[3])
        step *= 2
        column = low(column) if step < high else column
    return column


def add_half(halves, *earlier):
    kept, came = halves
    return low(kept.astype(jnp.float32) + after(came, *earlier).astype(jnp.float32))


def scatter_core(whole, rows, *earlier):
    parts = whole.reshape(-1, 2, 2, rows, whole.shape[1])
    return other_half(add_half(other_half(parts, "c", 2), *earlier), "x", 1)


def scatter_across(halves, *earlier):
    summed = add_half(halves, *earlier)
    return summed.reshape(-1, summed.shape[4])


def rotate_rows(value_rows, cosine, sine):
    return value_rows * cosine + pltpu.roll(value_rows, value_rows.shape[1] // 2, 1) * sine


def mask_bias(place_ref, begin, span):
    rows = place_ref.shape[1]
    key_index = begin + lax.broadcasted_iota(jnp.int32, (span, rows), 0)
    allowed = (key_index >= place_ref[0:1, :]) & (key_index <= place_ref[1:2, :])
    return jnp.where(allowed, 0.0, -1e30)


def turned(value):
    return value.astype(jnp.float32).T.astype(value.dtype)


def attend_kernel(
    bounds_ref, query_ref, cosine_ref, sine_ref, place_ref, pair_ref,
    rotated_ref, attended_ref, totals_ref, sums_ref,
):
    rows, wide = query_ref.shape
    head = cosine_ref.shape[1]
    factor = math.log2(math.e) / math.sqrt(head)
    cosine = cosine_ref[...]
    sine = sine_ref[...]
    for at in range(0, wide, head):
        rotated_ref[:, at : at + head] = low(
            rotate_rows(query_ref[:, at : at + head], cosine, sine)
        )
    sums_ref[...] = jnp.zeros_like(sums_ref)
    totals_ref[...] = jnp.zeros_like(totals_ref)

    def step(number, carry):
        begin = pl.multiple_of(number * rows, rows)
        keys = pair_ref[pl.ds(begin, rows), :head]
        values_turned = turned(pair_ref[pl.ds(begin, rows), head:])
        bias = mask_bias(place_ref, begin, rows)
        for order in range(wide // head):
            at = order * head
            scores = product_right(keys, rotated_ref[:, at : at + head])
            weights = jnp.exp2(scores * factor + bias)
            totals_ref[order : order + 1, :] += jnp.sum(weights, axis=0, keepdims=True)
            sums_ref[at : at + head, :] += product(values_turned, low(weights))
        return carry

    lax.fori_loop(bounds_ref[0], bounds_ref[1] + 1, step, 0)
    for order in range(wide // head):
        at = order * head
        attended_ref[:, at : at + head] = (
            sums_ref[at : at + head, :] / totals_ref[order : order + 1, :]
        ).T


def attend_back_kernel(
    bounds_ref, rotated_ref, grad_ref, attended_ref, totals_ref, cosine_ref, sine_ref, place_ref,
    pair_ref, grad_query_ref, grad_pair_ref, sums_ref, accum_ref, delta_ref,
):
    rows, wide = rotated_ref.shape
    head = cosine_ref.shape[1]
    scale = 1.0 / math.sqrt(head)
    factor = math.log2(math.e) * scale
    for order in range(wide // head):
        at = order * head
        totals = jnp.broadcast_to(totals_ref[order : order + 1, :], (head, rows)).T
        divided = grad_ref[:, at : at + head] / totals
        accum_ref[:, at : at + head] = low(divided)
        delta_ref[order : order + 1, :] = jnp.sum(
            (divided * attended_ref[:, at : at + head]).T, axis=0, keepdims=True
        )

    def clear(number, carry):
        begin = pl.multiple_of(number * rows, rows)
        grad_pair_ref[pl.ds(begin, rows), :] = jnp.zeros((rows, 2 * head), jnp.bfloat16)
        return carry

    lax.fori_loop(0, grad_pair_ref.shape[0] // rows, clear, 0)
    sums_ref[...] = jnp.zeros_like(sums_ref)

    def step(number, carry):
        begin = pl.multiple_of(number * rows, rows)
        keys = pair_ref[pl.ds(begin, rows), :head]
        values = pair_ref[pl.ds(begin, rows), head:]
        keys_turned = turned(keys)
        bias = mask_bias(place_ref, begin, rows)
        grad_keys = jnp.zeros((rows, head), jnp.float32)
        grad_values = jnp.zeros((rows, head), jnp.float32)
        for order in range(wide // head):
            at = order * head
            query = rotated_ref[:, at : at + head]
            accum = accum_ref[:, at : at + head]
            weights = jnp.exp2(product_right(keys, query) * factor + bias)
            grad_scores = low(
                weights * (product_right(values, accum) - delta_ref[order : order + 1, :])
            )
            grad_values += product(low(weights), accum)
            grad_keys += product(grad_scores, query)
            sums_ref[at : at + head, :] += product(keys_turned, grad_scores)
        grad_pair_ref[pl.ds(begin, rows), :head] = low(grad_keys * scale)
        grad_pair_ref[pl.ds(begin, rows), head:] = low(grad_values)
        return carry

    lax.fori_loop(bounds_ref[0], bounds_ref[1] + 1, step, 0)
    cosine = cosine_ref[...]
    sine = -sine_ref[...]
    for order in range(wide // head):
        at = order * head
        grad_query_ref[:, at : at + head] = low(
            rotate_rows(sums_ref[at : at + head, :].T * scale, cosine, sine)
        )


def in_vmem(count):
    return [pl.BlockSpec(memory_space=pltpu.SMEM)] + [
        pl.BlockSpec(memory_space=pltpu.VMEM) for _ in range(count)
    ]


def attend(bounds, query_pre, cosine, sine, place, pair):
    rows, wide = query_pre.shape
    return pl.pallas_call(
        attend_kernel,
        out_shape=(
            jax.ShapeDtypeStruct((rows, wide), jnp.bfloat16),
            jax.ShapeDtypeStruct((rows, wide), jnp.float32),
            jax.ShapeDtypeStruct((8 * -(-wide // cosine.shape[1] // 8), rows), jnp.float32),
        ),
        in_specs=in_vmem(5),
        out_specs=tuple(in_vmem(3)[1:]),
        scratch_shapes=[pltpu.VMEM((wide, rows), jnp.float32)],
        cost_estimate=pl.CostEstimate(
            flops=4 * 9 * rows * rows * wide, transcendentals=9 * rows * rows * 6, bytes_accessed=20 << 20
        ),
        name="attend",
    )(bounds, query_pre, cosine, sine, place, pair)


def attend_back(bounds, rotated, grad, attended, totals, cosine, sine, place, pair):
    rows, wide = rotated.shape
    return pl.pallas_call(
        attend_back_kernel,
        out_shape=(
            jax.ShapeDtypeStruct((rows, wide), jnp.bfloat16),
            jax.ShapeDtypeStruct(pair.shape, jnp.bfloat16),
        ),
        in_specs=in_vmem(8),
        out_specs=tuple(in_vmem(2)[1:]),
        scratch_shapes=[
            pltpu.VMEM((wide, rows), jnp.float32),
            pltpu.VMEM((rows, wide), jnp.bfloat16),
            pltpu.VMEM(totals.shape, jnp.float32),
        ],
        cost_estimate=pl.CostEstimate(
            flops=rows * wide, transcendentals=0, bytes_accessed=rows * wide
        ),
        name="attend_back",
    )(bounds, rotated, grad, attended, totals, cosine, sine, place, pair)


def local(
    tokens,
    lengths,
    norm1_gain,
    w_query,
    b_query,
    key_projection,
    key_bias_vector,
    value_projection,
    value_bias_vector,
    w_out,
    norm2_gain,
    w_gate,
    w_up,
    w_down,
    cotangent,
):
    rows, width = tokens.shape
    devices = lax.axis_size(WIDE)
    own_index = lax.axis_index(WIDE)
    first = own_index * rows
    index = first + jnp.arange(rows, dtype=jnp.int32)
    ends = jnp.cumsum(lengths, dtype=jnp.int32)
    starts = ends - lengths
    seq_start = jnp.max(jnp.where(starts[None, :] <= index[:, None], starts[None, :], 0), axis=1)
    lowest = jnp.min(seq_start)
    highest = first + rows - 1
    head = key_projection.shape[1]
    freq = 1.0 / ROPE_BASE ** (jnp.arange(head // 2, dtype=jnp.float32) * 2.0 / head)
    angle = (index - seq_start).astype(jnp.float32)[:, None] * freq[None, :]
    cosine_table = jnp.cos(angle)[:, None, :]
    sine_table = jnp.sin(angle)[:, None, :]
    cosine_head = jnp.concatenate([cosine_table[:, 0], cosine_table[:, 0]], axis=1)
    sine_head = jnp.concatenate([-sine_table[:, 0], sine_table[:, 0]], axis=1)
    place = jnp.concatenate([seq_start[None], index[None], jnp.zeros((6, rows), jnp.int32)], axis=0)
    bounds = jnp.stack([lowest // rows, highest // rows])
    features = w_query.shape[0]
    heads_width = w_query.shape[1]
    query_group = heads_width // head
    projected = heads_width + 2 * head

    piece = b_query.shape[1]
    small_parts = [norm1_gain, norm2_gain, b_query.reshape(-1), key_bias_vector.reshape(-1),
                   value_bias_vector.reshape(-1)]
    small_sizes = [part.shape[0] for part in small_parts]
    small_rows = -(-sum(small_sizes) // head)
    small = jnp.concatenate(small_parts)
    small = jnp.pad(small, (0, features * head - small.shape[0])).reshape(features, head)
    square_pack = jnp.concatenate([w_query, w_out.T], axis=1)
    square_column = gather_z(square_pack)
    pair_pack = jnp.concatenate([key_projection, value_projection, small], axis=1)
    pair_column = gather_z(after(pair_pack, square_pack))
    gate_own = deal(after(w_gate, pair_column))
    w_pair = gather_rest(pair_column, features)
    pair_weights_came = other(w_pair[:, : 2 * head], "y")
    small_all = w_pair[:, 2 * head :].reshape(devices, features, head)[:, :small_rows]
    small_all = small_all.reshape(devices, small_rows * head).astype(jnp.float32)
    cuts = [0]
    for size in small_sizes:
        cuts.append(cuts[-1] + size)
    gain_one = small_all[:, cuts[0] : cuts[1]].reshape(-1)
    gain_two = small_all[:, cuts[1] : cuts[2]].reshape(-1)
    bias_query = small_all[:, cuts[2] : cuts[3]].reshape(devices, query_group, piece)
    bias_query = bias_query.transpose(1, 0, 2).reshape(-1)
    bias_key = small_all[:, cuts[3] : cuts[4]].reshape(-1)
    bias_value = small_all[:, cuts[4] : cuts[5]].reshape(-1)


    inputs = tokens.astype(jnp.float32)
    scale_one = norm_scale(inputs)
    normed_one = low(inputs * scale_one * gain_one)
    projections = product(normed_one, w_pair[:, : 2 * head])
    key_pre = projections[:, :head] + bias_key
    key_rows = low(
        rotate_halves(key_pre.reshape(rows, 1, head), cosine_table, sine_table).reshape(rows, head)
    )
    value_rows = low(projections[:, head:] + bias_value)
    key_value = jnp.concatenate([key_rows, value_rows], axis=1)
    gate_all = gather_z(gate_own)
    key_value_column = gather_z(after(key_value, gate_own, square_column))
    up_own = deal(after(w_up, key_value))
    w_square = gather_rest(square_column, features)
    w_query_all = w_square[:, :heads_width]
    w_out_all = w_square[:, heads_width:]
    query_pre = product(normed_one, w_query_all) + bias_query
    key_value_column = after(key_value_column, up_own)
    up_all = gather_z(up_own)
    down_own = deal(after(w_down, key_value_column).T)
    down_all = gather_z(down_own)
    key_value = after(gather_rest(key_value_column, rows), down_own, pair_weights_came)
    cotangent_group = gather_group(after(cotangent, key_value))
    cotangent_turned = lax.optimization_barrier(cotangent_group.T)
    query_rows, attended, totals = attend(
        bounds, query_pre, cosine_head, sine_head, place, key_value
    )
    attended_low = low(attended)
    attention = low(product_right(attended_low, w_out_all))
    attention_came = after(
        other(attention, "y"), cotangent_group, cotangent_turned
    )
    middle = inputs + (attention.astype(jnp.float32) + attention_came.astype(jnp.float32))
    scale_two = norm_scale(middle)
    normed_two = low(middle * scale_two * gain_two)
    normed_group = gather_group(normed_two)
    normed_turned = lax.optimization_barrier(normed_group.T)
    gate = product(normed_group, gate_all)
    up_all = after(up_all, normed_turned)
    up_part = product(normed_group, up_all)
    sigmoid_gate = jax.nn.sigmoid(gate)
    silu_gate = gate * sigmoid_gate
    hidden = low(silu_gate * up_part)
    grad_down = row_major(low(product(cotangent_turned, hidden)))
    down_sums = scatter_z(grad_down)
    grad_hidden = product(after(cotangent_group, grad_down), down_all)
    grad_gate = low(grad_hidden * up_part * sigmoid_gate * (1.0 + gate * (1.0 - sigmoid_gate)))
    grad_up = low(grad_hidden * silu_gate)
    grad_normed_part = product_right(grad_gate, gate_all) + product_right(grad_up, up_all)
    grad_normed_own, grad_normed_across = sum_core(grad_normed_part, rows)
    normed_came = other(grad_normed_across, "x")
    grad_gate_all = row_major(low(product(normed_turned, after(grad_gate, grad_normed_across))))
    gate_sums = scatter_z(grad_gate_all)
    grad_up_all = row_major(low(product(normed_turned, after(grad_up, grad_gate_all))))
    up_sums = scatter_z(grad_up_all)
    down_part = product_right(after(hidden, grad_up_all, down_sums), down_all)
    normed_came = after(normed_came, down_part)
    grad_normed_mine = low(grad_normed_own + normed_came.astype(jnp.float32))
    normed_pair = other(grad_normed_mine, "y")
    down_parts = undeal(after(down_sums, grad_normed_mine))
    normed_pair = after(normed_pair, down_parts)
    grad_normed_two = grad_normed_mine.astype(jnp.float32) + normed_pair.astype(jnp.float32)
    down_own, down_across = sum_core(after(down_part, normed_pair), rows)

    back_two, grad_gain_two = norm_back(middle, scale_two, gain_two, grad_normed_two)
    grad_middle = cotangent.astype(jnp.float32) + back_two
    grad_att = low(grad_middle)
    grad_out_all = product_left(attended_low, grad_att).T
    grad_attended = product(grad_att, w_out_all)
    grad_query_pre, buffer = attend_back(
        bounds, query_rows, grad_attended, attended, totals,
        cosine_head, sine_head, place, key_value,
    )
    grad_query_mine = low(product_right(grad_query_pre, w_query_all))
    query_came = other(grad_query_mine, "y")
    key_value_halves = scatter_core(buffer, rows)
    square_grads = row_major(
        low(jnp.concatenate([product_left(grad_query_pre, normed_one).T, grad_out_all], axis=1))
    )
    key_value_sums = scatter_across(
        key_value_halves, gate_sums, square_grads, grad_query_mine, down_across
    )
    down_came = other(after(down_across, key_value_sums), "x")
    gate_parts = undeal(after(gate_sums, key_value_sums))
    square_halves = scatter_core(after(square_grads, key_value_sums), features)
    key_value_grads = halve_z(key_value_sums, rows, (key_value_sums,), (query_came, gate_parts, down_came))
    square_sums = scatter_across(square_halves)
    key_value_grads = after(key_value_grads, up_sums)
    grad_key_pre = low(
        rotate_halves(key_value_grads[:, :head].reshape(rows, 1, head), cosine_table, -sine_table)
    ).reshape(rows, head)
    grad_value_pre = low(key_value_grads[:, head:])
    grad_pair = jnp.concatenate([grad_key_pre, grad_value_pre], axis=1)
    grad_project = jnp.concatenate([grad_query_pre, grad_pair], axis=1)
    grad_bias = jnp.sum(grad_project.astype(jnp.float32), axis=0)
    pair_both = in_order(grad_pair, other(grad_pair, "y"))
    query_came = after(query_came, grad_pair, square_halves[0])
    grad_normed_one = (
        grad_query_mine.astype(jnp.float32) + query_came.astype(jnp.float32)
    ) + product_right(
        pair_both, in_order(w_pair[:, : 2 * head], pair_weights_came)
    )
    down_mine = low(down_own + after(down_came, key_value_sums).astype(jnp.float32))
    down_pair = other(down_mine, "y")
    result = low(middle + down_mine.astype(jnp.float32) + down_pair.astype(jnp.float32))
    back_one, grad_gain_one = norm_back(inputs, scale_one, gain_one, grad_normed_one)
    grad_tokens = low(grad_middle + back_one)

    small_grads = jnp.concatenate(
        [
            grad_gain_one.reshape(devices, -1),
            grad_gain_two.reshape(devices, -1),
            grad_bias[:heads_width]
            .reshape(query_group, devices, piece)
            .transpose(1, 0, 2)
            .reshape(devices, -1),
            grad_bias[heads_width : heads_width + head].reshape(devices, -1),
            grad_bias[heads_width + head :].reshape(devices, -1),
        ],
        axis=1,
    )
    small_grads = jnp.pad(small_grads, ((0, 0), (0, features * head - small_grads.shape[1])))
    packed_grads = low(
        jnp.concatenate(
            [product_left(grad_pair, normed_one).T, small_grads.reshape(devices * features, head)],
            axis=1,
        )
    )
    packed_halves = other_half(
        packed_grads.reshape(-1, 2, 2, features, packed_grads.shape[1]), "c", 2
    )
    packed_grads = scatter_across(other_half(add_half(packed_halves, square_sums), "x", 1))
    up_parts = undeal(after(up_sums, packed_halves[1]))
    last_grads = scatter_z(jnp.concatenate([square_sums, packed_grads], axis=1)).astype(jnp.float32)
    square_grads = last_grads[:, : 2 * heads_width]
    packed_grads = last_grads[:, 2 * heads_width :]
    small_own = packed_grads[:, 2 * head :].reshape(-1)
    grad_w_out = square_grads[:, heads_width:].T
    grad_w_down = undeal_end(down_parts).T
    grad_w_gate = undeal_end(gate_parts)
    grad_w_up = undeal_end(up_parts)
    return (
        result,
        grad_tokens,
        small_own[cuts[0] : cuts[1]],
        square_grads[:, :heads_width],
        small_own[cuts[2] : cuts[3]].reshape(query_group, piece),
        packed_grads[:, :head],
        small_own[cuts[3] : cuts[4]].reshape(1, piece),
        packed_grads[:, head : 2 * head],
        small_own[cuts[4] : cuts[5]].reshape(1, piece),
        grad_w_out,
        small_own[cuts[1] : cuts[2]],
        grad_w_gate,
        grad_w_up,
        grad_w_down,
    )


def solution(mesh):
    wide, narrow = mesh.devices.shape
    grouped = Mesh(mesh.devices.reshape(wide // 4, 2, 2, narrow), WIDE + ("y",))
    rows = P(WIDE, None)
    vector = P(WIDE)
    columns = P(WIDE, "y")
    lines = P("y", WIDE)
    return jax.shard_map(
        local,
        mesh=grouped,
        in_specs=(rows, P(), vector, columns, lines, columns, lines, columns, lines, lines,
                  vector, columns, columns, lines, rows),
        out_specs=(rows, rows, vector, columns, lines, columns, lines, columns, lines, lines,
                   vector, columns, columns, lines),
        check_vma=False,
    )
```

```python
import math

import jax
import jax.numpy as jnp
from jax import lax
from jax.experimental import pallas as pl
from jax.experimental.layout import Layout, with_layout_constraint
from jax.experimental.pallas import tpu as pltpu
from jax.sharding import Mesh
from jax.sharding import PartitionSpec as P

ROPE_BASE = 10000.0
EPSILON = 1e-06


def product(left, right):
    return jnp.dot(left, right, preferred_element_type=jnp.float32)


def product_left(left, right):
    return lax.dot_general(
        left, right, (((0,), (0,)), ((), ())), preferred_element_type=jnp.float32
    )


def product_right(left, right):
    return lax.dot_general(
        left, right, (((1,), (1,)), ((), ())), preferred_element_type=jnp.float32
    )


def rotate_halves(value_rows, cosine_table, sine_table):
    middle_at = value_rows.shape[-1] // 2
    first = value_rows[..., :middle_at]
    second = value_rows[..., middle_at:]
    return jnp.concatenate(
        [first * cosine_table - second * sine_table, second * cosine_table + first * sine_table],
        axis=-1,
    )


def norm_scale(value_rows):
    return lax.rsqrt(jnp.mean(value_rows * value_rows, axis=-1, keepdims=True) + EPSILON)


def norm_back(value_rows, scale, gain, grad):
    normed = value_rows * scale
    inner = grad * gain
    back = scale * (inner - normed * jnp.mean(inner * normed, axis=-1, keepdims=True))
    return (back, jnp.sum(grad * normed, axis=0))


WIDE = ("z", "x", "c")
GROUP = ("x", "c")


def other(value, axis):
    return lax.ppermute(value, axis, [(0, 1), (1, 0)])


def low(value):
    return value.astype(jnp.bfloat16)


def after(value, *earlier):
    return lax.optimization_barrier((value, *earlier))[0]


def row_major(value):
    return with_layout_constraint(value, Layout(major_to_minor=(0, 1)))


def in_order(own, came):
    first = lax.axis_index("y") == 0
    return jnp.concatenate([jnp.where(first, own, came), jnp.where(first, came, own)], axis=1)


def gather_group(own):
    core = other(own, "c")
    across = other(own, "x")
    far = other(across, "c")
    return jnp.concatenate([own, core, across, far], axis=0)


def sum_core(partial, rows):
    sent = low(jnp.concatenate([partial[rows : 2 * rows], partial[3 * rows :]], axis=0))
    core = other(sent, "c").astype(jnp.float32)
    return partial[:rows] + core[:rows], low(partial[2 * rows : 3 * rows] + core[rows:])


def sum_narrow(partial):
    mine = low(partial)
    return mine.astype(jnp.float32) + other(mine, "y").astype(jnp.float32)


def deal(weight):
    features, hidden = weight.shape
    parts = weight.reshape(features, 4, hidden // 4).transpose(1, 0, 2)
    parts = lax.all_to_all(parts, GROUP, split_axis=0, concat_axis=0, tiled=True)
    return parts.reshape(4 * features, hidden // 4)


def gather_z(own):
    return lax.all_gather(own, "z", axis=0, tiled=True)


def scatter_z(whole):
    return lax.psum_scatter(whole, "z", scatter_dimension=0, tiled=True)


def undeal(grad):
    features = grad.shape[0] // 4
    parts = grad.reshape(4, features, grad.shape[1])
    return lax.all_to_all(parts, GROUP, split_axis=0, concat_axis=0, tiled=True)


def undeal_end(parts):
    count, features, hidden = parts.shape
    return parts.transpose(1, 0, 2).reshape(features, count * hidden).astype(jnp.float32)


def gather_rest(column, rows):
    own = column.reshape(-1, 1, 1, rows, column.shape[1])
    near = other(own, "x")
    at_x = lax.axis_index("x")
    at_c = lax.axis_index("c")
    whole = jnp.zeros((own.shape[0], 2, 2, *own.shape[3:]), column.dtype)
    for piece, x_place, c_place in (
        (own, at_x, at_c),
        (other(own, "c"), at_x, 1 - at_c),
        (near, 1 - at_x, at_c),
        (other(near, "c"), 1 - at_x, 1 - at_c),
    ):
        whole = lax.dynamic_update_slice(whole, piece, (0, x_place, c_place, 0, 0))
    return whole.reshape(-1, column.shape[1])


def other_half(whole, axis, position):
    at = lax.axis_index(axis)
    sent = lax.dynamic_slice_in_dim(whole, 1 - at, 1, position)
    return lax.dynamic_slice_in_dim(whole, at, 1, position), other(sent, axis)


def halve_z(column, rows, early, late):
    high = lax.axis_size("z")
    at_z = lax.axis_index("z")
    step = 1
    while step < high:
        parts = column.reshape(-1, 2, rows, column.shape[1])
        at = (at_z // step) % 2
        sent = lax.dynamic_slice_in_dim(parts, 1 - at, 1, 1)
        kept = lax.dynamic_slice_in_dim(parts, at, 1, 1)
        came = lax.ppermute(sent, "z", [(number, number ^ step) for number in range(high)])
        came = after(came, *(early if step == 1 else late))
        column = kept.astype(jnp.float32) + came.astype(jnp.float32)
        column = column.reshape(-1, column.shape[3])
        step *= 2
        column = low(column) if step < high else column
    return column


def add_half(halves, *earlier):
    kept, came = halves
    return low(kept.astype(jnp.float32) + after(came, *earlier).astype(jnp.float32))


def scatter_core(whole, rows, *earlier):
    parts = whole.reshape(-1, 2, 2, rows, whole.shape[1])
    return other_half(add_half(other_half(parts, "c", 2), *earlier), "x", 1)


def scatter_across(halves, *earlier):
    summed = add_half(halves, *earlier)
    return summed.reshape(-1, summed.shape[4])


def rotate_rows(value_rows, cosine, sine):
    return value_rows * cosine + pltpu.roll(value_rows, value_rows.shape[1] // 2, 1) * sine


def mask_bias(place_ref, begin, span):
    rows = place_ref.shape[1]
    key_index = begin + lax.broadcasted_iota(jnp.int32, (span, rows), 0)
    allowed = (key_index >= place_ref[0:1, :]) & (key_index <= place_ref[1:2, :])
    return jnp.where(allowed, 0.0, -1e30)


def turned(value):
    return value.astype(jnp.float32).T.astype(value.dtype)


def attend_kernel(
    bounds_ref, query_ref, cosine_ref, sine_ref, place_ref, pair_ref,
    rotated_ref, attended_ref, totals_ref, sums_ref,
):
    rows, wide = query_ref.shape
    head = cosine_ref.shape[1]
    factor = math.log2(math.e) / math.sqrt(head)
    cosine = cosine_ref[...]
    sine = sine_ref[...]
    for at in range(0, wide, head):
        rotated_ref[:, at : at + head] = low(
            rotate_rows(query_ref[:, at : at + head], cosine, sine)
        )
    sums_ref[...] = jnp.zeros_like(sums_ref)
    totals_ref[...] = jnp.zeros_like(totals_ref)

    def step(number, carry):
        begin = pl.multiple_of(number * rows, rows)
        keys = pair_ref[pl.ds(begin, rows), :head]
        values_turned = turned(pair_ref[pl.ds(begin, rows), head:])
        bias = mask_bias(place_ref, begin, rows)
        for order in range(wide // head):
            at = order * head
            scores = product_right(keys, rotated_ref[:, at : at + head])
            weights = jnp.exp2(scores * factor + bias)
            totals_ref[order : order + 1, :] += jnp.sum(weights, axis=0, keepdims=True)
            sums_ref[at : at + head, :] += product(values_turned, low(weights))
        return carry

    lax.fori_loop(bounds_ref[0], bounds_ref[1] + 1, step, 0)
    for order in range(wide // head):
        at = order * head
        attended_ref[:, at : at + head] = (
            sums_ref[at : at + head, :] / totals_ref[order : order + 1, :]
        ).T


def attend_back_kernel(
    bounds_ref, rotated_ref, grad_ref, attended_ref, totals_ref, cosine_ref, sine_ref, place_ref,
    pair_ref, grad_query_ref, grad_pair_ref, sums_ref, accum_ref, delta_ref,
):
    rows, wide = rotated_ref.shape
    head = cosine_ref.shape[1]
    scale = 1.0 / math.sqrt(head)
    factor = math.log2(math.e) * scale
    for order in range(wide // head):
        at = order * head
        totals = jnp.broadcast_to(totals_ref[order : order + 1, :], (head, rows)).T
        divided = grad_ref[:, at : at + head] / totals
        accum_ref[:, at : at + head] = low(divided)
        delta_ref[order : order + 1, :] = jnp.sum(
            (divided * attended_ref[:, at : at + head]).T, axis=0, keepdims=True
        )

    def clear(number, carry):
        begin = pl.multiple_of(number * rows, rows)
        grad_pair_ref[pl.ds(begin, rows), :] = jnp.zeros((rows, 2 * head), jnp.bfloat16)
        return carry

    lax.fori_loop(0, grad_pair_ref.shape[0] // rows, clear, 0)
    sums_ref[...] = jnp.zeros_like(sums_ref)

    def step(number, carry):
        begin = pl.multiple_of(number * rows, rows)
        keys = pair_ref[pl.ds(begin, rows), :head]
        values = pair_ref[pl.ds(begin, rows), head:]
        keys_turned = turned(keys)
        bias = mask_bias(place_ref, begin, rows)
        grad_keys = jnp.zeros((rows, head), jnp.float32)
        grad_values = jnp.zeros((rows, head), jnp.float32)
        for order in range(wide // head):
            at = order * head
            query = rotated_ref[:, at : at + head]
            accum = accum_ref[:, at : at + head]
            weights = jnp.exp2(product_right(keys, query) * factor + bias)
            grad_scores = low(
                weights * (product_right(values, accum) - delta_ref[order : order + 1, :])
            )
            grad_values += product(low(weights), accum)
            grad_keys += product(grad_scores, query)
            sums_ref[at : at + head, :] += product(keys_turned, grad_scores)
        grad_pair_ref[pl.ds(begin, rows), :head] = low(grad_keys * scale)
        grad_pair_ref[pl.ds(begin, rows), head:] = low(grad_values)
        return carry

    lax.fori_loop(bounds_ref[0], bounds_ref[1] + 1, step, 0)
    cosine = cosine_ref[...]
    sine = -sine_ref[...]
    for order in range(wide // head):
        at = order * head
        grad_query_ref[:, at : at + head] = low(
            rotate_rows(sums_ref[at : at + head, :].T * scale, cosine, sine)
        )


def in_vmem(count):
    return [pl.BlockSpec(memory_space=pltpu.SMEM)] + [
        pl.BlockSpec(memory_space=pltpu.VMEM) for _ in range(count)
    ]


def attend(bounds, query_pre, cosine, sine, place, pair):
    rows, wide = query_pre.shape
    return pl.pallas_call(
        attend_kernel,
        out_shape=(
            jax.ShapeDtypeStruct((rows, wide), jnp.bfloat16),
            jax.ShapeDtypeStruct((rows, wide), jnp.float32),
            jax.ShapeDtypeStruct((8 * -(-wide // cosine.shape[1] // 8), rows), jnp.float32),
        ),
        in_specs=in_vmem(5),
        out_specs=tuple(in_vmem(3)[1:]),
        scratch_shapes=[pltpu.VMEM((wide, rows), jnp.float32)],
        cost_estimate=pl.CostEstimate(
            flops=4 * 9 * rows * rows * wide, transcendentals=9 * rows * rows * 6, bytes_accessed=20 << 20
        ),
        name="attend",
    )(bounds, query_pre, cosine, sine, place, pair)


def attend_back(bounds, rotated, grad, attended, totals, cosine, sine, place, pair):
    rows, wide = rotated.shape
    return pl.pallas_call(
        attend_back_kernel,
        out_shape=(
            jax.ShapeDtypeStruct((rows, wide), jnp.bfloat16),
            jax.ShapeDtypeStruct(pair.shape, jnp.bfloat16),
        ),
        in_specs=in_vmem(8),
        out_specs=tuple(in_vmem(2)[1:]),
        scratch_shapes=[
            pltpu.VMEM((wide, rows), jnp.float32),
            pltpu.VMEM((rows, wide), jnp.bfloat16),
            pltpu.VMEM(totals.shape, jnp.float32),
        ],
        cost_estimate=pl.CostEstimate(
            flops=rows * wide, transcendentals=0, bytes_accessed=rows * wide
        ),
        name="attend_back",
    )(bounds, rotated, grad, attended, totals, cosine, sine, place, pair)


def local(
    tokens,
    lengths,
    norm1_gain,
    w_query,
    b_query,
    key_projection,
    key_bias_vector,
    value_projection,
    value_bias_vector,
    w_out,
    norm2_gain,
    w_gate,
    w_up,
    w_down,
    cotangent,
):
    rows, width = tokens.shape
    devices = lax.axis_size(WIDE)
    own_index = lax.axis_index(WIDE)
    first = own_index * rows
    index = first + jnp.arange(rows, dtype=jnp.int32)
    ends = jnp.cumsum(lengths, dtype=jnp.int32)
    starts = ends - lengths
    seq_start = jnp.max(jnp.where(starts[None, :] <= index[:, None], starts[None, :], 0), axis=1)
    lowest = jnp.min(seq_start)
    highest = first + rows - 1
    head = key_projection.shape[1]
    freq = 1.0 / ROPE_BASE ** (jnp.arange(head // 2, dtype=jnp.float32) * 2.0 / head)
    angle = (index - seq_start).astype(jnp.float32)[:, None] * freq[None, :]
    cosine_table = jnp.cos(angle)[:, None, :]
    sine_table = jnp.sin(angle)[:, None, :]
    cosine_head = jnp.concatenate([cosine_table[:, 0], cosine_table[:, 0]], axis=1)
    sine_head = jnp.concatenate([-sine_table[:, 0], sine_table[:, 0]], axis=1)
    place = jnp.concatenate([seq_start[None], index[None], jnp.zeros((6, rows), jnp.int32)], axis=0)
    bounds = jnp.stack([lowest // rows, highest // rows])
    features = w_query.shape[0]
    heads_width = w_query.shape[1]
    query_group = heads_width // head
    projected = heads_width + 2 * head

    piece = b_query.shape[1]
    small_parts = [norm1_gain, norm2_gain, b_query.reshape(-1), key_bias_vector.reshape(-1),
                   value_bias_vector.reshape(-1)]
    small_sizes = [part.shape[0] for part in small_parts]
    small_rows = -(-sum(small_sizes) // head)
    small = jnp.concatenate(small_parts)
    small = jnp.pad(small, (0, features * head - small.shape[0])).reshape(features, head)
    square_pack = jnp.concatenate([w_query, w_out.T], axis=1)
    square_column = gather_z(square_pack)
    pair_pack = jnp.concatenate([key_projection, value_projection, small], axis=1)
    pair_column = gather_z(after(pair_pack, square_pack))
    gate_own = deal(after(w_gate, pair_column))
    w_pair = gather_rest(pair_column, features)
    pair_weights_came = other(w_pair[:, : 2 * head], "y")
    small_all = w_pair[:, 2 * head :].reshape(devices, features, head)[:, :small_rows]
    small_all = small_all.reshape(devices, small_rows * head).astype(jnp.float32)
    cuts = [0]
    for size in small_sizes:
        cuts.append(cuts[-1] + size)
    gain_one = small_all[:, cuts[0] : cuts[1]].reshape(-1)
    gain_two = small_all[:, cuts[1] : cuts[2]].reshape(-1)
    bias_query = small_all[:, cuts[2] : cuts[3]].reshape(devices, query_group, piece)
    bias_query = bias_query.transpose(1, 0, 2).reshape(-1)
    bias_key = small_all[:, cuts[3] : cuts[4]].reshape(-1)
    bias_value = small_all[:, cuts[4] : cuts[5]].reshape(-1)


    inputs = tokens.astype(jnp.float32)
    scale_one = norm_scale(inputs)
    normed_one = low(inputs * scale_one * gain_one)
    projections = product(normed_one, w_pair[:, : 2 * head])
    key_pre = projections[:, :head] + bias_key
    key_rows = low(
        rotate_halves(key_pre.reshape(rows, 1, head), cosine_table, sine_table).reshape(rows, head)
    )
    value_rows = low(projections[:, head:] + bias_value)
    key_value = jnp.concatenate([key_rows, value_rows], axis=1)
    gate_all = gather_z(gate_own)
    key_value_column = gather_z(after(key_value, gate_own, square_column))
    up_own = deal(after(w_up, key_value))
    w_square = gather_rest(square_column, features)
    w_query_all = w_square[:, :heads_width]
    w_out_all = w_square[:, heads_width:]
    query_pre = product(normed_one, w_query_all) + bias_query
    key_value_column = after(key_value_column, up_own)
    up_all = gather_z(up_own)
    down_own = deal(after(w_down, key_value_column).T)
    down_all = gather_z(down_own)
    key_value = after(gather_rest(key_value_column, rows), down_own, pair_weights_came)
    cotangent_group = gather_group(after(cotangent, key_value))
    cotangent_turned = lax.optimization_barrier(cotangent_group.T)
    query_rows, attended, totals = attend(
        bounds, query_pre, cosine_head, sine_head, place, key_value
    )
    attended_low = low(attended)
    attention = low(product_right(attended_low, w_out_all))
    attention_came = after(
        other(attention, "y"), cotangent_group, cotangent_turned
    )
    middle = inputs + (attention.astype(jnp.float32) + attention_came.astype(jnp.float32))
    scale_two = norm_scale(middle)
    normed_two = low(middle * scale_two * gain_two)
    normed_group = gather_group(normed_two)
    normed_turned = lax.optimization_barrier(normed_group.T)
    gate = product(normed_group, gate_all)
    up_all = after(up_all, normed_turned)
    up_part = product(normed_group, up_all)
    sigmoid_gate = jax.nn.sigmoid(gate)
    silu_gate = gate * sigmoid_gate
    hidden = low(silu_gate * up_part)
    grad_down = row_major(low(product(cotangent_turned, hidden)))
    down_sums = scatter_z(grad_down)
    grad_hidden = product(after(cotangent_group, grad_down), down_all)
    grad_gate = low(grad_hidden * up_part * sigmoid_gate * (1.0 + gate * (1.0 - sigmoid_gate)))
    grad_up = low(grad_hidden * silu_gate)
    grad_normed_part = product_right(grad_gate, gate_all) + product_right(grad_up, up_all)
    grad_normed_own, grad_normed_across = sum_core(grad_normed_part, rows)
    normed_came = other(grad_normed_across, "x")
    grad_gate_all = row_major(low(product(normed_turned, after(grad_gate, grad_normed_across))))
    gate_sums = scatter_z(grad_gate_all)
    grad_up_all = row_major(low(product(normed_turned, after(grad_up, grad_gate_all))))
    up_sums = scatter_z(grad_up_all)
    down_part = product_right(after(hidden, grad_up_all, down_sums), down_all)
    normed_came = after(normed_came, down_part)
    grad_normed_mine = low(grad_normed_own + normed_came.astype(jnp.float32))
    normed_pair = other(grad_normed_mine, "y")
    down_parts = undeal(after(down_sums, grad_normed_mine))
    normed_pair = after(normed_pair, down_parts)
    grad_normed_two = grad_normed_mine.astype(jnp.float32) + normed_pair.astype(jnp.float32)
    down_own, down_across = sum_core(after(down_part, normed_pair), rows)

    back_two, grad_gain_two = norm_back(middle, scale_two, gain_two, grad_normed_two)
    grad_middle = cotangent.astype(jnp.float32) + back_two
    grad_att = low(grad_middle)
    grad_out_all = product_left(attended_low, grad_att).T
    grad_attended = product(grad_att, w_out_all)
    grad_query_pre, buffer = attend_back(
        bounds, query_rows, grad_attended, attended, totals,
        cosine_head, sine_head, place, key_value,
    )
    grad_query_mine = low(product_right(grad_query_pre, w_query_all))
    query_came = other(grad_query_mine, "y")
    key_value_halves = scatter_core(buffer, rows)
    square_grads = row_major(
        low(jnp.concatenate([product_left(grad_query_pre, normed_one).T, grad_out_all], axis=1))
    )
    key_value_sums = scatter_across(
        key_value_halves, gate_sums, square_grads, grad_query_mine, down_across
    )
    gate_parts = undeal(after(gate_sums, key_value_sums))
    square_halves = scatter_core(after(square_grads, key_value_sums), features)
    key_value_grads = halve_z(key_value_sums, rows, (key_value_sums,), (query_came, gate_parts, square_halves[1]))
    square_sums = scatter_across(square_halves)
    down_came = other(after(down_across, square_halves[1]), "x")
    key_value_grads = after(key_value_grads, up_sums)
    grad_key_pre = low(
        rotate_halves(key_value_grads[:, :head].reshape(rows, 1, head), cosine_table, -sine_table)
    ).reshape(rows, head)
    grad_value_pre = low(key_value_grads[:, head:])
    grad_pair = jnp.concatenate([grad_key_pre, grad_value_pre], axis=1)
    grad_project = jnp.concatenate([grad_query_pre, grad_pair], axis=1)
    grad_bias = jnp.sum(grad_project.astype(jnp.float32), axis=0)
    pair_both = in_order(grad_pair, other(grad_pair, "y"))
    query_came = after(query_came, grad_pair)
    grad_normed_one = (
        grad_query_mine.astype(jnp.float32) + query_came.astype(jnp.float32)
    ) + product_right(
        pair_both, in_order(w_pair[:, : 2 * head], pair_weights_came)
    )
    down_mine = low(down_own + after(down_came, key_value_sums).astype(jnp.float32))
    down_pair = other(down_mine, "y")
    result = low(middle + down_mine.astype(jnp.float32) + down_pair.astype(jnp.float32))
    back_one, grad_gain_one = norm_back(inputs, scale_one, gain_one, grad_normed_one)
    grad_tokens = low(grad_middle + back_one)

    small_grads = jnp.concatenate(
        [
            grad_gain_one.reshape(devices, -1),
            grad_gain_two.reshape(devices, -1),
            grad_bias[:heads_width]
            .reshape(query_group, devices, piece)
            .transpose(1, 0, 2)
            .reshape(devices, -1),
            grad_bias[heads_width : heads_width + head].reshape(devices, -1),
            grad_bias[heads_width + head :].reshape(devices, -1),
        ],
        axis=1,
    )
    small_grads = jnp.pad(small_grads, ((0, 0), (0, features * head - small_grads.shape[1])))
    packed_grads = low(
        jnp.concatenate(
            [product_left(grad_pair, normed_one).T, small_grads.reshape(devices * features, head)],
            axis=1,
        )
    )
    packed_halves = other_half(
        packed_grads.reshape(-1, 2, 2, features, packed_grads.shape[1]), "c", 2
    )
    packed_grads = scatter_across(other_half(add_half(packed_halves, down_came), "x", 1))
    up_parts = undeal(after(up_sums, packed_halves[1]))
    last_grads = scatter_z(jnp.concatenate([square_sums, packed_grads], axis=1)).astype(jnp.float32)
    square_grads = last_grads[:, : 2 * heads_width]
    packed_grads = last_grads[:, 2 * heads_width :]
    small_own = packed_grads[:, 2 * head :].reshape(-1)
    grad_w_out = square_grads[:, heads_width:].T
    grad_w_down = undeal_end(down_parts).T
    grad_w_gate = undeal_end(gate_parts)
    grad_w_up = undeal_end(up_parts)
    return (
        result,
        grad_tokens,
        small_own[cuts[0] : cuts[1]],
        square_grads[:, :heads_width],
        small_own[cuts[2] : cuts[3]].reshape(query_group, piece),
        packed_grads[:, :head],
        small_own[cuts[3] : cuts[4]].reshape(1, piece),
        packed_grads[:, head : 2 * head],
        small_own[cuts[4] : cuts[5]].reshape(1, piece),
        grad_w_out,
        small_own[cuts[1] : cuts[2]],
        grad_w_gate,
        grad_w_up,
        grad_w_down,
    )


def solution(mesh):
    wide, narrow = mesh.devices.shape
    grouped = Mesh(mesh.devices.reshape(wide // 4, 2, 2, narrow), WIDE + ("y",))
    rows = P(WIDE, None)
    vector = P(WIDE)
    columns = P(WIDE, "y")
    lines = P("y", WIDE)
    return jax.shard_map(
        local,
        mesh=grouped,
        in_specs=(rows, P(), vector, columns, lines, columns, lines, columns, lines, lines,
                  vector, columns, columns, lines, rows),
        out_specs=(rows, rows, vector, columns, lines, columns, lines, columns, lines, lines,
                   vector, columns, columns, lines),
        check_vma=False,
    )
```
